32 devices in a mesh: dp: 16 (over z, x, core), tensor: 2 (over y).
Axes of the slice: x: 2, y: 2, z: 4, core: 2. Of those that a mesh axis runs over, the one named last changes fastest.
Arguments:
- inputs: bfloat16 [16, 2048, 512], P('dp', 'tensor'), may hold values from -6 to 6
- lengths: int32 [16], P('dp'), may hold values from 512 to 2048, as said below
- norm1_gain: float32 [512], replicated, may hold values from 0.25 to 1.75
- norm1_bias: float32 [512], replicated, may hold values from -4 to 4
- query_key_value_weight: bfloat16 [3, 512, 512], P(None, None, 'tensor'), may hold values from -0.25 to 0.25
- content_bias: float32 [8, 64], P('tensor'), may hold values from -6 to 6
- position_bias: float32 [8, 64], P('tensor'), may hold values from -6 to 6
- pos_weight: bfloat16 [512, 512], P(None, 'tensor'), may hold values from -0.25 to 0.25
- output_weight: bfloat16 [512, 512], P('tensor'), may hold values from -3 to 3
- out_bias: float32 [512], replicated, may hold values from -4 to 4
- norm2_gain: float32 [512], replicated, may hold values from 0.25 to 1.75
- norm2_bias: float32 [512], replicated, may hold values from -4 to 4
- up_projection_weight: bfloat16 [512, 2048], P(None, 'tensor'), may hold values from -0.25 to 0.25
- up_bias: float32 [2048], P('tensor'), may hold values from -4 to 4
- down_projection_weight: bfloat16 [2048, 512], P('tensor'), may hold values from -0.125 to 0.125
- down_bias: float32 [512], replicated, may hold values from -4 to 4
- cotangent: bfloat16 [16, 2048, 512], P('dp', 'tensor'), may hold values from -6 to 6
Outputs:
- output: bfloat16 [16, 2048, 512], P('dp', 'tensor')
- input_grad: float32 [16, 2048, 512], P('dp', 'tensor')
- norm1_gain_grad: float32 [512], replicated
- norm1_bias_grad: float32 [512], replicated
- qkv_weight_grad: float32 [3, 512, 512], P(None, None, 'tensor')
- content_bias_grad: float32 [8, 64], P('tensor')
- position_bias_grad: float32 [8, 64], P('tensor')
- pos_weight_grad: float32 [512, 512], P(None, 'tensor')
- out_weight_grad: float32 [512, 512], P('tensor')
- out_bias_grad: float32 [512], replicated
- norm2_gain_grad: float32 [512], replicated
- norm2_bias_grad: float32 [512], replicated
- up_projection_gradient: float32 [512, 2048], P(None, 'tensor')
- up_bias_grad: float32 [2048], P('tensor')
- down_weight_grad: float32 [2048, 512], P('tensor')
- down_bias_grad: float32 [512], replicated
The draws below stay inside these ranges and needn't reach their ends.
Inputs may be any that keep to these rules, and one draw needn't show every extreme that they name: `lengths`: the valid tokens of a sequence are its first positions, the rest is padding. Every draw holds a sequence of 2048 and one of 512 tokens.
All inputs are finite; a program needn't handle non-finite values.
Results may differ from the reference program's by a relative error of at most 0.024.
Values may be sent and summed in bfloat16 or wider, within the bound.
No kernel may reach another device: no remote copies, remote signals or barrier semaphores. Data moves between devices by JAX's collectives and lax.ppermute only.
A program may use at most 192 MiB of HBM per device.

```python
import jax
import jax.numpy as jnp
from jax import lax

D = 512
HEADS = 8
HEAD_DIM = 64
FF = 2048
SEQ_LEN = 2048
BLOCK = 512
SEQS = 16


def draw_lengths(key, part):
    value_key = jax.random.fold_in(key, 11)
    place_key = jax.random.fold_in(key, 23)
    drawn = jax.random.randint(value_key, (SEQS,), SEQ_LEN // 4, SEQ_LEN + 1)
    places = jax.random.permutation(place_key, SEQS)
    drawn = drawn.at[places[0]].set(SEQ_LEN)
    drawn = drawn.at[places[1]].set(SEQ_LEN // 4)
    return drawn.astype(jnp.int32)


def block_levels(rng, extent, pieces, low, high):
    def one(dim, blocks):
        steps = jax.random.uniform(jax.random.fold_in(jax.random.fold_in(rng, 6), dim), (blocks,), jnp.float32, low / len(pieces), high / len(pieces))
        return jnp.repeat(jnp.exp(steps), extent[dim] // blocks).reshape((-1,) + (1,) * (len(extent) - dim - 1))

    level = one(*pieces[0])
    for cut in pieces[1:]:
        level = level * one(*cut)
    return level


def gaussian(key, dims, deviation, most, cuts=(), kind=jnp.bfloat16):
    gain = block_levels(key, dims, cuts, -0.22, 0.18) if cuts else 1.0
    result = jax.random.normal(key, dims, jnp.float32) * deviation * gain
    return jnp.minimum(jnp.maximum(result, -most), most).astype(kind)


def setup_inputs(seed: int = 0) -> dict:
    streams_of = jax.random.split(jax.random.key(seed), 18)
    inputs = gaussian(streams_of[0], (SEQS, SEQ_LEN, D), 1.0, 6.0, ((0, 16), (1, 2)))
    lengths = draw_lengths(jax.random.fold_in(streams_of[17], 71), 0)
    norm1_gain = jnp.clip(1.0 + 0.15 * jax.random.normal(streams_of[2], (D,), jnp.float32), 0.25, 1.75)
    norm1_bias = gaussian(streams_of[3], (D,), 0.3, 4.0, (), jnp.float32)
    query_key_value_weight = gaussian(streams_of[4], (3, D, D), D ** -0.5, 0.25, ((2, 2),))
    content_bias = gaussian(streams_of[5], (HEADS, HEAD_DIM), 0.5, 6.0, ((0, 2),), jnp.float32)
    position_bias = gaussian(streams_of[6], (HEADS, HEAD_DIM), 0.5, 6.0, ((0, 2),), jnp.float32)
    pos_weight = gaussian(streams_of[7], (D, D), D ** -0.5, 0.25, ((1, 2),))
    output_weight = gaussian(streams_of[8], (D, D), 4 ** -0.5, 3.0, ((0, 2),))
    out_bias = gaussian(streams_of[9], (D,), 0.3, 4.0, (), jnp.float32)
    norm2_gain = jnp.clip(1.0 + 0.15 * jax.random.normal(streams_of[10], (D,), jnp.float32), 0.25, 1.75)
    norm2_bias = gaussian(streams_of[11], (D,), 0.3, 4.0, (), jnp.float32)
    up_projection_weight = gaussian(streams_of[12], (D, FF), D ** -0.5, 0.25, ((1, 2),))
    up_bias = gaussian(streams_of[13], (FF,), 0.3, 4.0, ((0, 2),), jnp.float32)
    down_projection_weight = gaussian(streams_of[14], (FF, D), FF ** -0.5, 0.125, ((0, 2),))
    down_bias = gaussian(streams_of[15], (D,), 0.3, 4.0, (), jnp.float32)
    cotangent = gaussian(streams_of[16], (SEQS, SEQ_LEN, D), 1.0, 6.0, ((0, 16), (1, 2)))
    return {"inputs": inputs, "lengths": lengths, "norm1_gain": norm1_gain, "norm1_bias": norm1_bias, "query_key_value_weight": query_key_value_weight, "content_bias": content_bias, "position_bias": position_bias, "pos_weight": pos_weight, "output_weight": output_weight, "out_bias": out_bias, "norm2_gain": norm2_gain, "norm2_bias": norm2_bias, "up_projection_weight": up_projection_weight, "up_bias": up_bias, "down_projection_weight": down_projection_weight, "down_bias": down_bias, "cotangent": cotangent}


epsilon = 1e-05
score_scale = 0.125
masked_score = -1e+30
highest = lax.Precision.HIGHEST

@jax.custom_vjp
def low(v):
    return lax.optimization_barrier(v.astype(jnp.bfloat16)).astype(jnp.float32)

@jax.custom_vjp
def low_back(v):
    return v

def low_keep(v):
    return (low(v), None)

def low_pass(kept, grad):
    return (grad,)

def back_keep(v):
    return (v, None)

def back_low(kept, grad):
    return (low(grad),)
low.defvjp(low_keep, low_pass)
low_back.defvjp(back_keep, back_low)

def norm_rows(values, norm_gain, norm_bias):
    centre = values - lax.optimization_barrier(jnp.mean(values, axis=-1, keepdims=True))
    variance = lax.optimization_barrier(jnp.mean(centre * centre, axis=-1, keepdims=True))
    return centre * lax.rsqrt(variance + epsilon) * norm_gain + norm_bias

def sin_rows(row_count, model_width, seq_len):
    distance = (seq_len - 1 - jnp.arange(row_count, dtype=jnp.int32)).astype(jnp.float32)
    frequency = jnp.power(10000.0, -jnp.arange(0, model_width, 2, dtype=jnp.int32).astype(jnp.float32) / model_width)
    angles = distance[:, None] * frequency[None, :]
    return jnp.concatenate([jnp.sin(angles), jnp.cos(angles)], axis=1)

def shift_rows(wide_scores, key_count):
    head_count, row_count, column_count = wide_scores.shape
    flattened = wide_scores.reshape(head_count, row_count * column_count)
    trimmed = lax.slice_in_dim(flattened, row_count - 1, row_count - 1 + row_count * (column_count - 1), axis=1)
    return trimmed.reshape(head_count, row_count, column_count - 1)[:, :, :key_count]

def attend_block(block_index, query_content, query_offset, key_rows, value_rows, position):
    query_part = lax.dynamic_slice_in_dim(query_content, block_index * BLOCK, BLOCK, 0)
    offset_part = lax.dynamic_slice_in_dim(query_offset, block_index * BLOCK, BLOCK, 0)
    window = lax.dynamic_slice_in_dim(position, SEQ_LEN - (block_index + 1) * BLOCK, SEQ_LEN + BLOCK, 0)
    content = jnp.einsum('rhe,che->hrc', query_part, key_rows, precision=highest)
    wide_scores = jnp.einsum('rhe,khe->hrk', offset_part, window, precision=highest)
    raw_scores = low_back((content + shift_rows(wide_scores, SEQ_LEN)) * score_scale)
    row_pos = block_index * BLOCK + jnp.arange(BLOCK, dtype=jnp.int32)
    allowed = row_pos[:, None] >= jnp.arange(SEQ_LEN, dtype=jnp.int32)[None, :]
    scores = jnp.where(allowed[None], raw_scores, masked_score)
    top_score = lax.optimization_barrier(jnp.max(scores, axis=-1, keepdims=True))
    weights = jnp.exp(scores - top_score)
    probs = weights / lax.optimization_barrier(jnp.sum(weights, axis=-1, keepdims=True))
    return jnp.einsum('hrc,che->rhe', low(probs), value_rows, precision=highest)
block_step = jax.checkpoint(attend_block)

def layer(source, params, length):
    norm1_gain, norm1_bias, query_key_value_weight, content_bias, position_bias, pos_weight, output_weight, out_bias, norm2_gain, norm2_bias, up_projection_weight, up_bias, down_projection_weight, down_bias = params
    shaped = (SEQ_LEN, HEADS, HEAD_DIM)
    valid_rows = (jnp.arange(SEQ_LEN, dtype=jnp.int32) < length).astype(source.dtype)[:, None]
    first_rows = low(norm_rows(source, norm1_gain, norm1_bias))
    projected = low_back(jnp.einsum('ld,cdh->clh', first_rows, query_key_value_weight, precision=highest))
    query_content = low(projected[0] + content_bias.reshape(-1)).reshape(shaped)
    query_offset = low(projected[0] + position_bias.reshape(-1)).reshape(shaped)
    key_rows = low(projected[1]).reshape(shaped)
    value_rows = low(projected[2]).reshape(shaped)
    sin_table = low(sin_rows(2 * SEQ_LEN, D, SEQ_LEN).astype(source.dtype))
    position = low(low_back(jnp.dot(sin_table, pos_weight, precision=highest))).reshape(2 * SEQ_LEN, HEADS, HEAD_DIM)
    blocks = lax.map(lambda block_index: block_step(block_index, query_content, query_offset, key_rows, value_rows, position), jnp.arange(SEQ_LEN // BLOCK, dtype=jnp.int32))
    attention_result = low(low_back(blocks.reshape(SEQ_LEN, D)))
    branch = low_back(jnp.dot(attention_result, output_weight, precision=highest) + out_bias)
    middle = source + branch
    second_rows = low(norm_rows(middle, norm2_gain, norm2_bias))
    hidden_pre = low_back(jnp.dot(second_rows, up_projection_weight, precision=highest) + up_bias)
    active_mask = low(jax.nn.gelu(hidden_pre, approximate=False))
    return valid_rows * (middle + (jnp.dot(active_mask, down_projection_weight, precision=highest) + down_bias))

def reference(inputs, lengths, norm1_gain, norm1_bias, query_key_value_weight, content_bias, position_bias, pos_weight, output_weight, out_bias, norm2_gain, norm2_bias, up_projection_weight, up_bias, down_projection_weight, down_bias, cotangent):
    params = tuple((weight_item.astype(jnp.float32) for weight_item in (norm1_gain, norm1_bias, query_key_value_weight, content_bias, position_bias, pos_weight, output_weight, out_bias, norm2_gain, norm2_bias, up_projection_weight, up_bias, down_projection_weight, down_bias)))
    zeros_grad = tuple((jnp.zeros(weight_item.shape, jnp.float32) for weight_item in params))

    def one_sequence(totals, seq_item):
        source, length, cot_rows = seq_item
        outcome, pull_back = jax.vjp(lambda rows_in, weight_set: layer(rows_in, weight_set, length), source.astype(jnp.float32), params)
        source_grad, weight_grads = pull_back(cot_rows.astype(jnp.float32))
        summed = tuple((total_item + grad_item for total_item, grad_item in zip(totals, weight_grads)))
        return (summed, (outcome.astype(jnp.bfloat16), source_grad))
    totals, (output, input_grad) = lax.scan(one_sequence, zeros_grad, (inputs, lengths, cotangent))
    return (output, input_grad, totals[0], totals[1], totals[2], totals[3], totals[4], totals[5], totals[6], totals[7], totals[8], totals[9], totals[10], totals[11], totals[12], totals[13])
```

```python
import functools

import jax
import jax.numpy as jnp
from jax import lax
from jax.experimental import pallas as pl
from jax.experimental.pallas import tpu as pltpu
from jax.sharding import PartitionSpec as P

ROWS = 512
HALF = 256
epsilon = 1e-05
score_scale = 0.125
masked_score = -1e30
NN = (((1,), (0,)), ((), ()))
NT = (((1,), (1,)), ((), ()))
f32 = jnp.float32
bf16 = jnp.bfloat16


def dot(a, b, dims=NN):
    return lax.dot_general(a, b, dims, preferred_element_type=f32)


def pieces(block):
    out = [(key * ROWS, ROWS, 0) for key in range(block)]
    out.append((block * ROWS, HALF, 0))
    out.append((block * ROWS + HALF, HALF, HALF))
    return out


def chunk(index, shift, blocks):
    return pl.ds(pl.multiple_of(lax.rem(index + shift, blocks) * ROWS, ROWS), ROWS)


def forward_kernel(
    blocks, shift_ref, qo_ref, qc_ref, k_ref, v_ref, w_ref, sin_ref, cos_ref, table_ref,
    o_ref, inv_ref, e_ref, keys, values, scores, query,
):
    width = qo_ref.shape[0]
    model = table_ref.shape[1]
    half = model // 2
    block = pl.program_id(1)

    @pl.when((pl.program_id(0) == 0) & (block == 0))
    def _():
        keys[:, :model] = table_ref[...]

    @pl.when(block == 0)
    def _():
        for index in range(blocks):
            lanes = chunk(index, shift_ref[0], blocks)
            here = pl.ds(index * ROWS, ROWS)
            keys[here, model:] = k_ref[:, lanes].T
            values[:, here] = v_ref[:, lanes]

    def run(index):
        pair = dot(w_ref[...], qo_ref[...])
        up, low = pair[:half], pair[half:]
        sine, cosine = sin_ref[...], cos_ref[...]
        query[:half] = ((up * sine + low * cosine) * score_scale).astype(bf16)
        query[half:model] = ((low * sine - up * cosine) * score_scale).astype(bf16)
        query[model:] = (qc_ref[...].astype(f32) * score_scale).astype(bf16)
        top = jnp.full((8, ROWS), masked_score, f32)
        for start, count, first in pieces(index):
            part = dot(keys[start : start + count, :], query[:, first:])
            if start >= index * ROWS:
                row = lax.broadcasted_iota(jnp.int32, part.shape, 0) + (start - index * ROWS)
                col = lax.broadcasted_iota(jnp.int32, part.shape, 1) + first
                part = jnp.where(col >= row, part, masked_score)
            scores[start : start + count, first:] = part
            best = jnp.max(part.reshape(count // 8, 8, ROWS - first), axis=0)
            if first:
                best = jnp.maximum(top[:, first:], best)
                top = jnp.concatenate([top[:, :first], best], axis=1)
            else:
                top = jnp.maximum(top, best)
        peak = jnp.max(top, axis=0, keepdims=True)
        total = jnp.zeros((8, ROWS), f32)
        out = jnp.zeros((width, ROWS), f32)
        for start, count, first in pieces(index):
            weight = jnp.exp(scores[start : start + count, first:] - peak[:, first:])
            gain = jnp.sum(weight.reshape(count // 8, 8, ROWS - first), axis=0)
            rounded = weight.astype(bf16)
            e_ref[start : start + count, first:] = rounded
            add = dot(values[:, start : start + count], rounded)
            if first:
                total = jnp.concatenate([total[:, :first], total[:, first:] + gain], axis=1)
                out = jnp.concatenate([out[:, :first], out[:, first:] + add], axis=1)
            else:
                total = total + gain
                out = out + add
        inverse = 1.0 / jnp.sum(total, axis=0, keepdims=True)
        o_ref[...] = out * inverse
        inv_ref[...] = inverse

    for index in range(blocks):
        pl.when(block == index)(functools.partial(run, index))


def attend_forward(shift, qo, qc, k, v, w, sine, cosine, table):
    heads, width, seq = qo.shape
    model = table.shape[1]
    blocks = seq // ROWS
    part = pl.BlockSpec((None, width, ROWS), lambda h, i, s: (h, 0, lax.rem(i + s[0], blocks)))
    whole = pl.BlockSpec((None, width, seq), lambda h, i, s: (h, 0, 0))
    wave = pl.BlockSpec((model // 2, ROWS), lambda h, i, s: (0, i))
    return pl.pallas_call(
        functools.partial(forward_kernel, blocks),
        grid_spec=pltpu.PrefetchScalarGridSpec(
            num_scalar_prefetch=1,
            grid=(heads, blocks),
            in_specs=[
                part, part, whole, whole,
                pl.BlockSpec((None, model, width), lambda h, i, s: (h, 0, 0)),
                wave, wave,
                pl.BlockSpec((seq, model), lambda h, i, s: (0, 0), pipeline_mode=pl.Buffered(1)),
            ],
            out_specs=[
                part,
                pl.BlockSpec((None, 1, ROWS), lambda h, i, s: (h, 0, i)),
                pl.BlockSpec((None, None, seq, ROWS), lambda h, i, s: (h, i, 0, 0)),
            ],
            scratch_shapes=[
                pltpu.VMEM((seq, model + width), bf16),
                pltpu.VMEM((width, seq), bf16),
                pltpu.VMEM((seq, ROWS), f32),
                pltpu.VMEM((model + width, ROWS), bf16),
            ],
        ),
        out_shape=[
            jax.ShapeDtypeStruct((heads, width, seq), f32),
            jax.ShapeDtypeStruct((heads, 1, seq), f32),
            jax.ShapeDtypeStruct((heads, blocks, seq, ROWS), bf16),
        ],
        compiler_params=pltpu.CompilerParams(vmem_limit_bytes=56 << 20),
        cost_estimate=pl.CostEstimate(
            flops=2 * heads * seq * seq * (model + 2 * width) * 5 // 8,
            bytes_accessed=heads * seq * seq * 2,
            transcendentals=heads * seq * seq // 2,
        ),
        name="attend_forward",
    )(shift, qo, qc, k, v, w, sine, cosine, table)


def backward_kernel(
    blocks, shift_ref, e_ref, do_ref, o_ref, inv_ref, qo_ref, qc_ref, k_ref, v_ref, w_ref,
    sin_ref, cos_ref, table_ref, dq_ref, dk_ref, dv_ref, dw_ref, bias_ref,
    keys, values, small, query_acc, k_acc, v_acc, w_acc, b_acc,
):
    width = qo_ref.shape[0]
    model = table_ref.shape[0]
    half = model // 2
    block = pl.program_id(1)

    @pl.when((pl.program_id(0) == 0) & (block == 0))
    def _():
        keys[:model] = table_ref[...]

    @pl.when(block == 0)
    def _():
        for index in range(blocks):
            lanes = chunk(index, shift_ref[0], blocks)
            here = pl.ds(index * ROWS, ROWS)
            keys[model:, here] = k_ref[:, lanes]
            values[here, :] = v_ref[:, lanes].T
        k_acc[...] = jnp.zeros_like(k_acc)
        v_acc[...] = jnp.zeros_like(v_acc)
        w_acc[...] = jnp.zeros_like(w_acc)
        b_acc[...] = jnp.zeros_like(b_acc)

    def run(index):
        scaled = (do_ref[...].astype(f32) * (inv_ref[...] * score_scale)).astype(bf16)
        delta = jnp.sum(scaled.astype(f32) * o_ref[...], axis=0, keepdims=True)
        for start, count, first in pieces(index):
            weight = e_ref[start : start + count, first:]
            grad = dot(values[start : start + count, :], scaled[:, first:])
            change = (weight.astype(f32) * (grad - delta[:, first:])).astype(bf16)
            add = dot(keys[:, start : start + count], change)
            if start == 0:
                query_acc[...] = add
            else:
                query_acc[:, first:] += add
            v_acc[:, start : start + count] += dot(scaled[:, first:], weight, NT)
            k_acc[:, start : start + count] += dot(qc_ref[:, first:], change, NT)
        sine, cosine = sin_ref[...], cos_ref[...]
        up, low = query_acc[:half], query_acc[half:model]
        small[:half] = (up * sine - low * cosine).astype(bf16)
        small[half:] = (up * cosine + low * sine).astype(bf16)
        offset = dot(w_ref[...], small[...])
        content = query_acc[model:]
        dq_ref[...] = (content + offset).astype(bf16)
        w_acc[...] += dot(qo_ref[...], small[...], NT)
        for lane in range(0, ROWS, 128):
            b_acc[0] += content[:, lane : lane + 128]
            b_acc[1] += offset[:, lane : lane + 128]

    for index in range(blocks):
        pl.when(block == index)(functools.partial(run, index))

    @pl.when(block == blocks - 1)
    def _():
        for index in range(blocks):
            lanes = chunk(index, shift_ref[0], blocks)
            here = pl.ds(index * ROWS, ROWS)
            dk_ref[:, lanes] = k_acc[:, here].astype(bf16)
            dv_ref[:, lanes] = (v_acc[:, here] * (1.0 / score_scale)).astype(bf16)
        dw_ref[...] = w_acc[...]
        bias_ref[...] = b_acc[...]


def attend_backward(shift, e, do, o, inv, qo, qc, k, v, w, sine, cosine, table):
    heads, width, seq = qo.shape
    model = table.shape[0]
    blocks = seq // ROWS
    part = pl.BlockSpec((None, width, ROWS), lambda h, i, s: (h, 0, lax.rem(i + s[0], blocks)))
    whole = pl.BlockSpec((None, width, seq), lambda h, i, s: (h, 0, 0))
    wave = pl.BlockSpec((model // 2, ROWS), lambda h, i, s: (0, i))
    weight = pl.BlockSpec((None, width, model), lambda h, i, s: (h, 0, 0))
    return pl.pallas_call(
        functools.partial(backward_kernel, blocks),
        grid_spec=pltpu.PrefetchScalarGridSpec(
            num_scalar_prefetch=1,
            grid=(heads, blocks),
            in_specs=[
                pl.BlockSpec((None, None, seq, ROWS), lambda h, i, s: (h, i, 0, 0)),
                part, part,
                pl.BlockSpec((None, 1, ROWS), lambda h, i, s: (h, 0, i)),
                part, part, whole, whole, weight, wave, wave,
                pl.BlockSpec((model, seq), lambda h, i, s: (0, 0), pipeline_mode=pl.Buffered(1)),
            ],
            out_specs=[
                part, whole, whole, weight,
                pl.BlockSpec((None, 2, width, 128), lambda h, i, s: (h, 0, 0, 0)),
            ],
            scratch_shapes=[
                pltpu.VMEM((model + width, seq), bf16),
                pltpu.VMEM((seq, width), bf16),
                pltpu.VMEM((model, ROWS), bf16),
                pltpu.VMEM((model + width, ROWS), f32),
                pltpu.VMEM((width, seq), f32),
                pltpu.VMEM((width, seq), f32),
                pltpu.VMEM((width, model), f32),
                pltpu.VMEM((2, width, 128), f32),
            ],
        ),
        out_shape=[
            jax.ShapeDtypeStruct((heads, width, seq), bf16),
            jax.ShapeDtypeStruct((heads, width, seq), bf16),
            jax.ShapeDtypeStruct((heads, width, seq), bf16),
            jax.ShapeDtypeStruct((heads, width, model), f32),
            jax.ShapeDtypeStruct((heads, 2, width, 128), f32),
        ],
        compiler_params=pltpu.CompilerParams(vmem_limit_bytes=56 << 20),
        cost_estimate=pl.CostEstimate(
            flops=2 * heads * seq * seq * (model + 4 * width) * 5 // 8,
            bytes_accessed=heads * seq * seq * 2,
            transcendentals=0,
        ),
        name="attend_backward",
    )(shift, e, do, o, inv, qo, qc, k, v, w, sine, cosine, table)


def waves(seq, model):
    frequency = jnp.power(
        10000.0, -jnp.arange(0, model, 2, dtype=jnp.int32).astype(f32) / model
    )
    angle = frequency[:, None] * jnp.arange(seq, dtype=jnp.int32).astype(f32)[None, :]
    sine, cosine = jnp.sin(angle), jnp.cos(angle)
    return sine, cosine, jnp.concatenate([cosine, sine], axis=0).astype(bf16)


class Paired:
    def __init__(self, dp_count):
        self.dp_count = dp_count
        self.core = lax.rem(lax.axis_index("dp"), 2)
        self.side = lax.axis_index("tensor")
        self.index = self.core

    def trade(self, value):
        pairs = []
        for place in range(2 * self.dp_count):
            group, core, side = place // 4, place // 2 % 2, place % 2
            pairs.append((place, group * 4 + side * 2 + core))
        return lax.ppermute(value, ("dp", "tensor"), pairs)

    def cross(self, value, flip):
        return lax.ppermute(value, "dp", [(i, i ^ flip) for i in range(self.dp_count)])

    def across(self, value):
        return lax.ppermute(value, "tensor", [(0, 1), (1, 0)])

    def shift(self, blocks):
        return jnp.reshape(self.index * (blocks // 2), (1,)).astype(jnp.int32)

    def gather(self, value):
        return jnp.concatenate([value, self.cross(value, 1)], axis=0)

    def scatter(self, value):
        rows = value.shape[0] // 2
        other = self.cross(value[rows:].astype(bf16), 1)
        return value[:rows] + other.astype(f32)

    def flips(self):
        flips, flip = [], 2
        while flip < self.dp_count:
            flips.append(flip)
            flip *= 2
        return flips

    def total(self, value):
        for flip in [1] + self.flips():
            value = value + self.cross(value, flip)
        return value + self.across(value)

    def sums(self, value):
        bits = [lax.rem(lax.axis_index("dp") // flip, 2) for flip in self.flips()]
        value = value.astype(bf16)

        def halve(value, bit, move):
            rows = value.shape[0] // 2
            keep = lax.dynamic_slice_in_dim(value, bit * rows, rows, 0)
            send = lax.dynamic_slice_in_dim(value, (1 - bit) * rows, rows, 0)
            return (keep.astype(f32) + move(send).astype(f32)).astype(bf16)

        def double(value, bit, move):
            other = move(value)
            return jnp.where(
                bit == 0,
                jnp.concatenate([value, other], axis=0),
                jnp.concatenate([other, value], axis=0),
            )

        for flip, bit in zip(self.flips(), bits):
            value = halve(value, bit, functools.partial(self.cross, flip=flip))
        value = self.trade(halve(value, self.side, self.across))
        value = double(value, self.core, functools.partial(self.cross, flip=1))
        for flip, bit in reversed(list(zip(self.flips(), bits))):
            value = double(value, bit, functools.partial(self.cross, flip=flip))
        return value.astype(f32)


class Plain:
    def __init__(self, tensor_count):
        self.index = lax.axis_index("tensor")

    def trade(self, value):
        return value

    def shift(self, blocks):
        return jnp.zeros((1,), jnp.int32)

    def gather(self, value):
        return lax.all_gather(value, "tensor", axis=0, tiled=True)

    def scatter(self, value):
        return lax.psum_scatter(value, "tensor", scatter_dimension=0, tiled=True)

    def total(self, value):
        return lax.psum(value, ("dp", "tensor"))

    def sums(self, value):
        return lax.psum(value.astype(bf16), "dp").astype(f32)


def norm_rows(values, norm_gain, norm_bias):
    centre = values - jnp.mean(values, axis=-1, keepdims=True)
    inverse = lax.rsqrt(jnp.mean(centre * centre, axis=-1, keepdims=True) + epsilon)
    normal = centre * inverse
    return (normal * norm_gain + norm_bias, normal, inverse)


def norm_back(upstream, normal, inverse, norm_gain):
    scaled = upstream * norm_gain
    centred = scaled - jnp.mean(scaled, axis=-1, keepdims=True)
    centred = centred - normal * jnp.mean(scaled * normal, axis=-1, keepdims=True)
    return (
        inverse * centred,
        jnp.sum(upstream * normal, axis=0),
        jnp.sum(upstream, axis=0),
    )


def product(spec, a, b):
    return jnp.einsum(spec, a, b, preferred_element_type=f32)


def local(
    inputs, lengths, norm1_gain, norm1_bias, query_key_value_weight, content_bias, position_bias,
    pos_weight, output_weight, out_bias, norm2_gain, norm2_bias, up_projection_weight, up_bias,
    down_projection_weight, down_bias, cotangent,
):
    tensor_count = lax.axis_size("tensor")
    dp_count = lax.axis_size("dp")
    moves = Paired(dp_count) if tensor_count == 2 and dp_count % 2 == 0 else Plain(tensor_count)
    _, shard_rows, model = inputs.shape
    seq = shard_rows * tensor_count
    heads, width = content_bias.shape
    flat = heads * width
    hidden = up_bias.shape[0]
    blocks = seq // ROWS
    shift = moves.shift(blocks)
    after = lax.optimization_barrier

    row = lax.axis_index("tensor") * shard_rows + jnp.arange(shard_rows, dtype=jnp.int32)
    valid = (row < lengths[0])[:, None]

    vectors = jnp.concatenate([content_bias.reshape(-1), position_bias.reshape(-1), up_bias])
    source, qkv_weight, vectors = (
        moves.trade(inputs[0]), moves.trade(query_key_value_weight), moves.trade(vectors)
    )
    later = after((source, qkv_weight, pos_weight, output_weight, up_projection_weight))
    source, qkv_weight = later[0], later[1]
    pos_weight, out_weight = moves.trade(later[2]), moves.trade(later[3])
    up_weight = moves.trade(later[4])
    down_weight = moves.trade(after((pos_weight, down_projection_weight))[1])
    cot = jnp.where(valid, cotangent[0], jnp.zeros_like(cotangent[0]))
    cot = moves.trade(after((up_weight, cot))[1])
    content_vector, position_vector = vectors[:flat], vectors[flat : 2 * flat]
    up_vector = vectors[2 * flat :]

    sine, cosine, table_t = waves(seq, model)
    table = table_t.T

    source = source.astype(f32)
    normed1, unit1, inverse1 = norm_rows(source, norm1_gain, norm1_bias)
    first_rows = moves.gather(normed1.astype(bf16))
    projected = product("nrk,sr->nks", qkv_weight, first_rows)
    shaped = (heads, width, seq)
    query_content = (projected[0] + content_vector[:, None]).astype(bf16).reshape(shaped)
    query_offset = (projected[0] + position_vector[:, None]).astype(bf16).reshape(shaped)
    key_rows = projected[1].astype(bf16).reshape(shaped)
    value_rows = projected[2].astype(bf16).reshape(shaped)
    pos_heads = pos_weight.reshape(model, heads, width)
    attended, inverse_sum, weights = attend_forward(
        shift, query_offset, query_content, key_rows, value_rows, pos_heads.transpose(1, 0, 2),
        sine, cosine, table,
    )
    attended_low = attended.reshape(flat, seq).astype(bf16)
    branch = moves.scatter(product("ks,ku->su", attended_low, out_weight))
    middle = source + (branch + out_bias)

    normed2, unit2, inverse2 = norm_rows(middle, norm2_gain, norm2_bias)
    second_rows = moves.gather(normed2.astype(bf16))
    hidden_pre = product("sr,rk->sk", second_rows, up_weight) + up_vector
    active, gelu_pull = jax.vjp(lambda v: jax.nn.gelu(v, approximate=False), hidden_pre)
    active = active.astype(bf16)
    ffn_out = moves.scatter(product("sk,ku->su", active, down_weight)) + down_bias
    output = moves.trade((middle + ffn_out).astype(bf16))
    output = jnp.where(valid, output, jnp.zeros_like(output))

    grad_rows = cot.astype(f32)
    all_grad = moves.gather(cot)
    down_weight_grad = product("sk,su->ku", active, all_grad)
    hidden_grad = product("su,ku->sk", all_grad, down_weight)
    pre_grad = gelu_pull(hidden_grad)[0].astype(bf16)
    up_weight_grad = product("sr,sk->rk", second_rows, pre_grad)
    up_bias_grad = jnp.sum(pre_grad.astype(f32), axis=0)
    upstream2 = moves.scatter(product("sk,rk->sr", pre_grad, up_weight))
    middle_part, gain2_grad, bias2_grad = norm_back(upstream2, unit2, inverse2, norm2_gain)
    middle_grad = grad_rows + middle_part
    branch_grad = middle_grad.astype(bf16)
    all_branch = moves.gather(branch_grad)
    out_weight_grad = product("ks,su->ku", attended_low, all_branch)
    early = moves.sums(
        jnp.concatenate([up_weight_grad.reshape(-1, model), down_weight_grad, out_weight_grad])
    )
    attended_grad = product("ku,su->ks", out_weight, all_branch).astype(bf16).reshape(shaped)
    query_grad, key_grad, value_grad, pos_grad, bias_grads = attend_backward(
        shift, weights, attended_grad, attended, inverse_sum, query_offset, query_content,
        key_rows, value_rows, pos_heads.transpose(1, 2, 0), sine, cosine, table_t,
    )
    stacked = jnp.stack([query_grad, key_grad, value_grad]).reshape(3, flat, seq)
    qkv_weight_grad = product("nks,sr->nkr", stacked, first_rows)
    late = moves.sums(
        jnp.concatenate([qkv_weight_grad.reshape(3 * flat, model), pos_grad.reshape(flat, model)])
    )
    upstream1 = moves.scatter(product("nks,nrk->sr", stacked, qkv_weight))
    input_part, gain1_grad, bias1_grad = norm_back(upstream1, unit1, inverse1, norm1_gain)
    input_grad = moves.trade((middle_grad + input_part).astype(bf16)).astype(f32)

    bias_grads = jnp.sum(bias_grads, axis=-1)

    def placed(vector):
        count = vector.shape[0]
        room = jnp.zeros((count * tensor_count,), f32)
        return lax.dynamic_update_slice_in_dim(room, vector, moves.index * count, 0)

    parts = [
        gain1_grad, bias1_grad, jnp.sum(branch_grad.astype(f32), axis=0), gain2_grad, bias2_grad,
        jnp.sum(grad_rows, axis=0), placed(bias_grads[:, 0].reshape(-1)),
        placed(bias_grads[:, 1].reshape(-1)), placed(up_bias_grad),
    ]
    small = moves.total(jnp.concatenate(parts).reshape(-1, 128)).reshape(-1)
    side = lax.axis_index("tensor")
    vectors, place = [], 0
    for part in parts[:6]:
        vectors.append(small[place : place + model])
        place += model
    for count in (flat, flat, hidden):
        here = small[place : place + count * tensor_count]
        vectors.append(lax.dynamic_slice_in_dim(here, side * count, count, 0))
        place += count * tensor_count

    up_rows = model * hidden // model
    return (
        output[None],
        input_grad[None],
        vectors[0],
        vectors[1],
        late[: 3 * flat].reshape(3, flat, model).transpose(0, 2, 1),
        vectors[6].reshape(heads, width),
        vectors[7].reshape(heads, width),
        late[3 * flat :].T,
        early[up_rows + hidden :],
        vectors[2],
        vectors[3],
        vectors[4],
        early[:up_rows].reshape(model, hidden),
        vectors[8],
        early[up_rows : up_rows + hidden],
        vectors[5],
    )


def solution(mesh):
    rows = P("dp", "tensor", None)
    return jax.shard_map(
        local,
        mesh=mesh,
        in_specs=(
            rows, P("dp"), P(), P(), P(None, None, "tensor"), P("tensor", None),
            P("tensor", None), P(None, "tensor"), P("tensor", None), P(), P(), P(),
            P(None, "tensor"), P("tensor"), P("tensor", None), P(), rows,
        ),
        out_specs=(
            rows, rows, P(), P(), P(None, None, "tensor"), P("tensor", None),
            P("tensor", None), P(None, "tensor"), P("tensor", None), P(), P(), P(),
            P(None, "tensor"), P("tensor"), P("tensor", None), P(),
        ),
        check_vma=False,
    )
```

```python
import functools

import jax
import jax.numpy as jnp
from jax import lax
from jax.experimental import pallas as pl
from jax.experimental.pallas import tpu as pltpu
from jax.sharding import PartitionSpec as P

ROWS = 512
HALF = 256
epsilon = 1e-05
score_scale = 0.125
masked_score = -1e30
NN = (((1,), (0,)), ((), ()))
NT = (((1,), (1,)), ((), ()))
TN = (((0,), (0,)), ((), ()))
TT = (((0,), (1,)), ((), ()))
f32 = jnp.float32
bf16 = jnp.bfloat16
FORWARD_CALLS = 2
BACKWARD_CALLS = 2


def dot(a, b, dims=NN):
    return lax.dot_general(a, b, dims, preferred_element_type=f32)


def resident(shape):
    return pl.BlockSpec(shape, lambda *_: (0,) * len(shape), pipeline_mode=pl.Buffered(1))


def project_kernel(part_count, flag_ref, *refs):
    rows = refs[:part_count]
    own_ref, got_ref, q_ref, kv_ref, weight = refs[part_count:]
    part, block = pl.program_id(0), pl.program_id(1)
    model, flat = own_ref.shape[1:]

    def fill(read):
        for index in range(3):
            weight[index * flat : (index + 1) * flat, :] = read(index).T

    first = (part == 0) & (block == 0)
    pl.when(first & (flag_ref[0] == 1))(lambda: fill(lambda index: own_ref[index]))
    pl.when(first & (flag_ref[0] == 0))(
        lambda: fill(lambda index: got_ref[index * model : (index + 1) * model, :])
    )

    def run(ref):
        here = ref[pl.ds(pl.multiple_of(block * ROWS, ROWS), ROWS), :]
        result = dot(weight[...], here, NT)
        q_ref[...] = result[:flat]
        kv_ref[0] = result[flat : 2 * flat].astype(bf16)
        kv_ref[1] = result[2 * flat :].astype(bf16)

    for index in range(part_count):
        pl.when(part == index)(functools.partial(run, rows[index]))


def project(home, rows, own, got):
    count = len(rows)
    n, model = rows[0].shape
    flat = own.shape[2]
    return pl.pallas_call(
        functools.partial(project_kernel, count),
        grid_spec=pltpu.PrefetchScalarGridSpec(
            num_scalar_prefetch=1,
            grid=(count, n // ROWS),
            in_specs=[resident((n, model))] * count + [resident(own.shape), resident((3 * model, flat))],
            out_specs=[
                pl.BlockSpec((None, flat, ROWS), lambda p, j, s: (p, 0, j)),
                pl.BlockSpec((2, None, flat, ROWS), lambda p, j, s: (0, p, 0, j)),
            ],
            scratch_shapes=[pltpu.VMEM((3 * flat, model), bf16)],
        ),
        out_shape=[
            jax.ShapeDtypeStruct((count, flat, n), f32),
            jax.ShapeDtypeStruct((2, count, flat, n), bf16),
        ],
        compiler_params=pltpu.CompilerParams(vmem_limit_bytes=32 << 20),
        cost_estimate=pl.CostEstimate(
            flops=6 * count * n * model * flat, bytes_accessed=count * n * (model + 4 * flat) * 2,
            transcendentals=0,
        ),
        name="project",
    )(home, *rows, own, got)


def pieces(block):
    out = [(key * ROWS, ROWS, 0) for key in range(block)]
    out.append((block * ROWS, HALF, 0))
    out.append((block * ROWS + HALF, HALF, HALF))
    return out


def place(index, shift, blocks, per_part):
    held = lax.rem(index + shift, blocks)
    lanes = pl.ds(pl.multiple_of(lax.rem(held, per_part) * ROWS, ROWS), ROWS)
    return held // per_part, lanes


def forward_kernel(
    blocks, shift_ref, q_ref, kv_ref, bias_ref, w_ref, sin_ref, cos_ref, table_ref,
    low_ref, o_ref, inv_ref, e_ref, keys, values, scores, query,
):
    width = q_ref.shape[0]
    model = table_ref.shape[1]
    half = model // 2
    per_part = kv_ref.shape[3] // ROWS
    block = pl.program_id(1)

    @pl.when((pl.program_id(0) == 0) & (block == 0))
    def _():
        keys[:, :model] = table_ref[...]

    @pl.when(block == 0)
    def _():
        for index in range(blocks):
            part, lanes = place(index, shift_ref[0], blocks, per_part)
            here = pl.ds(index * ROWS, ROWS)
            keys[here, model:] = kv_ref[0, part, :, lanes].T
            values[:, here] = kv_ref[1, part, :, lanes]

    def run(index):
        offset = (q_ref[...] + bias_ref[:, 1:]).astype(bf16)
        pair = dot(w_ref[...], offset, TN)
        up, low = pair[:half], pair[half:]
        sine, cosine = sin_ref[...], cos_ref[...]
        query[:half] = ((up * sine + low * cosine) * score_scale).astype(bf16)
        query[half:model] = ((low * sine - up * cosine) * score_scale).astype(bf16)
        content = (q_ref[...] + bias_ref[:, :1]).astype(bf16)
        query[model:] = (content.astype(f32) * score_scale).astype(bf16)
        top = jnp.full((8, ROWS), masked_score, f32)
        for start, count, first in pieces(index):
            part = dot(keys[start : start + count, :], query[:, first:])
            if start >= index * ROWS:
                row = lax.broadcasted_iota(jnp.int32, part.shape, 0) + (start - index * ROWS)
                col = lax.broadcasted_iota(jnp.int32, part.shape, 1) + first
                part = jnp.where(col >= row, part, masked_score)
            scores[start : start + count, first:] = part
            best = jnp.max(part.reshape(count // 8, 8, ROWS - first), axis=0)
            if first:
                best = jnp.maximum(top[:, first:], best)
                top = jnp.concatenate([top[:, :first], best], axis=1)
            else:
                top = jnp.maximum(top, best)
        peak = jnp.max(top, axis=0, keepdims=True)
        total = jnp.zeros((8, ROWS), f32)
        out = jnp.zeros((width, ROWS), f32)
        for start, count, first in pieces(index):
            weight = jnp.exp(scores[start : start + count, first:] - peak[:, first:])
            gain = jnp.sum(weight.reshape(count // 8, 8, ROWS - first), axis=0)
            rounded = weight.astype(bf16)
            e_ref[start : start + count, first:] = rounded
            add = dot(values[:, start : start + count], rounded)
            if first:
                total = jnp.concatenate([total[:, :first], total[:, first:] + gain], axis=1)
                out = jnp.concatenate([out[:, :first], out[:, first:] + add], axis=1)
            else:
                total = total + gain
                out = out + add
        inverse = 1.0 / jnp.sum(total, axis=0, keepdims=True)
        out = out * inverse
        o_ref[...] = out
        low_ref[...] = out.astype(bf16)
        inv_ref[...] = inverse

    for index in range(blocks):
        pl.when(block == index)(functools.partial(run, index))


def attend_forward(width, first, heads, shift, q, kv, biases, w, sine, cosine, table):
    parts, _, n = q.shape
    seq, model = table.shape

    blocks, per_part = seq // ROWS, n // ROWS

    def part(offset):
        def index(h, i, s):
            held = lax.rem(i + s[0], blocks)
            return (held // per_part, h + offset, lax.rem(held, per_part))

        return pl.BlockSpec((None, width, ROWS), index)

    column = pl.BlockSpec((width, 2), lambda h, i, s: (h + first, 0))
    wave = pl.BlockSpec((model // 2, ROWS), lambda h, i, s: (0, i))
    return pl.pallas_call(
        functools.partial(forward_kernel, blocks),
        grid_spec=pltpu.PrefetchScalarGridSpec(
            num_scalar_prefetch=1,
            grid=(heads, blocks),
            in_specs=[
                part(first),
                pl.BlockSpec((2, parts, width, n), lambda h, i, s: (0, 0, h + first, 0)),
                column,
                pl.BlockSpec((width, model), lambda h, i, s: (h + first, 0)),
                wave, wave, resident((seq, model)),
            ],
            out_specs=[
                part(0),
                pl.BlockSpec((None, width, ROWS), lambda h, i, s: (h, 0, i)),
                pl.BlockSpec((None, 1, ROWS), lambda h, i, s: (h, 0, i)),
                pl.BlockSpec((None, None, seq, ROWS), lambda h, i, s: (h, i, 0, 0)),
            ],
            scratch_shapes=[
                pltpu.VMEM((seq, model + width), bf16),
                pltpu.VMEM((width, seq), bf16),
                pltpu.VMEM((seq, ROWS), f32),
                pltpu.VMEM((model + width, ROWS), bf16),
            ],
        ),
        out_shape=[
            jax.ShapeDtypeStruct((parts, heads * width, n), bf16),
            jax.ShapeDtypeStruct((heads, width, seq), f32),
            jax.ShapeDtypeStruct((heads, 1, seq), f32),
            jax.ShapeDtypeStruct((heads, blocks, seq, ROWS), bf16),
        ],
        compiler_params=pltpu.CompilerParams(vmem_limit_bytes=56 << 20),
        cost_estimate=pl.CostEstimate(
            flops=2 * heads * seq * seq * (model + 2 * width) * 5 // 8,
            bytes_accessed=heads * seq * seq * 2,
            transcendentals=heads * seq * seq // 2,
        ),
        name="attend_forward",
    )(shift, q, kv, biases, w, sine, cosine, table)


def backward_kernel(
    blocks, part_count, chained, shift_ref, e_ref, o_ref, inv_ref, q_ref, kv_ref, bias_ref, w_ref, sin_ref, cos_ref, table_ref, *refs,
):
    rows, dos = refs[:part_count], refs[part_count : 2 * part_count]
    refs = refs[2 * part_count + chained :]
    grad_ref, weight_ref, bias_grad_ref = refs[:3]
    keys, values, small, query_acc, k_acc, v_acc, w_acc, b_acc = refs[3:]
    width = q_ref.shape[0]
    model = table_ref.shape[0]
    half = model // 2
    per_part = kv_ref.shape[3] // ROWS
    block = pl.program_id(1)

    @pl.when((pl.program_id(0) == 0) & (block == 0))
    def _():
        keys[:model] = table_ref[...]

    @pl.when(block == 0)
    def _():
        for index in range(blocks):
            part, lanes = place(index, shift_ref[0], blocks, per_part)
            here = pl.ds(index * ROWS, ROWS)
            keys[model:, here] = kv_ref[0, part, :, lanes]
            values[here, :] = kv_ref[1, part, :, lanes].T
        k_acc[...] = jnp.zeros_like(k_acc)
        v_acc[...] = jnp.zeros_like(v_acc)
        w_acc[...] = jnp.zeros_like(w_acc)
        b_acc[...] = jnp.zeros_like(b_acc)

    def run(index):
        held = place(index, shift_ref[0], blocks, per_part)[0]
        out_grad = dos[0][...]
        for part in range(1, part_count):
            out_grad = jnp.where(held == part, dos[part][...], out_grad)
        scaled = (out_grad.astype(f32) * (inv_ref[...] * score_scale)).astype(bf16)
        delta = jnp.sum(scaled.astype(f32) * o_ref[...], axis=0, keepdims=True)
        content_low = (q_ref[...] + bias_ref[:, :1]).astype(bf16)
        for start, count, first in pieces(index):
            weight = e_ref[start : start + count, first:]
            grad = dot(values[start : start + count, :], scaled[:, first:])
            change = (weight.astype(f32) * (grad - delta[:, first:])).astype(bf16)
            add = dot(keys[:, start : start + count], change)
            if start == 0:
                query_acc[...] = add
            else:
                query_acc[:, first:] += add
            v_acc[:, start : start + count] += dot(scaled[:, first:], weight, NT)
            k_acc[:, start : start + count] += dot(content_low[:, first:], change, NT)
        sine, cosine = sin_ref[...], cos_ref[...]
        up, low = query_acc[:half], query_acc[half:model]
        small[:half] = (up * sine - low * cosine).astype(bf16)
        small[half:] = (up * cosine + low * sine).astype(bf16)
        offset = dot(w_ref[...], small[...])
        content = query_acc[model:]
        part, lanes = place(index, shift_ref[0], blocks, per_part)
        grad_ref[part, 0, :, lanes] = (content + offset).astype(bf16)
        offset_low = (q_ref[...] + bias_ref[:, 1:]).astype(bf16)
        w_acc[...] += dot(offset_low, small[...], NT)
        for lane in range(0, ROWS, 128):
            b_acc[0] += content[:, lane : lane + 128]
            b_acc[1] += offset[:, lane : lane + 128]

    for index in range(blocks):
        pl.when(block == index)(functools.partial(run, index))

    @pl.when(block == blocks - 1)
    def _():
        for index in range(blocks):
            part, lanes = place(index, shift_ref[0], blocks, per_part)
            here = pl.ds(index * ROWS, ROWS)
            grad_ref[part, 1, :, lanes] = k_acc[:, here].astype(bf16)
            grad_ref[part, 2, :, lanes] = (v_acc[:, here] * (1.0 / score_scale)).astype(bf16)
        total = None
        for part in range(part_count):
            stacked = jnp.concatenate([grad_ref[part, index] for index in range(3)], axis=0)
            term = dot(stacked, rows[part][...])
            total = term if total is None else total + term
        weight_ref[: 3 * width] = total.astype(bf16)
        weight_ref[3 * width :] = w_acc[...].astype(bf16)
        bias_grad_ref[...] = b_acc[...]


def attend_backward(
    width, first, heads, kept_first, before, shift, e, dos, o, inv, q, kv, biases, w, sine, cosine, table, rows
):
    parts, flat, n = q.shape
    model, seq = table.shape

    blocks, per_part = seq // ROWS, n // ROWS
    skip = first - kept_first

    def index_part(h, i, s):
        held = lax.rem(i + s[0], blocks)
        return (held // per_part, h + first, lax.rem(held, per_part))

    def grad_part(number):
        def index(h, i, s):
            held = lax.rem(i + s[0], blocks)
            return (h + first, jnp.where(held // per_part == number, lax.rem(held, per_part), 0))

        return pl.BlockSpec((width, ROWS), index)

    part = pl.BlockSpec((None, width, ROWS), index_part)
    column = pl.BlockSpec((width, 2), lambda h, i, s: (h + first, 0))
    wave = pl.BlockSpec((model // 2, ROWS), lambda h, i, s: (0, i))
    chained = [] if before is None else [before]
    arguments = [
        shift, e, o, inv, q, kv, biases, w, sine, cosine, table, *rows, *dos, *chained
    ]
    return pl.pallas_call(
        functools.partial(backward_kernel, blocks, parts, len(chained)),
        grid_spec=pltpu.PrefetchScalarGridSpec(
            num_scalar_prefetch=1,
            grid=(heads, blocks),
            in_specs=[
                pl.BlockSpec((None, None, seq, ROWS), lambda h, i, s: (h + skip, i, 0, 0)),
                pl.BlockSpec((None, width, ROWS), lambda h, i, s: (h + skip, 0, i)),
                pl.BlockSpec((None, 1, ROWS), lambda h, i, s: (h + skip, 0, i)),
                part,
                pl.BlockSpec((2, parts, width, n), lambda h, i, s: (0, 0, h + first, 0)),
                column,
                pl.BlockSpec((width, model), lambda h, i, s: (h + first, 0)),
                wave, wave, resident((model, seq)),
                *[resident((n, model))] * parts,
                *[grad_part(index) for index in range(parts)],
                *[pl.BlockSpec(memory_space=pl.ANY)] * len(chained),
            ],
            out_specs=[
                pl.BlockSpec((parts, 3, width, n), lambda h, i, s: (0, 0, h + first, 0)),
                pl.BlockSpec((None, 4 * width, model), lambda h, i, s: (h, 0, 0)),
                pl.BlockSpec((None, 2, width, 128), lambda h, i, s: (h, 0, 0, 0)),
            ],
            scratch_shapes=[
                pltpu.VMEM((model + width, seq), bf16),
                pltpu.VMEM((seq, width), bf16),
                pltpu.VMEM((model, ROWS), bf16),
                pltpu.VMEM((model + width, ROWS), f32),
                pltpu.VMEM((width, seq), f32),
                pltpu.VMEM((width, seq), f32),
                pltpu.VMEM((width, model), f32),
                pltpu.VMEM((2, width, 128), f32),
            ],
        ),
        out_shape=[
            jax.ShapeDtypeStruct((parts, 3, flat, n), bf16),
            jax.ShapeDtypeStruct((heads, 4 * width, model), bf16),
            jax.ShapeDtypeStruct((heads, 2, width, 128), f32),
        ],
        input_output_aliases={len(arguments) - 1: 0} if chained else {},
        compiler_params=pltpu.CompilerParams(vmem_limit_bytes=56 << 20),
        cost_estimate=pl.CostEstimate(
            flops=2 * heads * seq * seq * (model + 4 * width) * 5 // 8,
            bytes_accessed=heads * seq * seq * 2,
            transcendentals=0,
        ),
        name="attend_backward",
    )(*arguments)


def waves_kernel(near_sin_ref, near_cos_ref, far_sin_ref, far_cos_ref, sin_ref, cos_ref, table_t_ref, table_ref):
    half = sin_ref.shape[0]
    for index in range(ROWS // 128):
        here = slice(index * 128, (index + 1) * 128)
        far_sin, far_cos = far_sin_ref[:, here], far_cos_ref[:, here]
        sin_ref[:, here] = far_sin * near_cos_ref[...] + far_cos * near_sin_ref[...]
        cos_ref[:, here] = far_cos * near_cos_ref[...] - far_sin * near_sin_ref[...]
    table_t_ref[:half] = cos_ref[...].astype(bf16)
    table_t_ref[half:] = sin_ref[...].astype(bf16)
    table_ref[...] = table_t_ref[...].T


def waves(seq, model):
    exponent = -jnp.arange(0, model, 2, dtype=jnp.int32).astype(f32) / model
    frequency = jnp.power(10000.0, exponent)[:, None]
    near = frequency * jnp.arange(128, dtype=jnp.int32).astype(f32)[None, :]
    far = frequency * (128 * jnp.arange(seq // 128, dtype=jnp.int32)).astype(f32)[None, :]

    def spread(value):
        return jnp.repeat(value, 128, axis=1)

    half = model // 2
    column = pl.BlockSpec((half, ROWS), lambda i: (0, i))
    return pl.pallas_call(
        waves_kernel,
        grid=(seq // ROWS,),
        in_specs=[resident((half, 128))] * 2 + [column] * 2,
        out_specs=[column, column, pl.BlockSpec((model, ROWS), lambda i: (0, i)),
                   pl.BlockSpec((ROWS, model), lambda i: (i, 0))],
        out_shape=[
            jax.ShapeDtypeStruct((half, seq), f32), jax.ShapeDtypeStruct((half, seq), f32),
            jax.ShapeDtypeStruct((model, seq), bf16), jax.ShapeDtypeStruct((seq, model), bf16),
        ],
        cost_estimate=pl.CostEstimate(flops=6 * half * seq, bytes_accessed=16 * half * seq, transcendentals=0),
        name="waves",
    )(jnp.sin(near), jnp.cos(near), spread(jnp.sin(far)), spread(jnp.cos(far)))


def middle_kernel(piece_count, flag_ref, *refs):
    refs = list(refs)

    def take(count):
        out = refs[:count]
        del refs[:count]
        return out

    ins, cots, mine, theirs = take(2), take(2), take(piece_count), take(piece_count)
    out_hbm, down_hbm, up_hbm, first_hbm, second_hbm, bias_ref, vec_ref = take(7)
    y_ref, mg_ref, ag_mine_ref, ag_other_ref, keep_ref, send_ref, sum_ref, bias_grad_ref = take(8)
    source, cotangent, att, out_w, down_w, up_w, first_w, second_w, sems = refs
    model = source.shape[1]
    size = out_hbm.shape[0]
    core, side = flag_ref[0], flag_ref[1]
    rest = first_hbm.shape[0] - size // 2
    copies = []

    def copy(from_ref, to_ref):
        copies.append(pltpu.make_async_copy(from_ref, to_ref, sems.at[len(copies)]))
        return copies[-1]

    def aligned(start, count):
        return pl.ds(pl.multiple_of(start, count), count)

    begin = []
    for pieces_of, half, index in ((mine, core, 0), (theirs, 1 - core, 1)):
        for number, ref in enumerate(pieces_of):
            count = ref.shape[1]
            begin.append(copy(ref.at[index], att.at[aligned(half * size + number * count, count), :]))
    begin.append(copy(out_hbm, out_w.at[aligned(side * size, size), :]))
    quarter = size // 2
    for ref, part in ((first_hbm, core), (second_hbm, 1 - core)):
        to = out_w.at[aligned((1 - side) * size + part * quarter, quarter), :]
        begin.append(copy(ref.at[pl.ds(0, quarter), :], to))
    ups = copy(up_hbm, up_w)
    downs = copy(down_hbm, down_w)
    extra = [
        copy(ref.at[pl.ds(quarter, rest), :], to)
        for ref, to in ((first_hbm, first_w), (second_hbm, second_w))
    ]
    at = len(copies)

    def choose(pair, to, number):
        both = [pltpu.make_async_copy(ref, to, sems.at[number]) for ref in pair]
        pl.when(core == side)(both[0].start)
        pl.when(core != side)(both[1].start)
        return both[0]

    for item in begin:
        item.start()
    source_copy = choose(ins, source, at)
    ups.start()
    cot_copy = choose(cots, cotangent, at + 1)
    downs.start()
    for item in extra:
        item.start()

    out_bias, gain, bias, down_bias = (vec_ref[i : i + 1, :] for i in range(4))
    for item in begin:
        item.wait()
    branch = dot(att[...], out_w[...], TN)
    source_copy.wait()
    middle = source[...].astype(f32) + (branch + out_bias)
    centre = middle - jnp.mean(middle, axis=1, keepdims=True)
    inverse = lax.rsqrt(jnp.mean(centre * centre, axis=1, keepdims=True) + epsilon)
    unit = centre * inverse
    rows2 = (unit * gain + bias).astype(bf16)
    ups.wait()
    cot_copy.wait()
    downs.wait()
    for item in extra:
        item.wait()
    cot = cotangent[...]
    y = e = None
    for number in range(4):
        if number < 2:
            part = core if number == 0 else 1 - core
            here = aligned(part * model, model)
            down, up, up_bias = down_w[here, :], up_w[:, here], bias_ref[:, here]
            half = side
        else:
            part = core if number == 2 else 1 - core
            ref = first_w if number == 2 else second_w
            down, up = ref[:model, :], ref[model : 2 * model, :]
            up_bias = jnp.sum(ref[2 * model : 2 * model + 16, :].astype(f32), axis=0, keepdims=True)
            half = 1 - side
        result = (keep_ref, send_ref)[number % 2]
        pre = dot(rows2, up) + up_bias
        cdf = 0.5 * (1.0 + lax.erf(pre * 0.7071067811865476))
        active = (pre * cdf).astype(bf16)
        slope = cdf + pre * (jnp.exp(pre * pre * -0.5) * 0.3989422804014327)
        low = (slope * dot(cot, down, NT)).astype(bf16)
        bias_grad_ref[pl.ds(half * 2 + part, 1), :] = jnp.sum(low.astype(f32), axis=0, keepdims=True)
        add_y, add_e = dot(active, down), dot(low, up, NT)
        y = add_y if y is None else y + add_y
        e = add_e if e is None else e + add_e
        result[number // 2, quarter : quarter + model, :] = dot(active, cot, TN).astype(bf16)
        result[number // 2, quarter + model :, :] = dot(rows2, low, TN).astype(bf16)
    y_ref[...] = (middle + (y + down_bias)).astype(bf16)
    grad = cot.astype(f32)
    scaled = e * gain
    change = scaled - jnp.mean(scaled, axis=1, keepdims=True)
    change = change - unit * jnp.mean(scaled * unit, axis=1, keepdims=True)
    middle_grad = grad + inverse * change
    mg_ref[...] = middle_grad
    low_grad = middle_grad.astype(bf16)
    sums = (low_grad.astype(f32), e * unit, e, grad)
    for index, term in enumerate(sums):
        sum_ref[index : index + 1, :] = jnp.sum(term, axis=0, keepdims=True)
    ag_mine_ref[...] = dot(out_w[aligned(core * size, size), :], low_grad, NT).astype(bf16)
    ag_other_ref[...] = dot(out_w[aligned((1 - core) * size, size), :], low_grad, NT).astype(bf16)
    for number, half in ((0, side), (1, 1 - side)):
        for ref, part in ((keep_ref, core), (send_ref, 1 - core)):
            rows = att[aligned(half * size + part * quarter, quarter), :]
            ref[number, :quarter, :] = dot(rows, low_grad).astype(bf16)


def middle_layer(flags, ins, cots, mine, theirs, own, first, second, bias, vectors):
    n, model = ins[0].shape
    size, hidden = own[0].shape[0], own[1].shape[0]
    quarter = size // 2
    packed = quarter + 2 * model
    extra = first.shape[0] - quarter
    anywhere = pl.BlockSpec(memory_space=pl.ANY)
    vmem = pl.BlockSpec(memory_space=pltpu.VMEM)
    arguments = [flags, *ins, *cots, *mine, *theirs, *own, first, second, bias, vectors]
    shapes = [
        jax.ShapeDtypeStruct((n, model), bf16),
        jax.ShapeDtypeStruct((n, model), f32),
        jax.ShapeDtypeStruct((size, n), bf16),
        jax.ShapeDtypeStruct((size, n), bf16),
        jax.ShapeDtypeStruct((2, packed, model), bf16),
        jax.ShapeDtypeStruct((2, packed, model), bf16),
        jax.ShapeDtypeStruct((4, model), f32),
        jax.ShapeDtypeStruct((4, model), f32),
    ]
    return pl.pallas_call(
        functools.partial(middle_kernel, len(mine)),
        in_specs=[pl.BlockSpec(memory_space=pltpu.SMEM)] + [anywhere] * (len(arguments) - 3) + [vmem] * 2,
        out_specs=[vmem] * len(shapes),
        out_shape=shapes,
        scratch_shapes=[
            pltpu.VMEM((n, model), bf16), pltpu.VMEM((n, model), bf16),
            pltpu.VMEM((2 * size, n), bf16), pltpu.VMEM((2 * size, model), bf16),
            pltpu.VMEM((hidden, model), bf16), pltpu.VMEM((model, hidden), bf16),
            pltpu.VMEM((extra, model), bf16), pltpu.VMEM((extra, model), bf16),
            pltpu.SemaphoreType.DMA((2 * len(mine) + 9,)),
        ],
        compiler_params=pltpu.CompilerParams(vmem_limit_bytes=60 << 20),
        cost_estimate=pl.CostEstimate(
            flops=2 * n * model * (6 * size + 12 * hidden),
            bytes_accessed=n * model * 14 + 8 * packed * model * 2,
            transcendentals=4 * n * hidden,
        ),
        name="middle_layer",
    )(*arguments)


class Paired:
    def __init__(self, dp_count):
        self.dp_count = dp_count
        self.core = lax.rem(lax.axis_index("dp"), 2)
        self.side = lax.axis_index("tensor")
        self.home = self.core == self.side
        self.index = self.core

    def trade(self, value):
        pairs = []
        for place in range(2 * self.dp_count):
            group, core, side = place // 4, place // 2 % 2, place % 2
            if core != side:
                pairs.append((place, group * 4 + side * 2 + core))
        return lax.ppermute(value, ("dp", "tensor"), pairs)

    def cross(self, value, flip):
        return lax.ppermute(value, "dp", [(i, i ^ flip) for i in range(self.dp_count)])

    def partner(self, value):
        return self.cross(value, 1)

    def across(self, value):
        return lax.ppermute(value, "tensor", [(0, 1), (1, 0)])

    def own(self, mine, traded):
        return jnp.where(self.home, mine, traded)

    def shift(self, blocks):
        return jnp.reshape(self.core * (blocks // 2), (1,)).astype(jnp.int32)

    def shared(self, value):
        return [value, self.partner(value)]

    def last_weights(self, out, down, up, bias):
        quarter, model = out.shape[0] // 2, out.shape[1]
        pack = jnp.concatenate([
            lax.dynamic_slice_in_dim(out, self.core * quarter, quarter, 0),
            lax.dynamic_slice_in_dim(down, self.core * model, model, 0),
            lax.dynamic_slice_in_dim(up, self.core * model, model, 1),
            terms_of(lax.dynamic_slice_in_dim(bias, self.core * model, model, 0), 16),
        ])
        return (out, down, up), self.across(pack), bias

    def last_second(self, first):
        return first, self.partner(first)

    def to_rows(self, attended):
        return attended, self.partner(attended)

    def to_heads(self, mine, other):
        return [mine, self.partner(other)]

    def scatter(self, terms):
        other = self.partner(terms[1]().astype(bf16))
        return terms[0]() + other.astype(f32)

    def total(self, value):
        flip = 1
        while flip < self.dp_count:
            value = value + self.cross(value, flip)
            flip *= 2
        return value + self.across(value)

    def swap(self, value):
        groups = [list(range(core, self.dp_count, 2)) for core in range(2)]
        return lax.all_to_all(value, "dp", 0, 0, axis_index_groups=groups, tiled=True)


    def early_start(self, keep, send):
        got = self.partner(send)
        kept, gone = (add(keep[index], got[index]) for index in range(2))
        return kept, self.across(gone)

    def late_start(self, grads):
        keep = jnp.where(self.core == 0, grads[0], grads[1])
        got = self.partner(jnp.where(self.core == 0, grads[1], grads[0]))
        kept = jnp.where(self.home, keep, got)
        return kept, self.across(jnp.where(self.home, got, keep))

    def spread(self, value):
        count = self.dp_count // 2
        terms = self.swap(value).reshape(count, value.shape[0] // count, -1)
        return jnp.sum(terms.astype(f32), axis=0).astype(bf16)

    def collect(self, value):
        copies = jnp.broadcast_to(value[None], (self.dp_count // 2, *value.shape))
        value = self.swap(copies.reshape(-1, value.shape[1]))
        other = self.partner(value)
        first = self.core == 0
        return jnp.where(first, value, other), jnp.where(first, other, value)


def add(a, b):
    return (a.astype(f32) + b.astype(f32)).astype(bf16)


def terms_of(vector, rows):
    terms, rest = [], vector
    for _ in range(3):
        terms.append(lax.reduce_precision(rest, 8, 7))
        rest = rest - terms[-1]
    terms += [jnp.zeros_like(vector)] * (rows - 3)
    return jnp.stack(terms).astype(bf16)


class Plain:
    def __init__(self):
        self.index = lax.axis_index("tensor")
        self.core = self.side = jnp.zeros((), jnp.int32)
        self.home = self.core == 0

    def trade(self, value):
        return value

    def own(self, mine, traded):
        return mine

    def shift(self, blocks):
        return jnp.zeros((1,), jnp.int32)

    def gather(self, value, axis=0):
        return lax.all_gather(value, "tensor", axis=axis, tiled=True)

    def shared(self, value):
        return [self.gather(value)]

    def last_weights(self, out, down, up, bias):
        out, down, up, bias = self.gather(out), self.gather(down), self.gather(up, 1), self.gather(bias)
        model = out.shape[1]
        half, wide = out.shape[0] // 2, down.shape[0] // 2
        packs = [
            jnp.concatenate([
                out[half + number * (half // 2) :][: half // 2],
                down[wide + number * model :][:model],
                up[:, wide + number * model :][:, :model],
                terms_of(bias[wide + number * model :][:model], 16),
            ])
            for number in range(2)
        ]
        return (out[:half], down[:wide], up[:, :wide]), packs, bias[:wide]

    def last_second(self, first):
        return first

    def to_rows(self, attended):
        rows = lax.all_to_all(attended[0], "tensor", 1, 0, tiled=True)
        rows = rows.reshape(2, rows.shape[0] // 2, rows.shape[1])
        return rows, rows

    def to_heads(self, mine, other):
        return [lax.all_to_all(jnp.concatenate([mine, other]), "tensor", 0, 1, tiled=True)]

    def scatter(self, terms):
        return lax.psum_scatter(terms[0](), "tensor", scatter_dimension=0, tiled=True)

    def total(self, value):
        return lax.psum(value, ("dp", "tensor"))

    def early_start(self, keep, send):
        quarters = [keep[0], send[0], keep[1], send[1]]
        model = keep.shape[2]
        quarter = keep.shape[1] - 2 * model
        pieces_of = (
            (jnp.concatenate([v[:quarter] for v in quarters]), 0),
            (jnp.concatenate([v[quarter : quarter + model] for v in quarters]), 0),
            (jnp.concatenate([v[quarter + model :] for v in quarters], axis=1), 1),
        )
        return [
            lax.psum_scatter(v.astype(f32), "tensor", scatter_dimension=d, tiled=True)
            for v, d in pieces_of
        ]


def norm_rows(values, norm_gain, norm_bias):
    centre = values - jnp.mean(values, axis=-1, keepdims=True)
    inverse = lax.rsqrt(jnp.mean(centre * centre, axis=-1, keepdims=True) + epsilon)
    normal = centre * inverse
    return (normal * norm_gain + norm_bias, normal, inverse)


def norm_back(upstream, normal, inverse, norm_gain):
    scaled = upstream * norm_gain
    centred = scaled - jnp.mean(scaled, axis=-1, keepdims=True)
    centred = centred - normal * jnp.mean(scaled * normal, axis=-1, keepdims=True)
    return (
        inverse * centred,
        jnp.sum(upstream * normal, axis=0),
        jnp.sum(upstream, axis=0),
    )


def local(
    inputs, lengths, norm1_gain, norm1_bias, query_key_value_weight, content_bias, position_bias,
    pos_weight, output_weight, out_bias, norm2_gain, norm2_bias, up_projection_weight, up_bias,
    down_projection_weight, down_bias, cotangent,
):
    tensor_count = lax.axis_size("tensor")
    dp_count = lax.axis_size("dp")
    heads, width = content_bias.shape
    paired = tensor_count == 2 and dp_count % 2 == 0 and heads % 2 == 0
    moves = Paired(dp_count) if paired else Plain()
    _, shard_rows, model = inputs.shape
    seq = shard_rows * tensor_count
    flat = heads * width
    hidden = up_bias.shape[0]
    shift = moves.shift(seq // ROWS)
    flags = jnp.stack([moves.core, moves.side]).astype(jnp.int32)
    home = jnp.reshape(moves.home, (1,)).astype(jnp.int32)

    def after(value, *others):
        return lax.optimization_barrier((value, *others))[0]

    row = lax.axis_index("tensor") * shard_rows + jnp.arange(shard_rows, dtype=jnp.int32)
    valid = (row < lengths[0])[:, None]

    got_source = moves.trade(inputs[0])
    vectors = jnp.concatenate([content_bias.reshape(-1), position_bias.reshape(-1)])
    terms = terms_of(vectors, 16).reshape(-1, flat)
    pieces_of = [query_key_value_weight.reshape(3 * model, flat), pos_weight, terms]
    got_pack = moves.trade(jnp.concatenate(pieces_of))
    own_last, first_last, own_bias = moves.last_weights(
        output_weight, down_projection_weight, up_projection_weight, up_bias
    )
    own_cot = jnp.where(valid, cotangent[0], jnp.zeros_like(cotangent[0]))
    got_cot = moves.trade(own_cot)
    sine, cosine, table_t, table = waves(seq, model)

    source = moves.own(inputs[0], got_source).astype(f32)
    normed1, unit1, inverse1 = norm_rows(source, norm1_gain, norm1_bias)
    rows1 = moves.shared(normed1.astype(bf16))
    q, kv = project(home, rows1, query_key_value_weight, got_pack)
    pos_rows = moves.own(pos_weight, got_pack[3 * model : 4 * model]).T
    got_vectors = jnp.sum(got_pack[4 * model :].reshape(16, -1).astype(f32), axis=0)
    biases = moves.own(vectors, got_vectors).reshape(2, flat).T
    calls = min(FORWARD_CALLS, heads)
    each = heads // calls
    kept, mine, theirs = [], [], []
    for call in range(calls):
        low, *keep = attend_forward(
            width, call * each, each, shift, q, kv, biases, pos_rows, sine, cosine, table
        )
        kept.append(keep)
        low, other = moves.to_rows(low)
        mine.append(low)
        theirs.append(other)
        if call == 0 and paired:
            first_last = after(first_last, low)
    first_last, second_last = moves.last_second(first_last)

    y, middle_grad, att_mine, att_other, keep, send, row_sums, up_bias_grad = middle_layer(
        flags, (inputs[0], got_source), (own_cot, got_cot), mine, theirs, own_last, first_last, second_last,
        own_bias[None], jnp.stack([out_bias, norm2_gain, norm2_bias, down_bias]),
    )
    att_grads = moves.to_heads(att_mine, att_other)
    early = moves.early_start(keep, send)

    calls = min(BACKWARD_CALLS, heads)
    step = heads // calls
    grads, weight_grads, bias_grads = None, [], []
    for call in range(calls):
        first = call * step
        held = first // each
        low_out, inverse_sum, weights = kept[held]
        grads, weight_grad, bias_grad = attend_backward(
            width, first, step, held * each, grads, shift, weights, att_grads, low_out, inverse_sum, q, kv,
            biases, pos_rows, sine, cosine, table_t, rows1,
        )
        weight_grads.append(weight_grad.reshape(step * 4 * width, model))
        bias_grads.append(bias_grad)
        if call == 0 and paired:
            early = add(after(early[0], weight_grad), early[1])
            early, grads = lax.optimization_barrier((early, grads))

    qkv_now = moves.own(query_key_value_weight, got_pack[: 3 * model].reshape(3, model, flat))

    def upstream(part):
        return jnp.einsum("nks,nrk->sr", grads[part], qkv_now, preferred_element_type=f32)

    output = moves.own(y, moves.trade(y))
    output = jnp.where(valid, output, jnp.zeros_like(output))
    if paired:
        early = moves.spread(early)
        early, output, *weight_grads = lax.optimization_barrier((early, output, *weight_grads))
        kept_late, got_late = moves.late_start(weight_grads)
    upstream1 = moves.scatter([functools.partial(upstream, part) for part in range(len(rows1))])
    input_part, gain1_grad, bias1_grad = norm_back(upstream1, unit1, inverse1, norm1_gain)
    input_grad = middle_grad + input_part
    got_grad = moves.trade(input_grad.astype(bf16))
    if paired:
        early = moves.collect(early)
        late = add(after(kept_late, gain1_grad), got_late)
        late = moves.collect(moves.spread(late))
        quarter = flat // 2
        early = [v.astype(f32) for v in early]
        out_grad = jnp.concatenate([v[:quarter] for v in early])
        down_grad = jnp.concatenate([v[quarter : quarter + model] for v in early])
        up_grad = jnp.concatenate([v[quarter + model :] for v in early], axis=1)
        late = jnp.concatenate(late)
    else:
        out_grad, down_grad, up_grad = (lax.psum(v.astype(bf16), "dp").astype(f32) for v in early)
        late = lax.psum(jnp.concatenate(weight_grads), "dp")
    late = late.astype(f32).reshape(heads, 4, width, model)
    input_grad = moves.own(input_grad, got_grad.astype(f32))

    bias_grads = jnp.sum(jnp.concatenate(bias_grads), axis=-1)

    def placed(vector):
        count = vector.shape[0]
        room = jnp.zeros((count * tensor_count,), f32)
        return lax.dynamic_update_slice_in_dim(room, vector, moves.index * count, 0)

    parts = [
        gain1_grad, bias1_grad, *row_sums, placed(bias_grads[:, 0].reshape(-1)),
        placed(bias_grads[:, 1].reshape(-1)), up_bias_grad.reshape(-1),
    ]
    small = moves.total(jnp.concatenate(parts).reshape(-1, 128)).reshape(-1)
    side = lax.axis_index("tensor")
    vectors, at = [], 0
    for part in parts[:6]:
        vectors.append(small[at : at + model])
        at += model
    for count in (flat, flat, hidden):
        here = small[at : at + count * tensor_count]
        vectors.append(lax.dynamic_slice_in_dim(here, side * count, count, 0))
        at += count * tensor_count

    return (
        output[None],
        input_grad[None],
        vectors[0],
        vectors[1],
        late[:, :3].transpose(1, 3, 0, 2).reshape(3, model, flat),
        vectors[6].reshape(heads, width),
        vectors[7].reshape(heads, width),
        late[:, 3].transpose(2, 0, 1).reshape(model, flat),
        out_grad,
        vectors[2],
        vectors[3],
        vectors[4],
        up_grad,
        vectors[8],
        down_grad,
        vectors[5],
    )


def solution(mesh):
    rows = P("dp", "tensor", None)
    return jax.shard_map(
        local,
        mesh=mesh,
        in_specs=(
            rows, P("dp"), P(), P(), P(None, None, "tensor"), P("tensor", None),
            P("tensor", None), P(None, "tensor"), P("tensor", None), P(), P(), P(),
            P(None, "tensor"), P("tensor"), P("tensor", None), P(), rows,
        ),
        out_specs=(
            rows, rows, P(), P(), P(None, None, "tensor"), P("tensor", None),
            P("tensor", None), P(None, "tensor"), P("tensor", None), P(), P(), P(),
            P(None, "tensor"), P("tensor"), P("tensor", None), P(),
        ),
        check_vma=False,
    )
```

```python
import functools

import jax
import jax.numpy as jnp
from jax import lax
from jax.experimental import pallas as pl
from jax.experimental.pallas import tpu as pltpu
from jax.sharding import PartitionSpec as P

ROWS = 512
HALF = 256
epsilon = 1e-05
score_scale = 0.125
masked_score = -1e30
NN = (((1,), (0,)), ((), ()))
NT = (((1,), (1,)), ((), ()))
TN = (((0,), (0,)), ((), ()))
TT = (((0,), (1,)), ((), ()))
f32 = jnp.float32
bf16 = jnp.bfloat16
FORWARD_CALLS = 2
VMEM_LIMIT = 60 << 20
ATTEND_VMEM_LIMIT = 56 << 20
BACKWARD_CALLS = 2


def dot(a, b, dims=NN):
    return lax.dot_general(a, b, dims, preferred_element_type=f32)


def resident(shape):
    return pl.BlockSpec(shape, lambda *_: (0,) * len(shape), pipeline_mode=pl.Buffered(1))


def project_kernel(part_count, flag_ref, *refs):
    rows = refs[:part_count]
    own_ref, pos_ref, vec_ref, got_ref, q_ref, kv_ref, pos_out_ref, bias_ref, weight = refs[part_count:]
    part, block = pl.program_id(0), pl.program_id(1)
    model, flat = own_ref.shape[1:]

    def fill(read, vectors):
        for index in range(3):
            weight[index] = read(index).T
        pos_out_ref[...] = read(3).T
        rows = jnp.concatenate([*vectors, jnp.zeros((6, flat), f32)], axis=0)
        bias_ref[...] = rows.T

    def fill_own():
        fill(lambda index: own_ref[index] if index < 3 else pos_ref[...], (vec_ref[0:1, :], vec_ref[1:2, :]))

    def fill_got():
        terms = got_ref[4 * model :, :].astype(f32)
        vectors = [terms[i : i + 1] + terms[i + 2 : i + 3] + terms[i + 4 : i + 5] for i in range(2)]
        fill(lambda index: got_ref[index * model : (index + 1) * model, :], vectors)

    first = (part == 0) & (block == 0)
    pl.when(first & (flag_ref[0] == 1))(fill_own)
    pl.when(first & (flag_ref[0] == 0))(fill_got)

    def run(ref):
        here = ref[pl.ds(pl.multiple_of(block * ROWS, ROWS), ROWS), :]
        result = dot(weight[...].reshape(3 * flat, model), here, NT)
        q_ref[...] = result[:flat]
        kv_ref[0] = result[flat : 2 * flat].astype(bf16)
        kv_ref[1] = result[2 * flat :].astype(bf16)

    for index in range(part_count):
        pl.when(part == index)(functools.partial(run, rows[index]))


def project(home, rows, own, pos, vectors, got):
    count = len(rows)
    n, model = rows[0].shape
    flat = own.shape[2]
    return pl.pallas_call(
        functools.partial(project_kernel, count),
        grid_spec=pltpu.PrefetchScalarGridSpec(
            num_scalar_prefetch=1,
            grid=(count, n // ROWS),
            in_specs=[resident(v.shape) for v in (*rows, own, pos, vectors, got)],
            out_specs=[
                pl.BlockSpec((None, flat, ROWS), lambda p, j, s: (p, 0, j)),
                pl.BlockSpec((2, None, flat, ROWS), lambda p, j, s: (0, p, 0, j)),
                pl.BlockSpec((flat, model), lambda p, j, s: (0, 0)),
                pl.BlockSpec((flat, 8), lambda p, j, s: (0, 0)),
                pl.BlockSpec((3, flat, model), lambda p, j, s: (0, 0, 0)),
            ],
        ),
        out_shape=[
            jax.ShapeDtypeStruct((count, flat, n), f32),
            jax.ShapeDtypeStruct((2, count, flat, n), bf16),
            jax.ShapeDtypeStruct((flat, model), bf16),
            jax.ShapeDtypeStruct((flat, 8), f32),
            jax.ShapeDtypeStruct((3, flat, model), bf16),
        ],
        compiler_params=pltpu.CompilerParams(vmem_limit_bytes=VMEM_LIMIT),
        cost_estimate=pl.CostEstimate(
            flops=6 * count * n * model * flat, bytes_accessed=count * n * (model + 4 * flat) * 2,
            transcendentals=0,
        ),
        name="project",
    )(home, *rows, own, pos, vectors, got)


def pieces(block):
    out = [(key * ROWS, ROWS, 0) for key in range(block)]
    out.append((block * ROWS, HALF, 0))
    out.append((block * ROWS + HALF, HALF, HALF))
    return out


def place(index, shift, blocks, per_part):
    held = lax.rem(index + shift, blocks)
    lanes = pl.ds(pl.multiple_of(lax.rem(held, per_part) * ROWS, ROWS), ROWS)
    return held // per_part, lanes


def forward_kernel(
    blocks, shift_ref, q_ref, kv_ref, bias_ref, w_ref, sin_ref, cos_ref, table_ref,
    low_ref, o_ref, inv_ref, e_ref, keys, values, scores, query,
):
    width = q_ref.shape[0]
    model = table_ref.shape[1]
    half = model // 2
    per_part = kv_ref.shape[3] // ROWS
    block = pl.program_id(1)

    @pl.when((pl.program_id(0) == 0) & (block == 0))
    def _():
        keys[:, :model] = table_ref[...]

    @pl.when(block == 0)
    def _():
        for index in range(blocks):
            part, lanes = place(index, shift_ref[0], blocks, per_part)
            here = pl.ds(index * ROWS, ROWS)
            keys[here, model:] = kv_ref[0, part, :, lanes].T
            values[:, here] = kv_ref[1, part, :, lanes]

    def run(index):
        offset = (q_ref[...] + bias_ref[:, 1:2]).astype(bf16)
        pair = dot(w_ref[...], offset, TN)
        up, low = pair[:half], pair[half:]
        sine, cosine = sin_ref[...], cos_ref[...]
        query[:half] = ((up * sine + low * cosine) * score_scale).astype(bf16)
        query[half:model] = ((low * sine - up * cosine) * score_scale).astype(bf16)
        content = (q_ref[...] + bias_ref[:, :1]).astype(bf16)
        query[model:] = (content.astype(f32) * score_scale).astype(bf16)
        top = jnp.full((8, ROWS), masked_score, f32)
        for start, count, first in pieces(index):
            part = dot(keys[start : start + count, :], query[:, first:])
            if start >= index * ROWS:
                row = lax.broadcasted_iota(jnp.int32, part.shape, 0) + (start - index * ROWS)
                col = lax.broadcasted_iota(jnp.int32, part.shape, 1) + first
                part = jnp.where(col >= row, part, masked_score)
            scores[start : start + count, first:] = part
            best = jnp.max(part.reshape(count // 8, 8, ROWS - first), axis=0)
            if first:
                best = jnp.maximum(top[:, first:], best)
                top = jnp.concatenate([top[:, :first], best], axis=1)
            else:
                top = jnp.maximum(top, best)
        peak = jnp.max(top, axis=0, keepdims=True)
        total = jnp.zeros((8, ROWS), f32)
        out = jnp.zeros((width, ROWS), f32)
        for start, count, first in pieces(index):
            weight = jnp.exp(scores[start : start + count, first:] - peak[:, first:])
            gain = jnp.sum(weight.reshape(count // 8, 8, ROWS - first), axis=0)
            rounded = weight.astype(bf16)
            e_ref[start : start + count, first:] = rounded
            add = dot(values[:, start : start + count], rounded)
            if first:
                total = jnp.concatenate([total[:, :first], total[:, first:] + gain], axis=1)
                out = jnp.concatenate([out[:, :first], out[:, first:] + add], axis=1)
            else:
                total = total + gain
                out = out + add
        inverse = 1.0 / jnp.sum(total, axis=0, keepdims=True)
        out = out * inverse
        o_ref[...] = out
        low_ref[...] = out.astype(bf16)
        inv_ref[...] = inverse

    for index in range(blocks):
        pl.when(block == index)(functools.partial(run, index))


def attend_forward(width, first, heads, shift, q, kv, biases, w, sine, cosine, table):
    parts, _, n = q.shape
    seq, model = table.shape

    blocks, per_part = seq // ROWS, n // ROWS

    def part(offset):
        def index(h, i, s):
            held = lax.rem(i + s[0], blocks)
            return (held // per_part, h + offset, lax.rem(held, per_part))

        return pl.BlockSpec((None, width, ROWS), index)

    column = pl.BlockSpec((width, 8), lambda h, i, s: (h + first, 0))
    wave = pl.BlockSpec((model // 2, ROWS), lambda h, i, s: (0, i))
    return pl.pallas_call(
        functools.partial(forward_kernel, blocks),
        grid_spec=pltpu.PrefetchScalarGridSpec(
            num_scalar_prefetch=1,
            grid=(heads, blocks),
            in_specs=[
                part(first),
                pl.BlockSpec((2, parts, width, n), lambda h, i, s: (0, 0, h + first, 0)),
                column,
                pl.BlockSpec((width, model), lambda h, i, s: (h + first, 0)),
                wave, wave, resident((seq, model)),
            ],
            out_specs=[
                part(0),
                pl.BlockSpec((None, width, ROWS), lambda h, i, s: (h, 0, i)),
                pl.BlockSpec((None, 1, ROWS), lambda h, i, s: (h, 0, i)),
                pl.BlockSpec((None, None, seq, ROWS), lambda h, i, s: (h, i, 0, 0)),
            ],
            scratch_shapes=[
                pltpu.VMEM((seq, model + width), bf16),
                pltpu.VMEM((width, seq), bf16),
                pltpu.VMEM((seq, ROWS), f32),
                pltpu.VMEM((model + width, ROWS), bf16),
            ],
        ),
        out_shape=[
            jax.ShapeDtypeStruct((parts, heads * width, n), bf16),
            jax.ShapeDtypeStruct((heads, width, seq), f32),
            jax.ShapeDtypeStruct((heads, 1, seq), f32),
            jax.ShapeDtypeStruct((heads, blocks, seq, ROWS), bf16),
        ],
        compiler_params=pltpu.CompilerParams(vmem_limit_bytes=ATTEND_VMEM_LIMIT),
        cost_estimate=pl.CostEstimate(
            flops=2 * heads * seq * seq * (model + 2 * width) * 5 // 8,
            bytes_accessed=heads * seq * seq * 2,
            transcendentals=heads * seq * seq // 2,
        ),
        name="attend_forward",
    )(shift, q, kv, biases, w, sine, cosine, table)


def backward_kernel(
    blocks, part_count, chained, shift_ref, e_ref, o_ref, inv_ref, q_ref, kv_ref, bias_ref, w_ref,
    sin_ref, cos_ref, table_ref, *refs,
):
    rows, dos = refs[:part_count], refs[part_count : 2 * part_count]
    refs = refs[2 * part_count + chained :]
    grad_ref, weight_ref, bias_grad_ref = refs[:3]
    keys, values, small, query_acc, k_acc, v_acc, w_acc, b_acc = refs[3:]
    width = q_ref.shape[0]
    model = table_ref.shape[0]
    half = model // 2
    per_part = kv_ref.shape[3] // ROWS
    block = pl.program_id(1)

    @pl.when((pl.program_id(0) == 0) & (block == 0))
    def _():
        keys[:model] = table_ref[...]

    @pl.when(block == 0)
    def _():
        for index in range(blocks):
            part, lanes = place(index, shift_ref[0], blocks, per_part)
            here = pl.ds(index * ROWS, ROWS)
            keys[model:, here] = kv_ref[0, part, :, lanes]
            values[here, :] = kv_ref[1, part, :, lanes].T
        k_acc[...] = jnp.zeros_like(k_acc)
        v_acc[...] = jnp.zeros_like(v_acc)
        w_acc[...] = jnp.zeros_like(w_acc)
        b_acc[...] = jnp.zeros_like(b_acc)

    def run(index):
        held = place(index, shift_ref[0], blocks, per_part)[0]
        out_grad = dos[0][...]
        for part in range(1, part_count):
            out_grad = jnp.where(held == part, dos[part][...], out_grad)
        scaled = (out_grad.astype(f32) * (inv_ref[...] * score_scale)).astype(bf16)
        delta = jnp.sum(scaled.astype(f32) * o_ref[...], axis=0, keepdims=True)
        content_low = (q_ref[...] + bias_ref[:, :1]).astype(bf16)
        for start, count, first in pieces(index):
            weight = e_ref[start : start + count, first:]
            grad = dot(values[start : start + count, :], scaled[:, first:])
            change = (weight.astype(f32) * (grad - delta[:, first:])).astype(bf16)
            add = dot(keys[:, start : start + count], change)
            if start == 0:
                query_acc[...] = add
            else:
                query_acc[:, first:] += add
            v_acc[:, start : start + count] += dot(scaled[:, first:], weight, NT)
            k_acc[:, start : start + count] += dot(content_low[:, first:], change, NT)
        sine, cosine = sin_ref[...], cos_ref[...]
        up, low = query_acc[:half], query_acc[half:model]
        small[:half] = (up * sine - low * cosine).astype(bf16)
        small[half:] = (up * cosine + low * sine).astype(bf16)
        offset = dot(w_ref[...], small[...])
        content = query_acc[model:]
        part, lanes = place(index, shift_ref[0], blocks, per_part)
        grad_ref[part, 0, :, lanes] = (content + offset).astype(bf16)
        offset_low = (q_ref[...] + bias_ref[:, 1:2]).astype(bf16)
        w_acc[...] += dot(offset_low, small[...], NT)
        for lane in range(0, ROWS, 128):
            b_acc[0] += content[:, lane : lane + 128]
            b_acc[1] += offset[:, lane : lane + 128]

    for index in range(blocks):
        pl.when(block == index)(functools.partial(run, index))

    @pl.when(block == blocks - 1)
    def _():
        for index in range(blocks):
            part, lanes = place(index, shift_ref[0], blocks, per_part)
            here = pl.ds(index * ROWS, ROWS)
            grad_ref[part, 1, :, lanes] = k_acc[:, here].astype(bf16)
            grad_ref[part, 2, :, lanes] = (v_acc[:, here] * (1.0 / score_scale)).astype(bf16)
        total = None
        for part in range(part_count):
            stacked = jnp.concatenate([grad_ref[part, index] for index in range(3)], axis=0)
            term = dot(stacked, rows[part][...])
            total = term if total is None else total + term
        weight_ref[: 3 * width] = total.astype(bf16)
        weight_ref[3 * width :] = w_acc[...].astype(bf16)
        for head in range(bias_grad_ref.shape[1] // width):

            @pl.when(pl.program_id(0) == head)
            def _():
                for index in range(2):
                    total = jnp.sum(b_acc[index].T, axis=0, keepdims=True)
                    bias_grad_ref[index : index + 1, head * width : (head + 1) * width] = total


def attend_backward(
    width, first, heads, kept_first, call, before, shift, e, dos, o, inv, q, kv, biases, w, sine, cosine, table,
    rows,
):
    parts, flat, n = q.shape
    model, seq = table.shape

    blocks, per_part = seq // ROWS, n // ROWS
    skip = first - kept_first

    def index_part(h, i, s):
        held = lax.rem(i + s[0], blocks)
        return (held // per_part, h + first, lax.rem(held, per_part))

    def grad_part(number):
        def index(h, i, s):
            held = lax.rem(i + s[0], blocks)
            return (h + first, jnp.where(held // per_part == number, lax.rem(held, per_part), 0))

        return pl.BlockSpec((width, ROWS), index)

    part = pl.BlockSpec((None, width, ROWS), index_part)
    column = pl.BlockSpec((width, 8), lambda h, i, s: (h + first, 0))
    wave = pl.BlockSpec((model // 2, ROWS), lambda h, i, s: (0, i))
    chained = list(before)
    arguments = [
        shift, e, o, inv, q, kv, biases, w, sine, cosine, table, *rows, *dos, *chained
    ]
    return pl.pallas_call(
        functools.partial(backward_kernel, blocks, parts, len(chained)),
        grid_spec=pltpu.PrefetchScalarGridSpec(
            num_scalar_prefetch=1,
            grid=(heads, blocks),
            in_specs=[
                pl.BlockSpec((None, None, seq, ROWS), lambda h, i, s: (h + skip, i, 0, 0)),
                pl.BlockSpec((None, width, ROWS), lambda h, i, s: (h + skip, 0, i)),
                pl.BlockSpec((None, 1, ROWS), lambda h, i, s: (h + skip, 0, i)),
                part,
                pl.BlockSpec((2, parts, width, n), lambda h, i, s: (0, 0, h + first, 0)),
                column,
                pl.BlockSpec((width, model), lambda h, i, s: (h + first, 0)),
                wave, wave, resident((model, seq)),
                *[resident((n, model))] * parts,
                *[grad_part(index) for index in range(parts)],
                *[pl.BlockSpec(memory_space=pl.ANY)] * len(chained),
            ],
            out_specs=[
                pl.BlockSpec((parts, 3, width, n), lambda h, i, s: (0, 0, h + first, 0)),
                pl.BlockSpec(
                    (None, None, 4 * width, model), lambda h, i, s: (jnp.where(s[1] == call, 0, 1), h, 0, 0)
                ),
                pl.BlockSpec((2, heads * width), lambda h, i, s: (0, 0)),
            ],
            scratch_shapes=[
                pltpu.VMEM((model + width, seq), bf16),
                pltpu.VMEM((seq, width), bf16),
                pltpu.VMEM((model, ROWS), bf16),
                pltpu.VMEM((model + width, ROWS), f32),
                pltpu.VMEM((width, seq), f32),
                pltpu.VMEM((width, seq), f32),
                pltpu.VMEM((width, model), f32),
                pltpu.VMEM((2, width, 128), f32),
            ],
        ),
        out_shape=[
            jax.ShapeDtypeStruct((parts, 3, flat, n), bf16),
            jax.ShapeDtypeStruct((2, heads, 4 * width, model), bf16),
            jax.ShapeDtypeStruct((2, heads * width), f32),
        ],
        input_output_aliases={len(arguments) - 2: 0, len(arguments) - 1: 1} if chained else {},
        compiler_params=pltpu.CompilerParams(vmem_limit_bytes=ATTEND_VMEM_LIMIT),
        cost_estimate=pl.CostEstimate(
            flops=2 * heads * seq * seq * (model + 4 * width) * 5 // 8,
            bytes_accessed=heads * seq * seq * 2,
            transcendentals=0,
        ),
        name="attend_backward",
    )(*arguments)


def waves_kernel(near_sin_ref, near_cos_ref, far_sin_ref, far_cos_ref, sin_ref, cos_ref, table_t_ref, table_ref):
    half, seq = sin_ref.shape
    for index in range(seq // 128):
        here = slice(index * 128, (index + 1) * 128)
        far_sin, far_cos = far_sin_ref[:, index : index + 1], far_cos_ref[:, index : index + 1]
        sine = far_sin * near_cos_ref[...] + far_cos * near_sin_ref[...]
        cosine = far_cos * near_cos_ref[...] - far_sin * near_sin_ref[...]
        sin_ref[:, here] = sine
        cos_ref[:, here] = cosine
        table_t_ref[:half, here] = cosine.astype(bf16)
        table_t_ref[half:, here] = sine.astype(bf16)
        table_ref[here, :half] = cosine.T.astype(bf16)
        table_ref[here, half:] = sine.T.astype(bf16)


def waves(seq, model):
    exponent = -jnp.arange(0, model, 2, dtype=jnp.int32).astype(f32) / model
    frequency = jnp.power(10000.0, exponent)[:, None]
    near = frequency * jnp.arange(128, dtype=jnp.int32).astype(f32)[None, :]
    far = frequency * (128 * jnp.arange(seq // 128, dtype=jnp.int32)).astype(f32)[None, :]
    half = model // 2
    return pl.pallas_call(
        waves_kernel,
        out_shape=[
            jax.ShapeDtypeStruct((half, seq), f32), jax.ShapeDtypeStruct((half, seq), f32),
            jax.ShapeDtypeStruct((model, seq), bf16), jax.ShapeDtypeStruct((seq, model), bf16),
        ],
        compiler_params=pltpu.CompilerParams(vmem_limit_bytes=VMEM_LIMIT),
        cost_estimate=pl.CostEstimate(flops=6 * half * seq, bytes_accessed=16 * half * seq, transcendentals=0),
        name="waves",
    )(jnp.sin(near), jnp.cos(near), jnp.sin(far), jnp.cos(far))


def middle_kernel(piece_count, core_ref, side_ref, *refs):
    refs = list(refs)

    def take(count):
        out = refs[:count]
        del refs[:count]
        return out

    ins, cots, mine, theirs = take(2), take(2), take(piece_count), take(piece_count)
    out_hbm, down_hbm, up_hbm, first_hbm, second_hbm, bias_ref = take(6)
    vectors = take(4)
    y_ref, mg_ref, ag_mine_ref, ag_other_ref = take(4)
    keeps, sends = take(2), take(2)
    sum_ref, bias_grad_ref = take(2)
    source, cotangent, att, out_w, down_w, up_w, first_w, second_w, sems = refs
    model = source.shape[1]
    size = out_hbm.shape[0]
    core, side = core_ref[0], side_ref[0]
    rest = first_hbm.shape[0] - size // 2
    copies = []

    def copy(from_ref, to_ref):
        copies.append(pltpu.make_async_copy(from_ref, to_ref, sems.at[len(copies)]))
        return copies[-1]

    def aligned(start, count):
        return pl.ds(pl.multiple_of(start, count), count)

    begin = []
    for pieces_of, half, index in ((mine, core, 0), (theirs, 1 - core, 1)):
        for number, ref in enumerate(pieces_of):
            count = ref.shape[1]
            begin.append(copy(ref.at[index], att.at[aligned(half * size + number * count, count), :]))
    begin.append(copy(out_hbm, out_w.at[aligned(side * size, size), :]))
    quarter = size // 2
    for ref, part in ((first_hbm, core), (second_hbm, 1 - core)):
        to = out_w.at[aligned((1 - side) * size + part * quarter, quarter), :]
        begin.append(copy(ref.at[pl.ds(0, quarter), :], to))
    ups = copy(up_hbm, up_w)
    downs = copy(down_hbm, down_w)
    extra = [
        copy(ref.at[pl.ds(quarter, rest), :], to)
        for ref, to in ((first_hbm, first_w), (second_hbm, second_w))
    ]
    at = len(copies)

    def choose(pair, to, number):
        both = [pltpu.make_async_copy(ref, to, sems.at[number]) for ref in pair]
        pl.when(core == side)(both[0].start)
        pl.when(core != side)(both[1].start)
        return both[0]

    for item in begin:
        item.start()
    source_copy = choose(ins, source, at)
    ups.start()
    cot_copy = choose(cots, cotangent, at + 1)
    downs.start()
    for item in extra:
        item.start()

    out_bias, gain, bias, down_bias = (ref[...] for ref in vectors)
    for item in begin:
        item.wait()
    branch = dot(att[...], out_w[...], TN)
    source_copy.wait()
    middle = source[...].astype(f32) + (branch + out_bias)
    centre = middle - jnp.mean(middle, axis=1, keepdims=True)
    inverse = lax.rsqrt(jnp.mean(centre * centre, axis=1, keepdims=True) + epsilon)
    unit = centre * inverse
    rows2 = (unit * gain + bias).astype(bf16)
    ups.wait()
    cot_copy.wait()
    downs.wait()
    for item in extra:
        item.wait()
    cot = cotangent[...]
    y = e = None
    for number in range(4):
        if number < 2:
            part = core if number == 0 else 1 - core
            here = aligned(part * model, model)
            down, up, up_bias = down_w[here, :], up_w[:, here], bias_ref[:, here]
            half = side
        else:
            part = core if number == 2 else 1 - core
            ref = first_w if number == 2 else second_w
            down, up = ref[:model, :], ref[model : 2 * model, :]
            up_bias = jnp.sum(ref[2 * model : 2 * model + 16, :].astype(f32), axis=0, keepdims=True)
            half = 1 - side
        result = (keeps, sends)[number % 2][number // 2]
        pre = dot(rows2, up) + up_bias
        cdf = 0.5 * (1.0 + lax.erf(pre * 0.7071067811865476))
        active = (pre * cdf).astype(bf16)
        slope = cdf + pre * (jnp.exp(pre * pre * -0.5) * 0.3989422804014327)
        low = (slope * dot(cot, down, NT)).astype(bf16)
        bias_grad_ref[pl.ds(half * 2 + part, 1), :] = jnp.sum(low.astype(f32), axis=0, keepdims=True)
        add_y, add_e = dot(active, down), dot(low, up, NT)
        y = add_y if y is None else y + add_y
        e = add_e if e is None else e + add_e
        result[quarter : quarter + model, :] = dot(active, cot, TN).astype(bf16)
        result[quarter + model :, :] = dot(rows2, low, TN).astype(bf16)
    y_ref[...] = (middle + (y + down_bias)).astype(bf16)
    grad = cot.astype(f32)
    scaled = e * gain
    change = scaled - jnp.mean(scaled, axis=1, keepdims=True)
    change = change - unit * jnp.mean(scaled * unit, axis=1, keepdims=True)
    middle_grad = grad + inverse * change
    mg_ref[...] = middle_grad
    low_grad = middle_grad.astype(bf16)
    sums = (low_grad.astype(f32), e * unit, e, grad)
    for index, term in enumerate(sums):
        sum_ref[index : index + 1, :] = jnp.sum(term, axis=0, keepdims=True)
    ag_mine_ref[...] = dot(out_w[aligned(core * size, size), :], low_grad, NT).astype(bf16)
    ag_other_ref[...] = dot(out_w[aligned((1 - core) * size, size), :], low_grad, NT).astype(bf16)
    for number, half in ((0, side), (1, 1 - side)):
        for ref, part in ((keeps[number], core), (sends[number], 1 - core)):
            rows = att[aligned(half * size + part * quarter, quarter), :]
            ref[:quarter, :] = dot(rows, low_grad).astype(bf16)


def middle_layer(core, side, ins, cots, mine, theirs, own, first, second, bias, vectors):
    n, model = ins[0].shape
    size, hidden = own[0].shape[0], own[1].shape[0]
    quarter = size // 2
    packed = quarter + 2 * model
    extra = first.shape[0] - quarter
    anywhere = pl.BlockSpec(memory_space=pl.ANY)
    vmem = pl.BlockSpec(memory_space=pltpu.VMEM)
    arguments = [core, side, *ins, *cots, *mine, *theirs, *own, first, second, bias, *vectors]
    shapes = [
        jax.ShapeDtypeStruct((n, model), bf16),
        jax.ShapeDtypeStruct((n, model), f32),
        jax.ShapeDtypeStruct((size, n), bf16),
        jax.ShapeDtypeStruct((size, n), bf16),
        *[jax.ShapeDtypeStruct((packed, model), bf16)] * 4,
        jax.ShapeDtypeStruct((4, model), f32),
        jax.ShapeDtypeStruct((4, model), f32),
    ]
    return pl.pallas_call(
        functools.partial(middle_kernel, len(mine)),
        in_specs=[pl.BlockSpec(memory_space=pltpu.SMEM)] * 2 + [anywhere] * (len(arguments) - 7) + [vmem] * 5,
        out_specs=[vmem] * len(shapes),
        out_shape=shapes,
        scratch_shapes=[
            pltpu.VMEM((n, model), bf16), pltpu.VMEM((n, model), bf16),
            pltpu.VMEM((2 * size, n), bf16), pltpu.VMEM((2 * size, model), bf16),
            pltpu.VMEM((hidden, model), bf16), pltpu.VMEM((model, hidden), bf16),
            pltpu.VMEM((extra, model), bf16), pltpu.VMEM((extra, model), bf16),
            pltpu.SemaphoreType.DMA((2 * len(mine) + 9,)),
        ],
        compiler_params=pltpu.CompilerParams(vmem_limit_bytes=VMEM_LIMIT),
        cost_estimate=pl.CostEstimate(
            flops=2 * n * model * (6 * size + 12 * hidden),
            bytes_accessed=n * model * 14 + 8 * packed * model * 2,
            transcendentals=4 * n * hidden,
        ),
        name="middle_layer",
    )(*arguments)


def first_norm_kernel(halves, core_ref, own_ref, got_ref, up_ref, got_up_ref, middle_ref, gain_ref, sum_ref, bias_ref, *refs):
    biases = refs[: -4]
    grad_ref, low_ref, small_ref, acc = refs[-4:]
    step = pl.program_id(0)
    model = own_ref.shape[1]

    @pl.when(step == 0)
    def _():
        acc[...] = jnp.zeros_like(acc)

    source = jnp.where(core_ref[1] == 1, own_ref[...].astype(f32), got_ref[...].astype(f32))
    upstream = up_ref[...] + got_up_ref[...].astype(f32)
    centre = source - jnp.mean(source, axis=1, keepdims=True)
    inverse = lax.rsqrt(jnp.mean(centre * centre, axis=1, keepdims=True) + epsilon)
    unit = centre * inverse
    scaled = upstream * gain_ref[...]
    change = scaled - jnp.mean(scaled, axis=1, keepdims=True)
    change = change - unit * jnp.mean(scaled * unit, axis=1, keepdims=True)
    grad = middle_ref[...] + inverse * change
    grad_ref[...] = grad
    low_ref[...] = grad.astype(bf16)
    acc[0:1, :] += jnp.sum(upstream * unit, axis=0, keepdims=True)
    acc[1:2, :] += jnp.sum(upstream, axis=0, keepdims=True)

    @pl.when(step == pl.num_programs(0) - 1)
    def _():
        small_ref[...] = jnp.zeros_like(small_ref)
        at = 0
        for ref, count in ((acc, 2), (sum_ref, 4)):
            for index in range(count):
                for lane in range(0, model, 128):
                    small_ref[at : at + 1, :] = ref[index : index + 1, lane : lane + 128]
                    at += 1
        width = sum(ref.shape[1] for ref in biases)
        for index in range(2):
            row = at + core_ref[0] * (width // 128)
            for ref in biases:
                for lane in range(0, ref.shape[1], 128):
                    small_ref[pl.ds(row, 1), :] = ref[index : index + 1, lane : lane + 128]
                    row = row + 1
            at += halves * width // 128
        for index in range(4):
            for lane in range(0, model, 128):
                small_ref[at : at + 1, :] = bias_ref[index : index + 1, lane : lane + 128]
                at += 1


def first_norm(halves, flags, own, got, up, got_up, middle, gain, sums, up_bias, biases):
    n, model = own.shape
    count = 4 if n % 32 == 0 and n >= 512 else 1
    rows = pl.BlockSpec((n // count, model), lambda i: (i, 0))
    size = (10 * model + 2 * halves * sum(v.shape[1] for v in biases)) // 128
    arguments = [flags, own, got, up, got_up, middle, gain, sums, up_bias, *biases]
    return pl.pallas_call(
        functools.partial(first_norm_kernel, halves),
        grid=(count,),
        in_specs=[pl.BlockSpec(memory_space=pltpu.SMEM)] + [rows] * 5 + [resident(v.shape) for v in arguments[6:]],
        out_specs=[rows, rows, pl.BlockSpec((size, 128), lambda i: (0, 0))],
        out_shape=[
            jax.ShapeDtypeStruct((n, model), f32), jax.ShapeDtypeStruct((n, model), bf16),
            jax.ShapeDtypeStruct((size, 128), f32),
        ],
        scratch_shapes=[pltpu.VMEM((2, model), f32)],
        compiler_params=pltpu.CompilerParams(vmem_limit_bytes=ATTEND_VMEM_LIMIT),
        cost_estimate=pl.CostEstimate(flops=20 * n * model, bytes_accessed=16 * n * model, transcendentals=0),
        name="first_norm",
    )(*arguments)


def finish_kernel(width, order_ref, first_ref, second_ref, qkv_ref, pos_ref):
    count = first_ref.shape[0] // (4 * width)

    def run(refs):
        for index in range(4):
            rows = []
            for ref in refs:
                for head in range(count):
                    start = (head * 4 + index) * width
                    rows.append(ref[start : start + width, :].astype(f32))
            value = jnp.concatenate(rows, axis=0).T
            if index < 3:
                qkv_ref[index] = value
            else:
                pos_ref[...] = value

    pl.when(order_ref[0] == 0)(lambda: run((first_ref, second_ref)))
    pl.when(order_ref[0] == 1)(lambda: run((second_ref, first_ref)))


def finish(order, first, second, flat, width):
    model = first.shape[1]
    return pl.pallas_call(
        functools.partial(finish_kernel, width),
        in_specs=[pl.BlockSpec(memory_space=pltpu.SMEM)] + [pl.BlockSpec(memory_space=pltpu.VMEM)] * 2,
        out_shape=[
            jax.ShapeDtypeStruct((3, model, flat), f32), jax.ShapeDtypeStruct((model, flat), f32),
        ],
        compiler_params=pltpu.CompilerParams(vmem_limit_bytes=VMEM_LIMIT),
        name="finish",
    )(order, first, second)


def unpack_kernel(order_ref, first_ref, second_ref, out_ref, down_ref, up_ref):
    model = up_ref.shape[0]
    quarter = out_ref.shape[0] // 2

    def run(refs):
        for index, ref in enumerate(refs):
            here = slice(index * model, (index + 1) * model)
            out_ref[index * quarter : (index + 1) * quarter, :] = ref[:quarter, :].astype(f32)
            down_ref[here, :] = ref[quarter : quarter + model, :].astype(f32)
            up_ref[:, here] = ref[quarter + model :, :].astype(f32)

    pl.when(order_ref[0] == 0)(lambda: run((first_ref, second_ref)))
    pl.when(order_ref[0] == 1)(lambda: run((second_ref, first_ref)))


def unpack(order, first, second, flat, hidden):
    model = first.shape[1]
    return pl.pallas_call(
        unpack_kernel,
        in_specs=[pl.BlockSpec(memory_space=pltpu.SMEM)] + [pl.BlockSpec(memory_space=pltpu.VMEM)] * 2,
        out_shape=[
            jax.ShapeDtypeStruct((flat, model), f32), jax.ShapeDtypeStruct((hidden, model), f32),
            jax.ShapeDtypeStruct((model, hidden), f32),
        ],
        compiler_params=pltpu.CompilerParams(vmem_limit_bytes=VMEM_LIMIT),
        name="unpack",
    )(order, first, second)


class Paired:
    def __init__(self, dp_count):
        self.dp_count = dp_count
        self.core = lax.rem(lax.axis_index("dp"), 2)
        self.side = lax.axis_index("tensor")
        self.home = self.core == self.side
        self.index = self.core

    def trade(self, value):
        pairs = []
        for place in range(2 * self.dp_count):
            group, core, side = place // 4, place // 2 % 2, place % 2
            if core != side:
                pairs.append((place, group * 4 + side * 2 + core))
        return lax.ppermute(value, ("dp", "tensor"), pairs)

    def cross(self, value, flip):
        return lax.ppermute(value, "dp", [(i, i ^ flip) for i in range(self.dp_count)])

    def partner(self, value):
        return self.cross(value, 1)

    def across(self, value):
        return lax.ppermute(value, "tensor", [(0, 1), (1, 0)])

    def own(self, mine, traded):
        return jnp.where(self.home, mine, traded)

    def shift(self, blocks):
        return jnp.reshape(self.core * (blocks // 2), (1,)).astype(jnp.int32)

    def shared(self, value):
        return [value, self.partner(value)]

    def last_weights(self, out, down, up, bias):
        quarter, model = out.shape[0] // 2, out.shape[1]
        pack = jnp.concatenate([
            lax.dynamic_slice_in_dim(out, self.core * quarter, quarter, 0),
            lax.dynamic_slice_in_dim(down, self.core * model, model, 0),
            lax.dynamic_slice_in_dim(up, self.core * model, model, 1),
            lax.optimization_barrier(terms_of(lax.dynamic_slice_in_dim(bias, self.core * model, model, 0), 16)),
        ])
        return (out, down, up), pack, bias

    def last_first(self, pack):
        return self.across(pack)

    def last_second(self, first):
        return first, self.partner(first)

    def to_rows(self, attended):
        return attended, self.partner(attended)

    def to_heads(self, mine, other):
        return [mine, self.partner(other)]

    def total(self, value):
        flip = 1
        while flip < self.dp_count:
            value = value + self.cross(value, flip)
            flip *= 2
        return value + self.across(value)

    def flips(self):
        flips, flip = [], 2
        while flip < self.dp_count:
            flips.append(flip)
            flip *= 2
        return flips

    def groups(self):
        order = [0]
        for flip in self.flips()[::-1]:
            order = order + [place + flip for place in order]
        return [[place + core for place in order] for core in range(2)]

    def swap(self, value):
        return lax.all_to_all(value, "dp", 0, 0, axis_index_groups=self.groups(), tiled=True)


    def early_start(self, keep, send):
        gone = self.across(add(keep[1], self.partner(send[1])))
        return keep[0], self.partner(send[0]), gone

    def late_start(self, grads):
        keep, got = grads[0], self.partner(grads)[1]
        return jnp.where(self.home, keep, got), jnp.where(self.home, got, keep)

    def spread(self, value):
        count = self.dp_count // 2
        return self.swap(value).reshape(count, value.shape[0] // count, -1)

    def collect(self, value):
        copies = jnp.broadcast_to(value[None], (self.dp_count // 2, *value.shape))
        return self.swap(copies.reshape(-1, value.shape[1]))

    def gather(self, value):
        for flip in self.flips()[::-1]:
            first = lax.rem(lax.axis_index("dp") // flip, 2) == 0
            other = self.cross(value, flip)
            value = jnp.concatenate([jnp.where(first, value, other), jnp.where(first, other, value)])
        return value


def total_of(terms):
    return jnp.sum(terms.astype(f32), axis=0).astype(bf16)


def add(a, b):
    return (a.astype(f32) + b.astype(f32)).astype(bf16)


def terms_of(vector, rows):
    terms, rest = [], vector
    for _ in range(3):
        terms.append(lax.reduce_precision(rest, 8, 7))
        rest = rest - terms[-1]
    terms += [jnp.zeros_like(vector)] * (rows - 3)
    return jnp.stack(terms).astype(bf16)


class Plain:
    def __init__(self):
        self.index = lax.axis_index("tensor")
        self.core = self.side = jnp.zeros((), jnp.int32)
        self.home = self.core == 0

    def trade(self, value):
        return value

    def own(self, mine, traded):
        return mine

    def shift(self, blocks):
        return jnp.zeros((1,), jnp.int32)

    def gather(self, value, axis=0):
        return lax.all_gather(value, "tensor", axis=axis, tiled=True)

    def shared(self, value):
        return [self.gather(value)]

    def last_weights(self, out, down, up, bias):
        out, down, up, bias = self.gather(out), self.gather(down), self.gather(up, 1), self.gather(bias)
        model = out.shape[1]
        half, wide = out.shape[0] // 2, down.shape[0] // 2
        packs = [
            jnp.concatenate([
                out[half + number * (half // 2) :][: half // 2],
                down[wide + number * model :][:model],
                up[:, wide + number * model :][:, :model],
                terms_of(bias[wide + number * model :][:model], 16),
            ])
            for number in range(2)
        ]
        return (out[:half], down[:wide], up[:, :wide]), packs, bias[:wide]

    def last_first(self, packs):
        return packs

    def last_second(self, first):
        return first

    def to_rows(self, attended):
        rows = lax.all_to_all(attended[0], "tensor", 1, 0, tiled=True)
        rows = rows.reshape(2, rows.shape[0] // 2, rows.shape[1])
        return rows, rows

    def to_heads(self, mine, other):
        return [lax.all_to_all(jnp.concatenate([mine, other]), "tensor", 0, 1, tiled=True)]

    def scatter(self, mine):
        return lax.psum_scatter(mine, "tensor", scatter_dimension=0, tiled=True)

    def total(self, value):
        return lax.psum(value, ("dp", "tensor"))

    def early_start(self, keep, send):
        quarters = [keep[0], send[0], keep[1], send[1]]
        model = keep[0].shape[1]
        quarter = keep[0].shape[0] - 2 * model
        pieces_of = (
            (jnp.concatenate([v[:quarter] for v in quarters]), 0),
            (jnp.concatenate([v[quarter : quarter + model] for v in quarters]), 0),
            (jnp.concatenate([v[quarter + model :] for v in quarters], axis=1), 1),
        )
        return [
            lax.psum_scatter(v.astype(f32), "tensor", scatter_dimension=d, tiled=True)
            for v, d in pieces_of
        ]


def norm_rows(values, norm_gain, norm_bias):
    centre = values - jnp.mean(values, axis=-1, keepdims=True)
    inverse = lax.rsqrt(jnp.mean(centre * centre, axis=-1, keepdims=True) + epsilon)
    normal = centre * inverse
    return normal * norm_gain + norm_bias


def local(
    inputs, lengths, norm1_gain, norm1_bias, query_key_value_weight, content_bias, position_bias,
    pos_weight, output_weight, out_bias, norm2_gain, norm2_bias, up_projection_weight, up_bias,
    down_projection_weight, down_bias, cotangent,
):
    tensor_count = lax.axis_size("tensor")
    dp_count = lax.axis_size("dp")
    heads, width = content_bias.shape
    paired = tensor_count == 2 and dp_count >= 2 and dp_count & (dp_count - 1) == 0 and heads % 2 == 0
    moves = Paired(dp_count) if paired else Plain()
    _, shard_rows, model = inputs.shape
    seq = shard_rows * tensor_count
    flat = heads * width
    hidden = up_bias.shape[0]
    shift = moves.shift(seq // ROWS)
    core, side = (jnp.reshape(v, (1,)).astype(jnp.int32) for v in (moves.core, moves.side))
    shift = jnp.concatenate([shift, core])
    home = jnp.reshape(moves.home, (1,)).astype(jnp.int32)

    together = lax.optimization_barrier

    row = lax.axis_index("tensor") * shard_rows + jnp.arange(shard_rows, dtype=jnp.int32)
    valid = (row < lengths[0])[:, None]

    got_source = moves.trade(inputs[0])
    vectors = jnp.concatenate([content_bias.reshape(-1), position_bias.reshape(-1)])
    terms = terms_of(vectors, 16).reshape(-1, flat)
    pieces_of = [query_key_value_weight.reshape(3 * model, flat), pos_weight, terms]
    got_pack = moves.trade(jnp.concatenate(pieces_of))
    own_last, last_pack, own_bias = moves.last_weights(
        output_weight, down_projection_weight, up_projection_weight, up_bias
    )
    own_cot = jnp.where(valid, cotangent[0], jnp.zeros_like(cotangent[0]))
    got_cot = moves.trade(own_cot)
    sine, cosine, table_t, table = waves(seq, model)
    got_pack, sine, cosine, table_t, table = together((got_pack, sine, cosine, table_t, table))

    source = moves.own(inputs[0], got_source).astype(f32)
    normed1 = norm_rows(source, norm1_gain, norm1_bias)
    rows1 = moves.shared(normed1.astype(bf16))
    q, kv, pos_rows, biases, qkv = project(
        home, rows1, query_key_value_weight, pos_weight, vectors.reshape(2, flat), got_pack
    )
    if paired:
        last_pack, pos_rows = together((last_pack, pos_rows))
    first_last = moves.last_first(last_pack)
    calls = min(FORWARD_CALLS, heads)
    each = heads // calls
    kept, mine, theirs = [], [], []
    for call in range(calls):
        low, *keep = attend_forward(
            width, call * each, each, shift, q, kv, biases, pos_rows, sine, cosine, table
        )
        kept.append(keep)
        low, other = moves.to_rows(low)
        mine.append(low)
        theirs.append(other)
        if call == 0 and paired:
            first_last, mine[0] = together((first_last, mine[0]))
    first_last, second_last = moves.last_second(first_last)

    y, middle_grad, att_mine, att_other, *packs, row_sums, up_bias_grad = middle_layer(
        core, side, (inputs[0], got_source), (own_cot, got_cot), mine, theirs, own_last, first_last, second_last,
        own_bias[None], [v[None] for v in (out_bias, norm2_gain, norm2_bias, down_bias)],
    )
    att_grads = moves.to_heads(att_mine, att_other)
    early = moves.early_start(packs[:2], packs[2:])

    calls = min(BACKWARD_CALLS, heads)
    step = heads // calls
    before, bias_grads = [], []
    for call in range(calls):
        first = call * step
        held = first // each
        low_out, inverse_sum, weights = kept[held]
        grads, weight_grads, bias_grad = attend_backward(
            width, first, step, held * each, call, before, shift, weights, att_grads, low_out, inverse_sum, q, kv,
            biases, pos_rows, sine, cosine, table_t, rows1,
        )
        bias_grads.append(bias_grad)
        if paired and call == 0:
            early = add(add(early[0], early[1]), early[2])
            early, weight_grads = together((early, weight_grads))
            early = moves.spread(early)
        before = [grads, weight_grads]

    def upstream(part):
        return jnp.einsum("nks,nkr->sr", grads[part], qkv, preferred_element_type=f32)

    got_y = moves.trade(y)
    if paired:
        early, weight_grads, got_y, grads = together((early, weight_grads, got_y, grads))
        kept_late, gone_late = moves.late_start(weight_grads.reshape(2, -1, model))
        gone_late, early, grads, *bias_grads = together((gone_late, early, grads, *bias_grads))
        got_late = moves.across(gone_late)
        early = total_of(early)
        got_up = moves.partner(upstream(1).astype(bf16))
        up = upstream(0)
        got_late, up = together((got_late, up))
        late = moves.spread(add(kept_late, got_late))
    else:
        up = lax.psum_scatter(upstream(0), "tensor", scatter_dimension=0, tiled=True)
        got_up = jnp.zeros(up.shape, bf16)
        room = jnp.zeros((2, flat * tensor_count), f32)
        bias_grads = jnp.concatenate(bias_grads, axis=1)
        bias_grads = [lax.dynamic_update_slice_in_dim(room, bias_grads, moves.index * flat, 1)]
    input_grad, input_low, small = first_norm(
        2 if paired else 1, jnp.concatenate([core, home]).astype(jnp.int32), inputs[0], got_source, up, got_up,
        middle_grad, norm1_gain[None], row_sums, up_bias_grad, bias_grads,
    )
    if paired:
        early = moves.gather(early)
        late, input_low, small, got_y = together((late, input_low, small, got_y))
        got_grad = moves.trade(input_low)
        late = total_of(late)
        input_grad = moves.own(input_grad, got_grad.astype(f32))
    output = moves.own(y, got_y)
    output = jnp.where(valid, output, jnp.zeros_like(output))

    small = moves.total(small).reshape(-1)
    vectors, at = [], 0
    for _ in range(6):
        vectors.append(small[at : at + model])
        at += model
    for count in (flat, flat, hidden):
        here = small[at : at + count * tensor_count]
        vectors.append(lax.dynamic_slice_in_dim(here, lax.axis_index("tensor") * count, count, 0))
        at += count * tensor_count

    if paired:
        late = moves.collect(late)
        out_grad, down_grad, up_grad = unpack(core, early, moves.partner(early), flat, hidden)
        late, out_grad, down_grad, up_grad, input_grad, output, *vectors = together(
            (late, out_grad, down_grad, up_grad, input_grad, output, *vectors)
        )
        qkv_grad, pos_grad = finish(core, late, moves.partner(late), flat, width)
    else:
        out_grad, down_grad, up_grad = (lax.psum(v.astype(bf16), "dp").astype(f32) for v in early)
        late = lax.psum(weight_grads[:calls], "dp").astype(f32).reshape(-1, 4, width, model)[:heads]
        qkv_grad = late[:, :3].transpose(1, 3, 0, 2).reshape(3, model, flat)
        pos_grad = late[:, 3].transpose(2, 0, 1).reshape(model, flat)

    return (
        output[None],
        input_grad[None],
        vectors[0],
        vectors[1],
        qkv_grad,
        vectors[6].reshape(heads, width),
        vectors[7].reshape(heads, width),
        pos_grad,
        out_grad,
        vectors[2],
        vectors[3],
        vectors[4],
        up_grad,
        vectors[8],
        down_grad,
        vectors[5],
    )


def solution(mesh):
    rows = P("dp", "tensor", None)
    return jax.shard_map(
        local,
        mesh=mesh,
        in_specs=(
            rows, P("dp"), P(), P(), P(None, None, "tensor"), P("tensor", None),
            P("tensor", None), P(None, "tensor"), P("tensor", None), P(), P(), P(),
            P(None, "tensor"), P("tensor"), P("tensor", None), P(), rows,
        ),
        out_specs=(
            rows, rows, P(), P(), P(None, None, "tensor"), P("tensor", None),
            P("tensor", None), P(None, "tensor"), P("tensor", None), P(), P(), P(),
            P(None, "tensor"), P("tensor"), P("tensor", None), P(),
        ),
        check_vma=False,
    )
```

```python
import functools

import jax
import jax.numpy as jnp
from jax import lax
from jax.experimental import pallas as pl
from jax.experimental.pallas import tpu as pltpu
from jax.sharding import PartitionSpec as P

ROWS = 512
HALF = 256
epsilon = 1e-05
score_scale = 0.125
masked_score = -1e30
NN = (((1,), (0,)), ((), ()))
NT = (((1,), (1,)), ((), ()))
TN = (((0,), (0,)), ((), ()))
TT = (((0,), (1,)), ((), ()))
f32 = jnp.float32
bf16 = jnp.bfloat16
FORWARD_CALLS = 2
VMEM_LIMIT = 60 << 20
ATTEND_VMEM_LIMIT = 56 << 20
BACKWARD_CALLS = 2


def dot(a, b, dims=NN):
    return lax.dot_general(a, b, dims, preferred_element_type=f32)


def resident(shape):
    return pl.BlockSpec(shape, lambda *_: (0,) * len(shape), pipeline_mode=pl.Buffered(1))


def project_kernel(part_count, flag_ref, *refs):
    rows = refs[:part_count]
    own_ref, pos_ref, vec_ref, got_ref, q_ref, kv_ref, pos_out_ref, bias_ref, weight = refs[part_count:]
    part, block = pl.program_id(0), pl.program_id(1)
    model, flat = own_ref.shape[1:]

    def fill(read, vectors):
        for index in range(3):
            weight[index] = read(index).T
        pos_out_ref[...] = read(3).T
        rows = jnp.concatenate([*vectors, jnp.zeros((6, flat), f32)], axis=0)
        bias_ref[...] = rows.T

    def fill_own():
        fill(lambda index: own_ref[index] if index < 3 else pos_ref[...], (vec_ref[0:1, :], vec_ref[1:2, :]))

    def fill_got():
        terms = got_ref[4 * model :, :].astype(f32)
        vectors = [terms[i : i + 1] + terms[i + 2 : i + 3] + terms[i + 4 : i + 5] for i in range(2)]
        fill(lambda index: got_ref[index * model : (index + 1) * model, :], vectors)

    first = (part == 0) & (block == 0)
    pl.when(first & (flag_ref[0] == 1))(fill_own)
    pl.when(first & (flag_ref[0] == 0))(fill_got)

    def run(ref):
        here = ref[pl.ds(pl.multiple_of(block * ROWS, ROWS), ROWS), :]
        result = dot(weight[...].reshape(3 * flat, model), here, NT)
        q_ref[...] = result[:flat]
        kv_ref[0] = result[flat : 2 * flat].astype(bf16)
        kv_ref[1] = result[2 * flat :].astype(bf16)

    for index in range(part_count):
        pl.when(part == index)(functools.partial(run, rows[index]))


def project(home, rows, own, pos, vectors, got):
    count = len(rows)
    n, model = rows[0].shape
    flat = own.shape[2]
    return pl.pallas_call(
        functools.partial(project_kernel, count),
        grid_spec=pltpu.PrefetchScalarGridSpec(
            num_scalar_prefetch=1,
            grid=(count, n // ROWS),
            in_specs=[resident(v.shape) for v in (*rows, own, pos, vectors, got)],
            out_specs=[
                pl.BlockSpec((None, flat, ROWS), lambda p, j, s: (p, 0, j)),
                pl.BlockSpec((2, None, flat, ROWS), lambda p, j, s: (0, p, 0, j)),
                pl.BlockSpec((flat, model), lambda p, j, s: (0, 0)),
                pl.BlockSpec((flat, 8), lambda p, j, s: (0, 0)),
                pl.BlockSpec((3, flat, model), lambda p, j, s: (0, 0, 0)),
            ],
        ),
        out_shape=[
            jax.ShapeDtypeStruct((count, flat, n), f32),
            jax.ShapeDtypeStruct((2, count, flat, n), bf16),
            jax.ShapeDtypeStruct((flat, model), bf16),
            jax.ShapeDtypeStruct((flat, 8), f32),
            jax.ShapeDtypeStruct((3, flat, model), bf16),
        ],
        compiler_params=pltpu.CompilerParams(vmem_limit_bytes=VMEM_LIMIT),
        cost_estimate=pl.CostEstimate(
            flops=6 * count * n * model * flat, bytes_accessed=count * n * (model + 4 * flat) * 2,
            transcendentals=0,
        ),
        name="project",
    )(home, *rows, own, pos, vectors, got)


def pieces(block):
    out = [(key * ROWS, ROWS, 0) for key in range(block)]
    out.append((block * ROWS, HALF, 0))
    out.append((block * ROWS + HALF, HALF, HALF))
    return out


def place(index, shift, blocks, per_part):
    held = lax.rem(index + shift, blocks)
    lanes = pl.ds(pl.multiple_of(lax.rem(held, per_part) * ROWS, ROWS), ROWS)
    return held // per_part, lanes


def forward_kernel(
    blocks, width, shift_ref, q_ref, kv_ref, bias_ref, w_ref, sin_ref, cos_ref, table_hbm,
    low_ref, o_ref, inv_ref, e_ref, keys, values, query, sems, *scores,
):
    group = len(scores)
    model = w_ref.shape[1]
    half = model // 2
    per_part = kv_ref.shape[3] // ROWS
    block = pl.program_id(1)

    def fetch(index):
        rows = pl.ds(index * ROWS, ROWS)
        return pltpu.make_async_copy(table_hbm.at[rows, :], keys.at[rows, pl.ds(0, model)], sems.at[index])

    @pl.when((pl.program_id(0) == 0) & (block == 0))
    def _():
        for index in range(blocks):
            fetch(index).start()
        query[...] = jnp.zeros_like(query)

    @pl.when(block == 0)
    def _():
        for index in range(blocks):
            part, lanes = place(index, shift_ref[0], blocks, per_part)
            here = pl.ds(index * ROWS, ROWS)
            keys[here, model:] = kv_ref[0, part, :, lanes].T
            values[:, here] = kv_ref[1, part, :, lanes]

    def run(index):
        pl.when(pl.program_id(0) == 0)(lambda: fetch(index).wait())
        sine, cosine = sin_ref[...], cos_ref[...]
        for head in range(group):
            rows = slice(head * width, (head + 1) * width)
            offset = (q_ref[rows, :] + bias_ref[rows, 1:2]).astype(bf16)
            pair = dot(w_ref[rows, :], offset, TN)
            up, low = pair[:half], pair[half:]
            query[head, :half] = ((up * sine + low * cosine) * score_scale).astype(bf16)
            query[head, half:model] = ((low * sine - up * cosine) * score_scale).astype(bf16)
            content = (q_ref[rows, :] + bias_ref[rows, :1]).astype(bf16)
            at = model + head * width
            query[head, at : at + width] = (content.astype(f32) * score_scale).astype(bf16)

        def score(head):
            top = jnp.full((8, ROWS), masked_score, f32)
            for start, count, first in pieces(index):
                part = dot(keys[start : start + count, :], query[head, :, first:])
                if start >= index * ROWS:
                    row = lax.broadcasted_iota(jnp.int32, part.shape, 0) + (start - index * ROWS)
                    col = lax.broadcasted_iota(jnp.int32, part.shape, 1) + first
                    part = jnp.where(col >= row, part, masked_score)
                scores[head][start : start + count, first:] = part
                best = jnp.max(part.reshape(count // 8, 8, ROWS - first), axis=0)
                if first:
                    best = jnp.maximum(top[:, first:], best)
                    top = jnp.concatenate([top[:, :first], best], axis=1)
                else:
                    top = jnp.maximum(top, best)
            return jnp.max(top, axis=0, keepdims=True)

        def attend(head, peak):
            rows = slice(head * width, (head + 1) * width)
            total = jnp.zeros((8, ROWS), f32)
            out = jnp.zeros((width, ROWS), f32)
            for start, count, first in pieces(index):
                weight = jnp.exp(scores[head][start : start + count, first:] - peak[:, first:])
                gain = jnp.sum(weight.reshape(count // 8, 8, ROWS - first), axis=0)
                rounded = weight.astype(bf16)
                e_ref[head, start : start + count, first:] = rounded
                add = dot(values[rows, start : start + count], rounded)
                if first:
                    total = jnp.concatenate([total[:, :first], total[:, first:] + gain], axis=1)
                    out = jnp.concatenate([out[:, :first], out[:, first:] + add], axis=1)
                else:
                    total = total + gain
                    out = out + add
            inverse = 1.0 / jnp.sum(total, axis=0, keepdims=True)
            out = out * inverse
            o_ref[head] = out
            low_ref[rows, :] = out.astype(bf16)
            inv_ref[head] = inverse

        peak = score(0)
        for head in range(group):
            following = score(head + 1) if head + 1 < group else None
            attend(head, peak)
            peak = following

    for index in range(blocks):
        pl.when(block == index)(functools.partial(run, index))


def attend_forward(width, first, heads, shift, q, kv, biases, w, sine, cosine, table):
    parts, _, n = q.shape
    seq, model = table.shape
    blocks, per_part = seq // ROWS, n // ROWS
    group = 2 if heads % 2 == 0 else 1
    wide, skip = group * width, first // group

    def part(offset):
        def index(h, i, s):
            held = lax.rem(i + s[0], blocks)
            return (held // per_part, h + offset, lax.rem(held, per_part))

        return pl.BlockSpec((None, wide, ROWS), index)

    wave = pl.BlockSpec((model // 2, ROWS), lambda h, i, s: (0, i))
    return pl.pallas_call(
        functools.partial(forward_kernel, blocks, width),
        grid_spec=pltpu.PrefetchScalarGridSpec(
            num_scalar_prefetch=1,
            grid=(heads // group, blocks),
            in_specs=[
                part(skip),
                pl.BlockSpec((2, parts, wide, n), lambda h, i, s: (0, 0, h + skip, 0)),
                pl.BlockSpec((wide, 8), lambda h, i, s: (h + skip, 0)),
                pl.BlockSpec((wide, model), lambda h, i, s: (h + skip, 0)),
                wave, wave, pl.BlockSpec(memory_space=pl.ANY),
            ],
            out_specs=[
                part(0),
                pl.BlockSpec((group, width, ROWS), lambda h, i, s: (h, 0, i)),
                pl.BlockSpec((group, 1, ROWS), lambda h, i, s: (h, 0, i)),
                pl.BlockSpec((group, None, seq, ROWS), lambda h, i, s: (h, i, 0, 0)),
            ],
            scratch_shapes=[
                pltpu.VMEM((seq, model + wide), bf16),
                pltpu.VMEM((wide, seq), bf16),
                pltpu.VMEM((group, model + wide, ROWS), bf16),
                pltpu.SemaphoreType.DMA((blocks,)),
                *[pltpu.VMEM((seq, ROWS), f32)] * group,
            ],
        ),
        out_shape=[
            jax.ShapeDtypeStruct((parts, heads * width, n), bf16),
            jax.ShapeDtypeStruct((heads, width, seq), f32),
            jax.ShapeDtypeStruct((heads, 1, seq), f32),
            jax.ShapeDtypeStruct((heads, blocks, seq, ROWS), bf16),
        ],
        compiler_params=pltpu.CompilerParams(vmem_limit_bytes=ATTEND_VMEM_LIMIT),
        cost_estimate=pl.CostEstimate(
            flops=2 * heads * seq * seq * (model + 2 * width) * 5 // 8,
            bytes_accessed=heads * seq * seq * 2,
            transcendentals=heads * seq * seq // 2,
        ),
        name="attend_forward",
    )(shift, q, kv, biases, w, sine, cosine, table)


def backward_kernel(
    blocks, width, part_count, chained, shift_ref, e_ref, o_ref, inv_ref, q_ref, kv_ref, bias_ref, w_ref,
    sin_ref, cos_ref, table_hbm, *refs,
):
    rows_hbm, dos = refs[:part_count], refs[part_count : 2 * part_count]
    refs = refs[2 * part_count + chained :]
    grad_ref, weight_ref, bias_grad_ref = refs[:3]
    values, small, w_acc, b_acc, rows, sems = refs[3:9]
    group = e_ref.shape[0]
    keys, query_acc, k_acc, v_acc = (refs[9 + i * group : 9 + (i + 1) * group] for i in range(4))
    model = w_ref.shape[1]
    half = model // 2
    per_part = kv_ref.shape[3] // ROWS
    block = pl.program_id(1)
    first_step = pl.program_id(0) == 0

    def fetch(head, index):
        lanes = pl.ds(index * ROWS, ROWS)
        to = keys[head].at[pl.ds(0, model), lanes]
        return pltpu.make_async_copy(table_hbm.at[:, lanes], to, sems.at[head * blocks + index])

    def fetch_rows(part):
        return pltpu.make_async_copy(rows_hbm[part], rows.at[part], sems.at[group * blocks + part])

    @pl.when(first_step & (block == 0))
    def _():
        for index in range(blocks):
            for head in range(group):
                fetch(head, index).start()
        for part in range(part_count):
            fetch_rows(part).start()

    @pl.when(block == 0)
    def _():
        for index in range(blocks):
            part, lanes = place(index, shift_ref[0], blocks, per_part)
            here = pl.ds(index * ROWS, ROWS)
            for head in range(group):
                own = slice(head * width, (head + 1) * width)
                keys[head][model:, here] = kv_ref[0, part, own, lanes]
            values[here, :] = kv_ref[1, part, :, lanes].T
        for ref in (*k_acc, *v_acc, w_acc, b_acc):
            ref[...] = jnp.zeros_like(ref)

    def run(index):
        @pl.when(first_step)
        def _():
            for head in range(group):
                fetch(head, index).wait()

        held = place(index, shift_ref[0], blocks, per_part)[0]
        sides = []
        for head in range(group):
            own = slice(head * width, (head + 1) * width)
            out_grad = dos[0][own, :]
            for part in range(1, part_count):
                out_grad = jnp.where(held == part, dos[part][own, :], out_grad)
            scaled = (out_grad.astype(f32) * (inv_ref[head] * score_scale)).astype(bf16)
            delta = jnp.sum(scaled.astype(f32) * o_ref[head], axis=0, keepdims=True)
            content_low = (q_ref[own, :] + bias_ref[own, :1]).astype(bf16)
            sides.append((own, scaled, delta, content_low))
        for start, count, first in pieces(index):
            here = slice(start, start + count)
            for head in range(group):
                own, scaled, delta, content_low = sides[head]
                weight = e_ref[head, here, first:]
                grad = dot(values[here, own], scaled[:, first:])
                change = (weight.astype(f32) * (grad - delta[:, first:])).astype(bf16)
                term = dot(keys[head][:, here], change)
                if start == 0:
                    query_acc[head][...] = term
                else:
                    query_acc[head][:, first:] += term
                v_acc[head][:, here] += dot(scaled[:, first:], weight, NT)
                k_acc[head][:, here] += dot(content_low[:, first:], change, NT)
        sine, cosine = sin_ref[...], cos_ref[...]
        part, lanes = place(index, shift_ref[0], blocks, per_part)
        for head in range(group):
            own = sides[head][0]
            up, low = query_acc[head][:half], query_acc[head][half:model]
            small[head, :half] = (up * sine - low * cosine).astype(bf16)
            small[head, half:] = (up * cosine + low * sine).astype(bf16)
            offset = dot(w_ref[own, :], small[head])
            content = query_acc[head][model:]
            grad_ref[part, 0, own, lanes] = (content + offset).astype(bf16)
            offset_low = (q_ref[own, :] + bias_ref[own, 1:2]).astype(bf16)
            w_acc[own, :] += dot(offset_low, small[head], NT)
            for lane in range(0, ROWS, 128):
                b_acc[0, own] += content[:, lane : lane + 128]
                b_acc[1, own] += offset[:, lane : lane + 128]

    for index in range(blocks):
        pl.when(block == index)(functools.partial(run, index))

    @pl.when(block == blocks - 1)
    def _():
        for index in range(blocks):
            part, lanes = place(index, shift_ref[0], blocks, per_part)
            here = pl.ds(index * ROWS, ROWS)
            for head in range(group):
                own = slice(head * width, (head + 1) * width)
                grad_ref[part, 1, own, lanes] = k_acc[head][:, here].astype(bf16)
                grad_ref[part, 2, own, lanes] = (v_acc[head][:, here] * (1.0 / score_scale)).astype(bf16)

        @pl.when(first_step)
        def _():
            for part in range(part_count):
                fetch_rows(part).wait()

        wide = group * width
        total = None
        for part in range(part_count):
            stacked = jnp.concatenate([grad_ref[part, index] for index in range(3)], axis=0)
            term = dot(stacked, rows[part])
            total = term if total is None else total + term
        for head in range(group):
            own = slice(head * width, (head + 1) * width)
            for index in range(3):
                at = index * wide + head * width
                weight_ref[head, index * width : (index + 1) * width] = total[at : at + width].astype(bf16)
            weight_ref[head, 3 * width :] = w_acc[own, :].astype(bf16)
        for step in range(bias_grad_ref.shape[1] // wide):

            @pl.when(pl.program_id(0) == step)
            def _():
                for index in range(2):
                    total = jnp.sum(b_acc[index].T, axis=0, keepdims=True)
                    bias_grad_ref[index : index + 1, step * wide : (step + 1) * wide] = total


def attend_backward(
    width, first, heads, kept_first, call, before, shift, e, dos, o, inv, q, kv, biases, w, sine, cosine, table,
    rows,
):
    parts, flat, n = q.shape
    model, seq = table.shape
    blocks, per_part = seq // ROWS, n // ROWS
    group = 2 if heads % 2 == 0 else 1
    wide, skip, kept_skip = group * width, first // group, (first - kept_first) // group

    def index_part(h, i, s):
        held = lax.rem(i + s[0], blocks)
        return (held // per_part, h + skip, lax.rem(held, per_part))

    def grad_part(number):
        def index(h, i, s):
            held = lax.rem(i + s[0], blocks)
            return (h + skip, jnp.where(held // per_part == number, lax.rem(held, per_part), 0))

        return pl.BlockSpec((wide, ROWS), index)

    wave = pl.BlockSpec((model // 2, ROWS), lambda h, i, s: (0, i))
    anywhere = pl.BlockSpec(memory_space=pl.ANY)
    chained = list(before)
    arguments = [
        shift, e, o, inv, q, kv, biases, w, sine, cosine, table, *rows, *dos, *chained
    ]
    return pl.pallas_call(
        functools.partial(backward_kernel, blocks, width, parts, len(chained)),
        grid_spec=pltpu.PrefetchScalarGridSpec(
            num_scalar_prefetch=1,
            grid=(heads // group, blocks),
            in_specs=[
                pl.BlockSpec((group, None, seq, ROWS), lambda h, i, s: (h + kept_skip, i, 0, 0)),
                pl.BlockSpec((group, width, ROWS), lambda h, i, s: (h + kept_skip, 0, i)),
                pl.BlockSpec((group, 1, ROWS), lambda h, i, s: (h + kept_skip, 0, i)),
                pl.BlockSpec((None, wide, ROWS), index_part),
                pl.BlockSpec((2, parts, wide, n), lambda h, i, s: (0, 0, h + skip, 0)),
                pl.BlockSpec((wide, 8), lambda h, i, s: (h + skip, 0)),
                pl.BlockSpec((wide, model), lambda h, i, s: (h + skip, 0)),
                wave, wave, anywhere,
                *[anywhere] * parts,
                *[grad_part(index) for index in range(parts)],
                *[anywhere] * len(chained),
            ],
            out_specs=[
                pl.BlockSpec((parts, 3, wide, n), lambda h, i, s: (0, 0, h + skip, 0)),
                pl.BlockSpec(
                    (None, group, 4 * width, model), lambda h, i, s: (jnp.where(s[1] == call, 0, 1), h, 0, 0)
                ),
                pl.BlockSpec((2, heads * width), lambda h, i, s: (0, 0)),
            ],
            scratch_shapes=[
                pltpu.VMEM((seq, wide), bf16),
                pltpu.VMEM((group, model, ROWS), bf16),
                pltpu.VMEM((wide, model), f32),
                pltpu.VMEM((2, wide, 128), f32),
                pltpu.VMEM((parts, n, model), bf16),
                pltpu.SemaphoreType.DMA((group * blocks + parts,)),
                *[pltpu.VMEM((model + width, seq), bf16)] * group,
                *[pltpu.VMEM((model + width, ROWS), f32)] * group,
                *[pltpu.VMEM((width, seq), f32)] * group,
                *[pltpu.VMEM((width, seq), f32)] * group,
            ],
        ),
        out_shape=[
            jax.ShapeDtypeStruct((parts, 3, flat, n), bf16),
            jax.ShapeDtypeStruct((2, heads, 4 * width, model), bf16),
            jax.ShapeDtypeStruct((2, heads * width), f32),
        ],
        input_output_aliases={len(arguments) - 2: 0, len(arguments) - 1: 1} if chained else {},
        compiler_params=pltpu.CompilerParams(vmem_limit_bytes=ATTEND_VMEM_LIMIT),
        cost_estimate=pl.CostEstimate(
            flops=2 * heads * seq * seq * (model + 4 * width) * 5 // 8,
            bytes_accessed=heads * seq * seq * 2,
            transcendentals=0,
        ),
        name="attend_backward",
    )(*arguments)


def waves_kernel(near_sin_ref, near_cos_ref, far_sin_ref, far_cos_ref, sin_ref, cos_ref, table_t_ref, table_ref):
    half, seq = sin_ref.shape
    for index in range(seq // 128):
        here = slice(index * 128, (index + 1) * 128)
        far_sin, far_cos = far_sin_ref[:, index : index + 1], far_cos_ref[:, index : index + 1]
        sine = far_sin * near_cos_ref[...] + far_cos * near_sin_ref[...]
        cosine = far_cos * near_cos_ref[...] - far_sin * near_sin_ref[...]
        sin_ref[:, here] = sine
        cos_ref[:, here] = cosine
        table_t_ref[:half, here] = cosine.astype(bf16)
        table_t_ref[half:, here] = sine.astype(bf16)
        table_ref[here, :half] = cosine.T.astype(bf16)
        table_ref[here, half:] = sine.T.astype(bf16)


def waves(seq, model):
    exponent = -jnp.arange(0, model, 2, dtype=jnp.int32).astype(f32) / model
    frequency = jnp.power(10000.0, exponent)[:, None]
    near = frequency * jnp.arange(128, dtype=jnp.int32).astype(f32)[None, :]
    far = frequency * (128 * jnp.arange(seq // 128, dtype=jnp.int32)).astype(f32)[None, :]
    half = model // 2
    return pl.pallas_call(
        waves_kernel,
        out_shape=[
            jax.ShapeDtypeStruct((half, seq), f32), jax.ShapeDtypeStruct((half, seq), f32),
            jax.ShapeDtypeStruct((model, seq), bf16), jax.ShapeDtypeStruct((seq, model), bf16),
        ],
        compiler_params=pltpu.CompilerParams(vmem_limit_bytes=VMEM_LIMIT),
        cost_estimate=pl.CostEstimate(flops=6 * half * seq, bytes_accessed=16 * half * seq, transcendentals=0),
        name="waves",
    )(jnp.sin(near), jnp.cos(near), jnp.sin(far), jnp.cos(far))


def middle_kernel(piece_count, core_ref, side_ref, *refs):
    refs = list(refs)

    def take(count):
        out = refs[:count]
        del refs[:count]
        return out

    ins, cots, mine, theirs = take(2), take(2), take(piece_count), take(piece_count)
    out_hbm, down_hbm, up_hbm, first_hbm, second_hbm, bias_ref = take(6)
    vectors = take(4)
    y_ref, mg_ref, ag_mine_ref, ag_other_ref = take(4)
    keeps, sends = take(2), take(2)
    sum_ref, bias_grad_ref = take(2)
    source, cotangent, att, out_w, down_w, up_w, first_w, second_w, sems = refs
    model = source.shape[1]
    size = out_hbm.shape[0]
    core, side = core_ref[0], side_ref[0]
    rest = first_hbm.shape[0] - size // 2
    copies = []

    def copy(from_ref, to_ref):
        copies.append(pltpu.make_async_copy(from_ref, to_ref, sems.at[len(copies)]))
        return copies[-1]

    def aligned(start, count):
        return pl.ds(pl.multiple_of(start, count), count)

    begin = []
    for pieces_of, half, index in ((mine, core, 0), (theirs, 1 - core, 1)):
        for number, ref in enumerate(pieces_of):
            count = ref.shape[1]
            begin.append(copy(ref.at[index], att.at[aligned(half * size + number * count, count), :]))
    begin.append(copy(out_hbm, out_w.at[aligned(side * size, size), :]))
    quarter = size // 2
    for ref, part in ((first_hbm, core), (second_hbm, 1 - core)):
        to = out_w.at[aligned((1 - side) * size + part * quarter, quarter), :]
        begin.append(copy(ref.at[pl.ds(0, quarter), :], to))
    ups = copy(up_hbm, up_w)
    downs = copy(down_hbm, down_w)
    extra = [
        copy(ref.at[pl.ds(quarter, rest), :], to)
        for ref, to in ((first_hbm, first_w), (second_hbm, second_w))
    ]
    at = len(copies)

    def choose(pair, to, number):
        both = [pltpu.make_async_copy(ref, to, sems.at[number]) for ref in pair]
        pl.when(core == side)(both[0].start)
        pl.when(core != side)(both[1].start)
        return both[0]

    for item in begin:
        item.start()
    source_copy = choose(ins, source, at)
    ups.start()
    cot_copy = choose(cots, cotangent, at + 1)
    downs.start()
    for item in extra:
        item.start()

    out_bias, gain, bias, down_bias = (ref[...] for ref in vectors)
    for item in begin:
        item.wait()
    branch = dot(att[...], out_w[...], TN)
    source_copy.wait()
    middle = source[...].astype(f32) + (branch + out_bias)
    centre = middle - jnp.mean(middle, axis=1, keepdims=True)
    inverse = lax.rsqrt(jnp.mean(centre * centre, axis=1, keepdims=True) + epsilon)
    unit = centre * inverse
    rows2 = (unit * gain + bias).astype(bf16)
    ups.wait()
    cot_copy.wait()
    downs.wait()
    for item in extra:
        item.wait()
    cot = cotangent[...]
    y = e = None
    for number in range(4):
        if number < 2:
            part = core if number == 0 else 1 - core
            here = aligned(part * model, model)
            down, up, up_bias = down_w[here, :], up_w[:, here], bias_ref[:, here]
            half = side
        else:
            part = core if number == 2 else 1 - core
            ref = first_w if number == 2 else second_w
            down, up = ref[:model, :], ref[model : 2 * model, :]
            up_bias = jnp.sum(ref[2 * model : 2 * model + 16, :].astype(f32), axis=0, keepdims=True)
            half = 1 - side
        result = (keeps, sends)[number % 2][number // 2]
        pre = dot(rows2, up) + up_bias
        cdf = 0.5 * (1.0 + lax.erf(pre * 0.7071067811865476))
        active = (pre * cdf).astype(bf16)
        slope = cdf + pre * (jnp.exp(pre * pre * -0.5) * 0.3989422804014327)
        low = (slope * dot(cot, down, NT)).astype(bf16)
        bias_grad_ref[pl.ds(half * 2 + part, 1), :] = jnp.sum(low.astype(f32), axis=0, keepdims=True)
        add_y, add_e = dot(active, down), dot(low, up, NT)
        y = add_y if y is None else y + add_y
        e = add_e if e is None else e + add_e
        result[quarter : quarter + model, :] = dot(active, cot, TN).astype(bf16)
        result[quarter + model :, :] = dot(rows2, low, TN).astype(bf16)
    y_ref[...] = (middle + (y + down_bias)).astype(bf16)
    grad = cot.astype(f32)
    scaled = e * gain
    change = scaled - jnp.mean(scaled, axis=1, keepdims=True)
    change = change - unit * jnp.mean(scaled * unit, axis=1, keepdims=True)
    middle_grad = grad + inverse * change
    mg_ref[...] = middle_grad
    low_grad = middle_grad.astype(bf16)
    sums = (low_grad.astype(f32), e * unit, e, grad)
    for index, term in enumerate(sums):
        sum_ref[index : index + 1, :] = jnp.sum(term, axis=0, keepdims=True)
    ag_mine_ref[...] = dot(out_w[aligned(core * size, size), :], low_grad, NT).astype(bf16)
    ag_other_ref[...] = dot(out_w[aligned((1 - core) * size, size), :], low_grad, NT).astype(bf16)
    for number, half in ((0, side), (1, 1 - side)):
        for ref, part in ((keeps[number], core), (sends[number], 1 - core)):
            rows = att[aligned(half * size + part * quarter, quarter), :]
            ref[:quarter, :] = dot(rows, low_grad).astype(bf16)


def middle_layer(core, side, ins, cots, mine, theirs, own, first, second, bias, vectors):
    n, model = ins[0].shape
    size, hidden = own[0].shape[0], own[1].shape[0]
    quarter = size // 2
    packed = quarter + 2 * model
    extra = first.shape[0] - quarter
    anywhere = pl.BlockSpec(memory_space=pl.ANY)
    vmem = pl.BlockSpec(memory_space=pltpu.VMEM)
    arguments = [core, side, *ins, *cots, *mine, *theirs, *own, first, second, bias, *vectors]
    shapes = [
        jax.ShapeDtypeStruct((n, model), bf16),
        jax.ShapeDtypeStruct((n, model), f32),
        jax.ShapeDtypeStruct((size, n), bf16),
        jax.ShapeDtypeStruct((size, n), bf16),
        *[jax.ShapeDtypeStruct((packed, model), bf16)] * 4,
        jax.ShapeDtypeStruct((4, model), f32),
        jax.ShapeDtypeStruct((4, model), f32),
    ]
    return pl.pallas_call(
        functools.partial(middle_kernel, len(mine)),
        in_specs=[pl.BlockSpec(memory_space=pltpu.SMEM)] * 2 + [anywhere] * (len(arguments) - 7) + [vmem] * 5,
        out_specs=[vmem] * len(shapes),
        out_shape=shapes,
        scratch_shapes=[
            pltpu.VMEM((n, model), bf16), pltpu.VMEM((n, model), bf16),
            pltpu.VMEM((2 * size, n), bf16), pltpu.VMEM((2 * size, model), bf16),
            pltpu.VMEM((hidden, model), bf16), pltpu.VMEM((model, hidden), bf16),
            pltpu.VMEM((extra, model), bf16), pltpu.VMEM((extra, model), bf16),
            pltpu.SemaphoreType.DMA((2 * len(mine) + 9,)),
        ],
        compiler_params=pltpu.CompilerParams(vmem_limit_bytes=VMEM_LIMIT),
        cost_estimate=pl.CostEstimate(
            flops=2 * n * model * (6 * size + 12 * hidden),
            bytes_accessed=n * model * 14 + 8 * packed * model * 2,
            transcendentals=4 * n * hidden,
        ),
        name="middle_layer",
    )(*arguments)


def first_norm_kernel(halves, core_ref, own_ref, got_ref, up_ref, got_up_ref, middle_ref, gain_ref, sum_ref, bias_ref, *refs):
    biases = refs[: -4]
    grad_ref, low_ref, small_ref, acc = refs[-4:]
    step = pl.program_id(0)
    model = own_ref.shape[1]

    @pl.when(step == 0)
    def _():
        acc[...] = jnp.zeros_like(acc)

    source = jnp.where(core_ref[1] == 1, own_ref[...].astype(f32), got_ref[...].astype(f32))
    upstream = up_ref[...] + got_up_ref[...].astype(f32)
    centre = source - jnp.mean(source, axis=1, keepdims=True)
    inverse = lax.rsqrt(jnp.mean(centre * centre, axis=1, keepdims=True) + epsilon)
    unit = centre * inverse
    scaled = upstream * gain_ref[...]
    change = scaled - jnp.mean(scaled, axis=1, keepdims=True)
    change = change - unit * jnp.mean(scaled * unit, axis=1, keepdims=True)
    grad = middle_ref[...] + inverse * change
    grad_ref[...] = grad
    low_ref[...] = grad.astype(bf16)
    acc[0:1, :] += jnp.sum(upstream * unit, axis=0, keepdims=True)
    acc[1:2, :] += jnp.sum(upstream, axis=0, keepdims=True)

    @pl.when(step == pl.num_programs(0) - 1)
    def _():
        small_ref[...] = jnp.zeros_like(small_ref)
        at = 0
        for ref, count in ((acc, 2), (sum_ref, 4)):
            for index in range(count):
                for lane in range(0, model, 128):
                    small_ref[at : at + 1, :] = ref[index : index + 1, lane : lane + 128]
                    at += 1
        width = sum(ref.shape[1] for ref in biases)
        for index in range(2):
            row = at + core_ref[0] * (width // 128)
            for ref in biases:
                for lane in range(0, ref.shape[1], 128):
                    small_ref[pl.ds(row, 1), :] = ref[index : index + 1, lane : lane + 128]
                    row = row + 1
            at += halves * width // 128
        for index in range(4):
            for lane in range(0, model, 128):
                small_ref[at : at + 1, :] = bias_ref[index : index + 1, lane : lane + 128]
                at += 1


def first_norm(halves, flags, own, got, up, got_up, middle, gain, sums, up_bias, biases):
    n, model = own.shape
    count = 4 if n % 32 == 0 and n >= 512 else 1
    rows = pl.BlockSpec((n // count, model), lambda i: (i, 0))
    size = (10 * model + 2 * halves * sum(v.shape[1] for v in biases)) // 128
    arguments = [flags, own, got, up, got_up, middle, gain, sums, up_bias, *biases]
    return pl.pallas_call(
        functools.partial(first_norm_kernel, halves),
        grid=(count,),
        in_specs=[pl.BlockSpec(memory_space=pltpu.SMEM)] + [rows] * 5 + [resident(v.shape) for v in arguments[6:]],
        out_specs=[rows, rows, pl.BlockSpec((size, 128), lambda i: (0, 0))],
        out_shape=[
            jax.ShapeDtypeStruct((n, model), f32), jax.ShapeDtypeStruct((n, model), bf16),
            jax.ShapeDtypeStruct((size, 128), f32),
        ],
        scratch_shapes=[pltpu.VMEM((2, model), f32)],
        compiler_params=pltpu.CompilerParams(vmem_limit_bytes=ATTEND_VMEM_LIMIT),
        cost_estimate=pl.CostEstimate(flops=20 * n * model, bytes_accessed=16 * n * model, transcendentals=0),
        name="first_norm",
    )(*arguments)


def finish_kernel(width, order_ref, first_ref, second_ref, qkv_ref, pos_ref):
    count = first_ref.shape[0] // (4 * width)

    def run(refs):
        for index in range(4):
            rows = []
            for ref in refs:
                for head in range(count):
                    start = (head * 4 + index) * width
                    rows.append(ref[start : start + width, :].astype(f32))
            value = jnp.concatenate(rows, axis=0).T
            if index < 3:
                qkv_ref[index] = value
            else:
                pos_ref[...] = value

    pl.when(order_ref[0] == 0)(lambda: run((first_ref, second_ref)))
    pl.when(order_ref[0] == 1)(lambda: run((second_ref, first_ref)))


def finish(order, first, second, flat, width):
    model = first.shape[1]
    return pl.pallas_call(
        functools.partial(finish_kernel, width),
        in_specs=[pl.BlockSpec(memory_space=pltpu.SMEM)] + [pl.BlockSpec(memory_space=pltpu.VMEM)] * 2,
        out_shape=[
            jax.ShapeDtypeStruct((3, model, flat), f32), jax.ShapeDtypeStruct((model, flat), f32),
        ],
        compiler_params=pltpu.CompilerParams(vmem_limit_bytes=VMEM_LIMIT),
        name="finish",
    )(order, first, second)


def unpack_kernel(order_ref, first_ref, second_ref, out_ref, down_ref, up_ref):
    model = up_ref.shape[0]
    quarter = out_ref.shape[0] // 2

    def run(refs):
        for index, ref in enumerate(refs):
            here = slice(index * model, (index + 1) * model)
            out_ref[index * quarter : (index + 1) * quarter, :] = ref[:quarter, :].astype(f32)
            down_ref[here, :] = ref[quarter : quarter + model, :].astype(f32)
            up_ref[:, here] = ref[quarter + model :, :].astype(f32)

    pl.when(order_ref[0] == 0)(lambda: run((first_ref, second_ref)))
    pl.when(order_ref[0] == 1)(lambda: run((second_ref, first_ref)))


def unpack(order, first, second, flat, hidden):
    model = first.shape[1]
    return pl.pallas_call(
        unpack_kernel,
        in_specs=[pl.BlockSpec(memory_space=pltpu.SMEM)] + [pl.BlockSpec(memory_space=pltpu.VMEM)] * 2,
        out_shape=[
            jax.ShapeDtypeStruct((flat, model), f32), jax.ShapeDtypeStruct((hidden, model), f32),
            jax.ShapeDtypeStruct((model, hidden), f32),
        ],
        compiler_params=pltpu.CompilerParams(vmem_limit_bytes=VMEM_LIMIT),
        name="unpack",
    )(order, first, second)


class Paired:
    def __init__(self, dp_count):
        self.dp_count = dp_count
        self.core = lax.rem(lax.axis_index("dp"), 2)
        self.side = lax.axis_index("tensor")
        self.home = self.core == self.side
        self.index = self.core

    def trade(self, value):
        pairs = []
        for place in range(2 * self.dp_count):
            group, core, side = place // 4, place // 2 % 2, place % 2
            if core != side:
                pairs.append((place, group * 4 + side * 2 + core))
        return lax.ppermute(value, ("dp", "tensor"), pairs)

    def cross(self, value, flip):
        return lax.ppermute(value, "dp", [(i, i ^ flip) for i in range(self.dp_count)])

    def partner(self, value):
        return self.cross(value, 1)

    def across(self, value):
        return lax.ppermute(value, "tensor", [(0, 1), (1, 0)])

    def own(self, mine, traded):
        return jnp.where(self.home, mine, traded)

    def shift(self, blocks):
        return jnp.reshape(self.core * (blocks // 2), (1,)).astype(jnp.int32)

    def shared(self, value):
        return [value, self.partner(value)]

    def last_weights(self, out, down, up, bias):
        quarter, model = out.shape[0] // 2, out.shape[1]
        pack = jnp.concatenate([
            lax.dynamic_slice_in_dim(out, self.core * quarter, quarter, 0),
            lax.dynamic_slice_in_dim(down, self.core * model, model, 0),
            lax.dynamic_slice_in_dim(up, self.core * model, model, 1),
            lax.optimization_barrier(terms_of(lax.dynamic_slice_in_dim(bias, self.core * model, model, 0), 16)),
        ])
        return (out, down, up), pack, bias

    def last_first(self, pack):
        return self.across(pack)

    def last_second(self, first):
        return first, self.partner(first)

    def to_rows(self, attended):
        return attended, self.partner(attended)

    def to_heads(self, mine, other):
        return [mine, self.partner(other)]

    def summed(self, value, flips):
        for flip in flips:
            value = value + self.cross(value, flip)
        return value

    def flips(self):
        flips, flip = [], 2
        while flip < self.dp_count:
            flips.append(flip)
            flip *= 2
        return flips

    def groups(self):
        order = [0]
        for flip in self.flips()[::-1]:
            order = order + [place + flip for place in order]
        return [[place + core for place in order] for core in range(2)]

    def swap(self, value):
        return lax.all_to_all(value, "dp", 0, 0, axis_index_groups=self.groups(), tiled=True)


    def early_start(self, keep, send):
        gone = self.across(add(keep[1], self.partner(send[1])))
        return keep[0], self.partner(send[0]), gone

    def late_start(self, grads):
        keep, got = grads[0], self.partner(grads)[1]
        return jnp.where(self.home, keep, got), jnp.where(self.home, got, keep)

    def spread(self, value):
        count = self.dp_count // 2
        return self.swap(value).reshape(count, value.shape[0] // count, -1)

    def collect(self, value):
        copies = jnp.broadcast_to(value[None], (self.dp_count // 2, *value.shape))
        return self.swap(copies.reshape(-1, value.shape[1]))

    def joined(self, value, flips):
        for flip in flips:
            first = lax.rem(lax.axis_index("dp") // flip, 2) == 0
            other = self.cross(value, flip)
            value = jnp.concatenate([jnp.where(first, value, other), jnp.where(first, other, value)])
        return value


def total_of(terms):
    return jnp.sum(terms.astype(f32), axis=0).astype(bf16)


def add(a, b):
    return (a.astype(f32) + b.astype(f32)).astype(bf16)


def terms_of(vector, rows):
    terms, rest = [], vector
    for _ in range(3):
        terms.append(lax.reduce_precision(rest, 8, 7))
        rest = rest - terms[-1]
    terms += [jnp.zeros_like(vector)] * (rows - 3)
    return jnp.stack(terms).astype(bf16)


class Plain:
    def __init__(self):
        self.index = lax.axis_index("tensor")
        self.core = self.side = jnp.zeros((), jnp.int32)
        self.home = self.core == 0

    def trade(self, value):
        return value

    def own(self, mine, traded):
        return mine

    def shift(self, blocks):
        return jnp.zeros((1,), jnp.int32)

    def gather(self, value, axis=0):
        return lax.all_gather(value, "tensor", axis=axis, tiled=True)

    def shared(self, value):
        return [self.gather(value)]

    def last_weights(self, out, down, up, bias):
        out, down, up, bias = self.gather(out), self.gather(down), self.gather(up, 1), self.gather(bias)
        model = out.shape[1]
        half, wide = out.shape[0] // 2, down.shape[0] // 2
        packs = [
            jnp.concatenate([
                out[half + number * (half // 2) :][: half // 2],
                down[wide + number * model :][:model],
                up[:, wide + number * model :][:, :model],
                terms_of(bias[wide + number * model :][:model], 16),
            ])
            for number in range(2)
        ]
        return (out[:half], down[:wide], up[:, :wide]), packs, bias[:wide]

    def last_first(self, packs):
        return packs

    def last_second(self, first):
        return first

    def to_rows(self, attended):
        rows = lax.all_to_all(attended[0], "tensor", 1, 0, tiled=True)
        rows = rows.reshape(2, rows.shape[0] // 2, rows.shape[1])
        return rows, rows

    def to_heads(self, mine, other):
        return [lax.all_to_all(jnp.concatenate([mine, other]), "tensor", 0, 1, tiled=True)]

    def scatter(self, mine):
        return lax.psum_scatter(mine, "tensor", scatter_dimension=0, tiled=True)

    def total(self, value):
        return lax.psum(value, ("dp", "tensor"))

    def early_start(self, keep, send):
        quarters = [keep[0], send[0], keep[1], send[1]]
        model = keep[0].shape[1]
        quarter = keep[0].shape[0] - 2 * model
        pieces_of = (
            (jnp.concatenate([v[:quarter] for v in quarters]), 0),
            (jnp.concatenate([v[quarter : quarter + model] for v in quarters]), 0),
            (jnp.concatenate([v[quarter + model :] for v in quarters], axis=1), 1),
        )
        return [
            lax.psum_scatter(v.astype(f32), "tensor", scatter_dimension=d, tiled=True)
            for v, d in pieces_of
        ]


def norm_rows(values, norm_gain, norm_bias):
    centre = values - jnp.mean(values, axis=-1, keepdims=True)
    inverse = lax.rsqrt(jnp.mean(centre * centre, axis=-1, keepdims=True) + epsilon)
    normal = centre * inverse
    return normal * norm_gain + norm_bias


def local(
    inputs, lengths, norm1_gain, norm1_bias, query_key_value_weight, content_bias, position_bias,
    pos_weight, output_weight, out_bias, norm2_gain, norm2_bias, up_projection_weight, up_bias,
    down_projection_weight, down_bias, cotangent,
):
    tensor_count = lax.axis_size("tensor")
    dp_count = lax.axis_size("dp")
    heads, width = content_bias.shape
    paired = tensor_count == 2 and dp_count >= 2 and dp_count & (dp_count - 1) == 0 and heads % 2 == 0
    moves = Paired(dp_count) if paired else Plain()
    _, shard_rows, model = inputs.shape
    seq = shard_rows * tensor_count
    flat = heads * width
    hidden = up_bias.shape[0]
    shift = moves.shift(seq // ROWS)
    core, side = (jnp.reshape(v, (1,)).astype(jnp.int32) for v in (moves.core, moves.side))
    shift = jnp.concatenate([shift, core])
    home = jnp.reshape(moves.home, (1,)).astype(jnp.int32)

    together = lax.optimization_barrier

    row = lax.axis_index("tensor") * shard_rows + jnp.arange(shard_rows, dtype=jnp.int32)
    valid = (row < lengths[0])[:, None]

    got_source = moves.trade(inputs[0])
    vectors = jnp.concatenate([content_bias.reshape(-1), position_bias.reshape(-1)])
    terms = terms_of(vectors, 16).reshape(-1, flat)
    pieces_of = [query_key_value_weight.reshape(3 * model, flat), pos_weight, terms]
    got_pack = moves.trade(jnp.concatenate(pieces_of))
    own_last, last_pack, own_bias = moves.last_weights(
        output_weight, down_projection_weight, up_projection_weight, up_bias
    )
    own_cot = jnp.where(valid, cotangent[0], jnp.zeros_like(cotangent[0]))
    got_cot = moves.trade(own_cot)
    sine, cosine, table_t, table = waves(seq, model)
    got_pack, sine, cosine, table_t, table = together((got_pack, sine, cosine, table_t, table))

    source = moves.own(inputs[0], got_source).astype(f32)
    normed1 = norm_rows(source, norm1_gain, norm1_bias)
    rows1 = moves.shared(normed1.astype(bf16))
    q, kv, pos_rows, biases, qkv = project(
        home, rows1, query_key_value_weight, pos_weight, vectors.reshape(2, flat), got_pack
    )
    if paired:
        last_pack, pos_rows = together((last_pack, pos_rows))
    first_last = moves.last_first(last_pack)
    calls = min(FORWARD_CALLS, heads)
    each = heads // calls
    kept, mine, theirs = [], [], []
    for call in range(calls):
        low, *keep = attend_forward(
            width, call * each, each, shift, q, kv, biases, pos_rows, sine, cosine, table
        )
        kept.append(keep)
        low, other = moves.to_rows(low)
        mine.append(low)
        theirs.append(other)
        if call == 0 and paired:
            first_last, mine[0] = together((first_last, mine[0]))
    first_last, second_last = moves.last_second(first_last)

    y, middle_grad, att_mine, att_other, *packs, row_sums, up_bias_grad = middle_layer(
        core, side, (inputs[0], got_source), (own_cot, got_cot), mine, theirs, own_last, first_last, second_last,
        own_bias[None], [v[None] for v in (out_bias, norm2_gain, norm2_bias, down_bias)],
    )
    att_grads = moves.to_heads(att_mine, att_other)
    early = moves.early_start(packs[:2], packs[2:])

    calls = min(BACKWARD_CALLS, heads)
    step = heads // calls
    before, bias_grads = [], []
    for call in range(calls):
        first = call * step
        held = first // each
        low_out, inverse_sum, weights = kept[held]
        grads, weight_grads, bias_grad = attend_backward(
            width, first, step, held * each, call, before, shift, weights, att_grads, low_out, inverse_sum, q, kv,
            biases, pos_rows, sine, cosine, table_t, rows1,
        )
        bias_grads.append(bias_grad)
        if paired and call == 0:
            early = add(add(early[0], early[1]), early[2])
            early, weight_grads = together((early, weight_grads))
            early = moves.spread(early)
        before = [grads, weight_grads]

    def upstream(part):
        return jnp.einsum("nks,nkr->sr", grads[part], qkv, preferred_element_type=f32)

    got_y = moves.trade(y)
    if paired:
        early, weight_grads, got_y, grads = together((early, weight_grads, got_y, grads))
        kept_late, gone_late = moves.late_start(weight_grads.reshape(2, -1, model))
        gone_late, early, grads, *bias_grads = together((gone_late, early, grads, *bias_grads))
        got_late = moves.across(gone_late)
        early = total_of(early)
        got_up = moves.partner(upstream(1).astype(bf16))
        up = upstream(0)
        early, up = together((early, up))
        early = moves.joined(early, moves.flips()[:0:-1])
        got_late, up = together((got_late, up))
        late = moves.spread(add(kept_late, got_late))
    else:
        up = lax.psum_scatter(upstream(0), "tensor", scatter_dimension=0, tiled=True)
        got_up = jnp.zeros(up.shape, bf16)
        room = jnp.zeros((2, flat * tensor_count), f32)
        bias_grads = jnp.concatenate(bias_grads, axis=1)
        bias_grads = [lax.dynamic_update_slice_in_dim(room, bias_grads, moves.index * flat, 1)]
    input_grad, input_low, small = first_norm(
        2 if paired else 1, jnp.concatenate([core, home]).astype(jnp.int32), inputs[0], got_source, up, got_up,
        middle_grad, norm1_gain[None], row_sums, up_bias_grad, bias_grads,
    )
    if paired:
        flips = moves.flips()
        small = moves.summed(small, [1, *flips[:1]])
        early, small = together((early, small))
        early = moves.joined(early, flips[:1])
        small = moves.summed(small, flips[1:])
        small = small + moves.across(small)
        got_grad = moves.trade(input_low)
    else:
        small = moves.total(small)
    small = small.reshape(-1)
    if paired:
        late, small = together((late, small))
        late = total_of(late)
        late, early, got_y, got_grad = together((late, early, got_y, got_grad))
        input_grad = moves.own(input_grad, got_grad.astype(f32))
    output = moves.own(y, got_y)
    output = jnp.where(valid, output, jnp.zeros_like(output))

    vectors, at = [], 0
    for _ in range(6):
        vectors.append(small[at : at + model])
        at += model
    for count in (flat, flat, hidden):
        here = small[at : at + count * tensor_count]
        vectors.append(lax.dynamic_slice_in_dim(here, lax.axis_index("tensor") * count, count, 0))
        at += count * tensor_count

    if paired:
        late = moves.collect(late)
        out_grad, down_grad, up_grad = unpack(core, early, moves.partner(early), flat, hidden)
        late, out_grad, down_grad, up_grad, input_grad, output, *vectors = together(
            (late, out_grad, down_grad, up_grad, input_grad, output, *vectors)
        )
        qkv_grad, pos_grad = finish(core, late, moves.partner(late), flat, width)
    else:
        out_grad, down_grad, up_grad = (lax.psum(v.astype(bf16), "dp").astype(f32) for v in early)
        late = lax.psum(weight_grads[:calls], "dp").astype(f32).reshape(-1, 4, width, model)[:heads]
        qkv_grad = late[:, :3].transpose(1, 3, 0, 2).reshape(3, model, flat)
        pos_grad = late[:, 3].transpose(2, 0, 1).reshape(model, flat)

    return (
        output[None],
        input_grad[None],
        vectors[0],
        vectors[1],
        qkv_grad,
        vectors[6].reshape(heads, width),
        vectors[7].reshape(heads, width),
        pos_grad,
        out_grad,
        vectors[2],
        vectors[3],
        vectors[4],
        up_grad,
        vectors[8],
        down_grad,
        vectors[5],
    )


def solution(mesh):
    rows = P("dp", "tensor", None)
    return jax.shard_map(
        local,
        mesh=mesh,
        in_specs=(
            rows, P("dp"), P(), P(), P(None, None, "tensor"), P("tensor", None),
            P("tensor", None), P(None, "tensor"), P("tensor", None), P(), P(), P(),
            P(None, "tensor"), P("tensor"), P("tensor", None), P(), rows,
        ),
        out_specs=(
            rows, rows, P(), P(), P(None, None, "tensor"), P("tensor", None),
            P("tensor", None), P(None, "tensor"), P("tensor", None), P(), P(), P(),
            P(None, "tensor"), P("tensor"), P("tensor", None), P(),
        ),
        check_vma=False,
    )
```

```python
import functools

import jax
import jax.numpy as jnp
from jax import lax
from jax.experimental import pallas as pl
from jax.experimental.pallas import tpu as pltpu
from jax.sharding import PartitionSpec as P

ROWS = 512
HALF = 256
epsilon = 1e-05
score_scale = 0.125
masked_score = -1e30
NN = (((1,), (0,)), ((), ()))
NT = (((1,), (1,)), ((), ()))
TN = (((0,), (0,)), ((), ()))
TT = (((0,), (1,)), ((), ()))
f32 = jnp.float32
bf16 = jnp.bfloat16
FORWARD_CALLS = 2
VMEM_LIMIT = 60 << 20
ATTEND_VMEM_LIMIT = 56 << 20
BACKWARD_CALLS = 2


def dot(a, b, dims=NN):
    return lax.dot_general(a, b, dims, preferred_element_type=f32)


def resident(shape):
    return pl.BlockSpec(shape, lambda *_: (0,) * len(shape), pipeline_mode=pl.Buffered(1))


def project_kernel(part_count, flag_ref, vec_ref, *refs):
    rows_hbm, (own_hbm, pos_hbm, got_hbm) = refs[:part_count], refs[part_count : part_count + 3]
    q_hbm, kv_hbm, pos_out_ref, bias_ref, weight_ref, rows, source, q, kv, sems = refs[part_count + 3 :]
    model, flat = own_hbm.shape[1:]
    used = []

    def copy(from_ref, to_ref):
        used.append(None)
        return pltpu.make_async_copy(from_ref, to_ref, sems.at[len(used) - 1])

    own = [copy(own_hbm.at[index], source.at[pl.ds(index * model, model), :]) for index in range(3)]
    own.append(copy(pos_hbm, source.at[pl.ds(3 * model, model), :]))
    got = [copy(got_hbm, source)]
    loads = [copy(rows_hbm[part], rows.at[part]) for part in range(part_count)]
    home = flag_ref[0] == 1
    for condition, items in ((home, own), (jnp.logical_not(home), got)):

        @pl.when(condition)
        def _():
            for item in items:
                item.start()

    for item in loads:
        item.start()
    for condition, items in ((home, own), (jnp.logical_not(home), got)):

        @pl.when(condition)
        def _():
            for item in items:
                item.wait()

    for index in range(3):
        weight_ref[index] = source[index * model : (index + 1) * model, :].T
    stores = []
    for part in range(part_count):
        loads[part].wait()
        result = dot(weight_ref[...].reshape(3 * flat, model), rows[part], NT)
        q[part] = result[:flat]
        kv[0, part] = result[flat : 2 * flat].astype(bf16)
        kv[1, part] = result[2 * flat :].astype(bf16)
        new = [copy(q.at[part], q_hbm.at[part])]
        new += [copy(kv.at[index, part], kv_hbm.at[index, part]) for index in range(2)]
        for item in new:
            item.start()
        stores += new
    pos_out_ref[...] = source[3 * model : 4 * model, :].T
    terms = source[4 * model :, :].astype(f32)
    lines = [
        jnp.where(home, vec_ref[i : i + 1, :], terms[i : i + 1] + terms[i + 2 : i + 3] + terms[i + 4 : i + 5])
        for i in range(2)
    ]
    bias_ref[...] = jnp.concatenate([*lines, jnp.zeros((6, flat), f32)], axis=0).T
    for item in stores:
        item.wait()


def project(home, rows, own, pos, vectors, got):
    count = len(rows)
    n, model = rows[0].shape
    flat = own.shape[2]
    vmem, anywhere = pl.BlockSpec(memory_space=pltpu.VMEM), pl.BlockSpec(memory_space=pl.ANY)
    return pl.pallas_call(
        functools.partial(project_kernel, count),
        in_specs=[pl.BlockSpec(memory_space=pltpu.SMEM), vmem] + [anywhere] * (count + 3),
        out_specs=[anywhere] * 2 + [vmem] * 3,
        out_shape=[
            jax.ShapeDtypeStruct((count, flat, n), f32),
            jax.ShapeDtypeStruct((2, count, flat, n), bf16),
            jax.ShapeDtypeStruct((flat, model), bf16),
            jax.ShapeDtypeStruct((flat, 8), f32),
            jax.ShapeDtypeStruct((3, flat, model), bf16),
        ],
        scratch_shapes=[
            pltpu.VMEM((count, n, model), bf16), pltpu.VMEM(got.shape, bf16),
            pltpu.VMEM((count, flat, n), f32), pltpu.VMEM((2, count, flat, n), bf16),
            pltpu.SemaphoreType.DMA((5 + 4 * count,)),
        ],
        compiler_params=pltpu.CompilerParams(vmem_limit_bytes=VMEM_LIMIT),
        cost_estimate=pl.CostEstimate(
            flops=6 * count * n * model * flat, bytes_accessed=count * n * (model + 4 * flat) * 2,
            transcendentals=0,
        ),
        name="project",
    )(home, vectors, *rows, own, pos, got)


def pieces(block):
    out = [(key * ROWS, ROWS, 0) for key in range(block)]
    out.append((block * ROWS, HALF, 0))
    out.append((block * ROWS + HALF, HALF, HALF))
    return out


def place(index, shift, blocks, per_part):
    held = lax.rem(index + shift, blocks)
    lanes = pl.ds(pl.multiple_of(lax.rem(held, per_part) * ROWS, ROWS), ROWS)
    return held // per_part, lanes


def forward_kernel(
    blocks, width, shift_ref, q_ref, kv_ref, bias_ref, w_ref, sin_ref, cos_ref, table_hbm,
    low_ref, o_ref, inv_ref, e_ref, keys, values, query, sems, *scores,
):
    group = len(scores)
    model = w_ref.shape[1]
    half = model // 2
    per_part = kv_ref.shape[3] // ROWS
    block = pl.program_id(1)

    def fetch(index):
        rows = pl.ds(index * ROWS, ROWS)
        return pltpu.make_async_copy(table_hbm.at[rows, :], keys.at[rows, pl.ds(0, model)], sems.at[index])

    @pl.when((pl.program_id(0) == 0) & (block == 0))
    def _():
        for index in range(blocks):
            fetch(index).start()
        query[...] = jnp.zeros_like(query)

    @pl.when(block == 0)
    def _():
        for index in range(blocks):
            part, lanes = place(index, shift_ref[0], blocks, per_part)
            here = pl.ds(index * ROWS, ROWS)
            keys[here, model:] = kv_ref[0, part, :, lanes].T
            values[:, here] = kv_ref[1, part, :, lanes]

    def run(index):
        pl.when(pl.program_id(0) == 0)(lambda: fetch(index).wait())
        sine, cosine = sin_ref[...], cos_ref[...]
        for head in range(group):
            rows = slice(head * width, (head + 1) * width)
            offset = (q_ref[rows, :] + bias_ref[rows, 1:2]).astype(bf16)
            pair = dot(w_ref[rows, :], offset, TN)
            up, low = pair[:half], pair[half:]
            query[head, :half] = ((up * sine + low * cosine) * score_scale).astype(bf16)
            query[head, half:model] = ((low * sine - up * cosine) * score_scale).astype(bf16)
            content = (q_ref[rows, :] + bias_ref[rows, :1]).astype(bf16)
            at = model + head * width
            query[head, at : at + width] = (content.astype(f32) * score_scale).astype(bf16)

        def score(head):
            top = jnp.full((8, ROWS), masked_score, f32)
            for start, count, first in pieces(index):
                part = dot(keys[start : start + count, :], query[head, :, first:])
                if start >= index * ROWS:
                    row = lax.broadcasted_iota(jnp.int32, part.shape, 0) + (start - index * ROWS)
                    col = lax.broadcasted_iota(jnp.int32, part.shape, 1) + first
                    part = jnp.where(col >= row, part, masked_score)
                scores[head][start : start + count, first:] = part
                best = jnp.max(part.reshape(count // 8, 8, ROWS - first), axis=0)
                if first:
                    best = jnp.maximum(top[:, first:], best)
                    top = jnp.concatenate([top[:, :first], best], axis=1)
                else:
                    top = jnp.maximum(top, best)
            return jnp.max(top, axis=0, keepdims=True)

        def attend(head, peak):
            rows = slice(head * width, (head + 1) * width)
            total = jnp.zeros((8, ROWS), f32)
            out = jnp.zeros((width, ROWS), f32)
            for start, count, first in pieces(index):
                weight = jnp.exp(scores[head][start : start + count, first:] - peak[:, first:])
                gain = jnp.sum(weight.reshape(count // 8, 8, ROWS - first), axis=0)
                rounded = weight.astype(bf16)
                e_ref[head, start : start + count, first:] = rounded
                add = dot(values[rows, start : start + count], rounded)
                if first:
                    total = jnp.concatenate([total[:, :first], total[:, first:] + gain], axis=1)
                    out = jnp.concatenate([out[:, :first], out[:, first:] + add], axis=1)
                else:
                    total = total + gain
                    out = out + add
            inverse = 1.0 / jnp.sum(total, axis=0, keepdims=True)
            out = out * inverse
            o_ref[head] = out
            low_ref[rows, :] = out.astype(bf16)
            inv_ref[head] = inverse

        peak = score(0)
        for head in range(group):
            following = score(head + 1) if head + 1 < group else None
            attend(head, peak)
            peak = following

    for index in range(blocks):
        pl.when(block == index)(functools.partial(run, index))


def attend_forward(width, first, heads, shift, q, kv, biases, w, sine, cosine, table):
    parts, _, n = q.shape
    seq, model = table.shape
    blocks, per_part = seq // ROWS, n // ROWS
    group = 2 if heads % 2 == 0 else 1
    wide, skip = group * width, first // group

    def part(offset):
        def index(h, i, s):
            held = lax.rem(i + s[0], blocks)
            return (held // per_part, h + offset, lax.rem(held, per_part))

        return pl.BlockSpec((None, wide, ROWS), index)

    wave = pl.BlockSpec((model // 2, ROWS), lambda h, i, s: (0, i))
    return pl.pallas_call(
        functools.partial(forward_kernel, blocks, width),
        grid_spec=pltpu.PrefetchScalarGridSpec(
            num_scalar_prefetch=1,
            grid=(heads // group, blocks),
            in_specs=[
                part(skip),
                pl.BlockSpec((2, parts, wide, n), lambda h, i, s: (0, 0, h + skip, 0)),
                pl.BlockSpec((wide, 8), lambda h, i, s: (h + skip, 0)),
                pl.BlockSpec((wide, model), lambda h, i, s: (h + skip, 0)),
                wave, wave, pl.BlockSpec(memory_space=pl.ANY),
            ],
            out_specs=[
                part(0),
                pl.BlockSpec((group, width, ROWS), lambda h, i, s: (h, 0, i)),
                pl.BlockSpec((group, 1, ROWS), lambda h, i, s: (h, 0, i)),
                pl.BlockSpec((group, None, seq, ROWS), lambda h, i, s: (h, i, 0, 0)),
            ],
            scratch_shapes=[
                pltpu.VMEM((seq, model + wide), bf16),
                pltpu.VMEM((wide, seq), bf16),
                pltpu.VMEM((group, model + wide, ROWS), bf16),
                pltpu.SemaphoreType.DMA((blocks,)),
                *[pltpu.VMEM((seq, ROWS), f32)] * group,
            ],
        ),
        out_shape=[
            jax.ShapeDtypeStruct((parts, heads * width, n), bf16),
            jax.ShapeDtypeStruct((heads, width, seq), f32),
            jax.ShapeDtypeStruct((heads, 1, seq), f32),
            jax.ShapeDtypeStruct((heads, blocks, seq, ROWS), bf16),
        ],
        compiler_params=pltpu.CompilerParams(vmem_limit_bytes=ATTEND_VMEM_LIMIT),
        cost_estimate=pl.CostEstimate(
            flops=2 * heads * seq * seq * (model + 2 * width) * 5 // 8,
            bytes_accessed=heads * seq * seq * 2,
            transcendentals=heads * seq * seq // 2,
        ),
        name="attend_forward",
    )(shift, q, kv, biases, w, sine, cosine, table)


def backward_kernel(
    blocks, width, part_count, chained, shift_ref, e_ref, o_ref, inv_ref, q_ref, kv_ref, bias_ref, w_ref,
    sin_ref, cos_ref, table_hbm, *refs,
):
    rows_hbm, dos = refs[:part_count], refs[part_count : 2 * part_count]
    refs = refs[2 * part_count + chained :]
    grad_ref, weight_ref, bias_grad_ref = refs[:3]
    values, small, w_acc, b_acc, rows, sems = refs[3:9]
    group = e_ref.shape[0]
    keys, query_acc, k_acc, v_acc = (refs[9 + i * group : 9 + (i + 1) * group] for i in range(4))
    model = w_ref.shape[1]
    half = model // 2
    per_part = kv_ref.shape[3] // ROWS
    block = pl.program_id(1)
    first_step = pl.program_id(0) == 0

    def fetch(head, index):
        lanes = pl.ds(index * ROWS, ROWS)
        to = keys[head].at[pl.ds(0, model), lanes]
        return pltpu.make_async_copy(table_hbm.at[:, lanes], to, sems.at[head * blocks + index])

    def fetch_rows(part):
        return pltpu.make_async_copy(rows_hbm[part], rows.at[part], sems.at[group * blocks + part])

    @pl.when(first_step & (block == 0))
    def _():
        for index in range(blocks):
            for head in range(group):
                fetch(head, index).start()
        for part in range(part_count):
            fetch_rows(part).start()

    @pl.when(block == 0)
    def _():
        for index in range(blocks):
            part, lanes = place(index, shift_ref[0], blocks, per_part)
            here = pl.ds(index * ROWS, ROWS)
            for head in range(group):
                own = slice(head * width, (head + 1) * width)
                keys[head][model:, here] = kv_ref[0, part, own, lanes]
            values[here, :] = kv_ref[1, part, :, lanes].T
        for ref in (*k_acc, *v_acc, w_acc, b_acc):
            ref[...] = jnp.zeros_like(ref)

    def run(index):
        @pl.when(first_step)
        def _():
            for head in range(group):
                fetch(head, index).wait()

        held = place(index, shift_ref[0], blocks, per_part)[0]
        sides = []
        for head in range(group):
            own = slice(head * width, (head + 1) * width)
            out_grad = dos[0][own, :]
            for part in range(1, part_count):
                out_grad = jnp.where(held == part, dos[part][own, :], out_grad)
            scaled = (out_grad.astype(f32) * (inv_ref[head] * score_scale)).astype(bf16)
            delta = jnp.sum(scaled.astype(f32) * o_ref[head], axis=0, keepdims=True)
            content_low = (q_ref[own, :] + bias_ref[own, :1]).astype(bf16)
            sides.append((own, scaled, delta, content_low))
        for start, count, first in pieces(index):
            here = slice(start, start + count)
            for head in range(group):
                own, scaled, delta, content_low = sides[head]
                weight = e_ref[head, here, first:]
                grad = dot(values[here, own], scaled[:, first:])
                change = (weight.astype(f32) * (grad - delta[:, first:])).astype(bf16)
                term = dot(keys[head][:, here], change)
                if start == 0:
                    query_acc[head][...] = term
                else:
                    query_acc[head][:, first:] += term
                v_acc[head][:, here] += dot(scaled[:, first:], weight, NT)
                k_acc[head][:, here] += dot(content_low[:, first:], change, NT)
        sine, cosine = sin_ref[...], cos_ref[...]
        part, lanes = place(index, shift_ref[0], blocks, per_part)
        for head in range(group):
            own = sides[head][0]
            up, low = query_acc[head][:half], query_acc[head][half:model]
            small[head, :half] = (up * sine - low * cosine).astype(bf16)
            small[head, half:] = (up * cosine + low * sine).astype(bf16)
            offset = dot(w_ref[own, :], small[head])
            content = query_acc[head][model:]
            grad_ref[part, 0, own, lanes] = (content + offset).astype(bf16)
            offset_low = (q_ref[own, :] + bias_ref[own, 1:2]).astype(bf16)
            w_acc[own, :] += dot(offset_low, small[head], NT)
            for lane in range(0, ROWS, 128):
                b_acc[0, own] += content[:, lane : lane + 128]
                b_acc[1, own] += offset[:, lane : lane + 128]

    for index in range(blocks):
        pl.when(block == index)(functools.partial(run, index))

    @pl.when(block == blocks - 1)
    def _():
        for index in range(blocks):
            part, lanes = place(index, shift_ref[0], blocks, per_part)
            here = pl.ds(index * ROWS, ROWS)
            for head in range(group):
                own = slice(head * width, (head + 1) * width)
                grad_ref[part, 1, own, lanes] = k_acc[head][:, here].astype(bf16)
                grad_ref[part, 2, own, lanes] = (v_acc[head][:, here] * (1.0 / score_scale)).astype(bf16)

        @pl.when(first_step)
        def _():
            for part in range(part_count):
                fetch_rows(part).wait()

        wide = group * width
        total = None
        for part in range(part_count):
            stacked = jnp.concatenate([grad_ref[part, index] for index in range(3)], axis=0)
            term = dot(stacked, rows[part])
            total = term if total is None else total + term
        for head in range(group):
            own = slice(head * width, (head + 1) * width)
            for index in range(3):
                at = index * wide + head * width
                weight_ref[head, index * width : (index + 1) * width] = total[at : at + width].astype(bf16)
            weight_ref[head, 3 * width :] = w_acc[own, :].astype(bf16)
        for step in range(bias_grad_ref.shape[1] // wide):

            @pl.when(pl.program_id(0) == step)
            def _():
                for index in range(2):
                    total = jnp.sum(b_acc[index].T, axis=0, keepdims=True)
                    bias_grad_ref[index : index + 1, step * wide : (step + 1) * wide] = total


def attend_backward(
    width, first, heads, kept_first, call, before, shift, e, dos, o, inv, q, kv, biases, w, sine, cosine, table,
    rows,
):
    parts, flat, n = q.shape
    model, seq = table.shape
    blocks, per_part = seq // ROWS, n // ROWS
    group = 2 if heads % 2 == 0 else 1
    wide, skip, kept_skip = group * width, first // group, (first - kept_first) // group

    def index_part(h, i, s):
        held = lax.rem(i + s[0], blocks)
        return (held // per_part, h + skip, lax.rem(held, per_part))

    def grad_part(number):
        def index(h, i, s):
            held = lax.rem(i + s[0], blocks)
            return (h + skip, jnp.where(held // per_part == number, lax.rem(held, per_part), 0))

        return pl.BlockSpec((wide, ROWS), index)

    wave = pl.BlockSpec((model // 2, ROWS), lambda h, i, s: (0, i))
    anywhere = pl.BlockSpec(memory_space=pl.ANY)
    chained = list(before)
    arguments = [
        shift, e, o, inv, q, kv, biases, w, sine, cosine, table, *rows, *dos, *chained
    ]
    return pl.pallas_call(
        functools.partial(backward_kernel, blocks, width, parts, len(chained)),
        grid_spec=pltpu.PrefetchScalarGridSpec(
            num_scalar_prefetch=1,
            grid=(heads // group, blocks),
            in_specs=[
                pl.BlockSpec((group, None, seq, ROWS), lambda h, i, s: (h + kept_skip, i, 0, 0)),
                pl.BlockSpec((group, width, ROWS), lambda h, i, s: (h + kept_skip, 0, i)),
                pl.BlockSpec((group, 1, ROWS), lambda h, i, s: (h + kept_skip, 0, i)),
                pl.BlockSpec((None, wide, ROWS), index_part),
                pl.BlockSpec((2, parts, wide, n), lambda h, i, s: (0, 0, h + skip, 0)),
                pl.BlockSpec((wide, 8), lambda h, i, s: (h + skip, 0)),
                pl.BlockSpec((wide, model), lambda h, i, s: (h + skip, 0)),
                wave, wave, anywhere,
                *[anywhere] * parts,
                *[grad_part(index) for index in range(parts)],
                *[anywhere] * len(chained),
            ],
            out_specs=[
                pl.BlockSpec((parts, 3, wide, n), lambda h, i, s: (0, 0, h + skip, 0)),
                pl.BlockSpec(
                    (None, group, 4 * width, model), lambda h, i, s: (jnp.where(s[1] == call, 0, 1), h, 0, 0)
                ),
                pl.BlockSpec((2, heads * width), lambda h, i, s: (0, 0)),
            ],
            scratch_shapes=[
                pltpu.VMEM((seq, wide), bf16),
                pltpu.VMEM((group, model, ROWS), bf16),
                pltpu.VMEM((wide, model), f32),
                pltpu.VMEM((2, wide, 128), f32),
                pltpu.VMEM((parts, n, model), bf16),
                pltpu.SemaphoreType.DMA((group * blocks + parts,)),
                *[pltpu.VMEM((model + width, seq), bf16)] * group,
                *[pltpu.VMEM((model + width, ROWS), f32)] * group,
                *[pltpu.VMEM((width, seq), f32)] * group,
                *[pltpu.VMEM((width, seq), f32)] * group,
            ],
        ),
        out_shape=[
            jax.ShapeDtypeStruct((parts, 3, flat, n), bf16),
            jax.ShapeDtypeStruct((2, heads, 4 * width, model), bf16),
            jax.ShapeDtypeStruct((2, heads * width), f32),
        ],
        input_output_aliases={len(arguments) - 2: 0, len(arguments) - 1: 1} if chained else {},
        compiler_params=pltpu.CompilerParams(vmem_limit_bytes=ATTEND_VMEM_LIMIT),
        cost_estimate=pl.CostEstimate(
            flops=2 * heads * seq * seq * (model + 4 * width) * 5 // 8,
            bytes_accessed=heads * seq * seq * 2,
            transcendentals=0,
        ),
        name="attend_backward",
    )(*arguments)


def waves_kernel(near_sin_ref, near_cos_ref, far_sin_ref, far_cos_ref, sin_ref, cos_ref, table_t_ref, table_ref):
    half, seq = sin_ref.shape
    for index in range(seq // 128):
        here = slice(index * 128, (index + 1) * 128)
        far_sin, far_cos = far_sin_ref[:, index : index + 1], far_cos_ref[:, index : index + 1]
        sine = far_sin * near_cos_ref[...] + far_cos * near_sin_ref[...]
        cosine = far_cos * near_cos_ref[...] - far_sin * near_sin_ref[...]
        sin_ref[:, here] = sine
        cos_ref[:, here] = cosine
        table_t_ref[:half, here] = cosine.astype(bf16)
        table_t_ref[half:, here] = sine.astype(bf16)
        table_ref[here, :half] = cosine.T.astype(bf16)
        table_ref[here, half:] = sine.T.astype(bf16)


def waves(seq, model):
    exponent = -jnp.arange(0, model, 2, dtype=jnp.int32).astype(f32) / model
    frequency = jnp.power(10000.0, exponent)[:, None]
    near = frequency * jnp.arange(128, dtype=jnp.int32).astype(f32)[None, :]
    far = frequency * (128 * jnp.arange(seq // 128, dtype=jnp.int32)).astype(f32)[None, :]
    half = model // 2
    return pl.pallas_call(
        waves_kernel,
        out_shape=[
            jax.ShapeDtypeStruct((half, seq), f32), jax.ShapeDtypeStruct((half, seq), f32),
            jax.ShapeDtypeStruct((model, seq), bf16), jax.ShapeDtypeStruct((seq, model), bf16),
        ],
        compiler_params=pltpu.CompilerParams(vmem_limit_bytes=VMEM_LIMIT),
        cost_estimate=pl.CostEstimate(flops=6 * half * seq, bytes_accessed=16 * half * seq, transcendentals=0),
        name="waves",
    )(jnp.sin(near), jnp.cos(near), jnp.sin(far), jnp.cos(far))


def middle_kernel(piece_count, core_ref, side_ref, *refs):
    refs = list(refs)

    def take(count):
        out = refs[:count]
        del refs[:count]
        return out

    ins, cots, mine, theirs = take(2), take(2), take(piece_count), take(piece_count)
    out_hbm, down_hbm, up_hbm, first_hbm, second_hbm, bias_ref = take(6)
    vectors = take(4)
    y_ref, mg_ref, ag_mine_ref, ag_other_ref = take(4)
    keeps, sends = take(2), take(2)
    sum_ref, bias_grad_ref = take(2)
    source, cotangent, att, out_w, down_w, up_w, first_w, second_w, sems = refs
    model = source.shape[1]
    size = out_hbm.shape[0]
    core, side = core_ref[0], side_ref[0]
    rest = first_hbm.shape[0] - size // 2
    copies = []

    def copy(from_ref, to_ref):
        copies.append(pltpu.make_async_copy(from_ref, to_ref, sems.at[len(copies)]))
        return copies[-1]

    def aligned(start, count):
        return pl.ds(pl.multiple_of(start, count), count)

    begin = []
    for pieces_of, half, index in ((mine, core, 0), (theirs, 1 - core, 1)):
        for number, ref in enumerate(pieces_of):
            count = ref.shape[1]
            begin.append(copy(ref.at[index], att.at[aligned(half * size + number * count, count), :]))
    begin.append(copy(out_hbm, out_w.at[aligned(side * size, size), :]))
    quarter = size // 2
    for ref, part in ((first_hbm, core), (second_hbm, 1 - core)):
        to = out_w.at[aligned((1 - side) * size + part * quarter, quarter), :]
        begin.append(copy(ref.at[pl.ds(0, quarter), :], to))
    ups = copy(up_hbm, up_w)
    downs = copy(down_hbm, down_w)
    extra = [
        copy(ref.at[pl.ds(quarter, rest), :], to)
        for ref, to in ((first_hbm, first_w), (second_hbm, second_w))
    ]
    at = len(copies)

    def choose(pair, to, number):
        both = [pltpu.make_async_copy(ref, to, sems.at[number]) for ref in pair]
        pl.when(core == side)(both[0].start)
        pl.when(core != side)(both[1].start)
        return both[0]

    for item in begin:
        item.start()
    source_copy = choose(ins, source, at)
    ups.start()
    cot_copy = choose(cots, cotangent, at + 1)
    downs.start()
    for item in extra:
        item.start()

    out_bias, gain, bias, down_bias = (ref[...] for ref in vectors)
    for item in begin:
        item.wait()
    branch = dot(att[...], out_w[...], TN)
    source_copy.wait()
    middle = source[...].astype(f32) + (branch + out_bias)
    centre = middle - jnp.mean(middle, axis=1, keepdims=True)
    inverse = lax.rsqrt(jnp.mean(centre * centre, axis=1, keepdims=True) + epsilon)
    unit = centre * inverse
    rows2 = (unit * gain + bias).astype(bf16)
    ups.wait()
    cot_copy.wait()
    downs.wait()
    for item in extra:
        item.wait()
    cot = cotangent[...]
    y = e = None
    for number in range(4):
        if number < 2:
            part = core if number == 0 else 1 - core
            here = aligned(part * model, model)
            down, up, up_bias = down_w[here, :], up_w[:, here], bias_ref[:, here]
            half = side
        else:
            part = core if number == 2 else 1 - core
            ref = first_w if number == 2 else second_w
            down, up = ref[:model, :], ref[model : 2 * model, :]
            up_bias = jnp.sum(ref[2 * model : 2 * model + 16, :].astype(f32), axis=0, keepdims=True)
            half = 1 - side
        result = (keeps, sends)[number % 2][number // 2]
        pre = dot(rows2, up) + up_bias
        cdf = 0.5 * (1.0 + lax.erf(pre * 0.7071067811865476))
        active = (pre * cdf).astype(bf16)
        slope = cdf + pre * (jnp.exp(pre * pre * -0.5) * 0.3989422804014327)
        low = (slope * dot(cot, down, NT)).astype(bf16)
        bias_grad_ref[pl.ds(half * 2 + part, 1), :] = jnp.sum(low.astype(f32), axis=0, keepdims=True)
        add_y, add_e = dot(active, down), dot(low, up, NT)
        y = add_y if y is None else y + add_y
        e = add_e if e is None else e + add_e
        result[quarter : quarter + model, :] = dot(active, cot, TN).astype(bf16)
        result[quarter + model :, :] = dot(rows2, low, TN).astype(bf16)
    y_ref[...] = (middle + (y + down_bias)).astype(bf16)
    grad = cot.astype(f32)
    scaled = e * gain
    change = scaled - jnp.mean(scaled, axis=1, keepdims=True)
    change = change - unit * jnp.mean(scaled * unit, axis=1, keepdims=True)
    middle_grad = grad + inverse * change
    mg_ref[...] = middle_grad
    low_grad = middle_grad.astype(bf16)
    sums = (low_grad.astype(f32), e * unit, e, grad)
    for index, term in enumerate(sums):
        sum_ref[index : index + 1, :] = jnp.sum(term, axis=0, keepdims=True)
    ag_mine_ref[...] = dot(out_w[aligned(core * size, size), :], low_grad, NT).astype(bf16)
    ag_other_ref[...] = dot(out_w[aligned((1 - core) * size, size), :], low_grad, NT).astype(bf16)
    for number, half in ((0, side), (1, 1 - side)):
        for ref, part in ((keeps[number], core), (sends[number], 1 - core)):
            rows = att[aligned(half * size + part * quarter, quarter), :]
            ref[:quarter, :] = dot(rows, low_grad).astype(bf16)


def middle_layer(core, side, ins, cots, mine, theirs, own, first, second, bias, vectors):
    n, model = ins[0].shape
    size, hidden = own[0].shape[0], own[1].shape[0]
    quarter = size // 2
    packed = quarter + 2 * model
    extra = first.shape[0] - quarter
    anywhere = pl.BlockSpec(memory_space=pl.ANY)
    vmem = pl.BlockSpec(memory_space=pltpu.VMEM)
    arguments = [core, side, *ins, *cots, *mine, *theirs, *own, first, second, bias, *vectors]
    shapes = [
        jax.ShapeDtypeStruct((n, model), bf16),
        jax.ShapeDtypeStruct((n, model), f32),
        jax.ShapeDtypeStruct((size, n), bf16),
        jax.ShapeDtypeStruct((size, n), bf16),
        *[jax.ShapeDtypeStruct((packed, model), bf16)] * 4,
        jax.ShapeDtypeStruct((4, model), f32),
        jax.ShapeDtypeStruct((4, model), f32),
    ]
    return pl.pallas_call(
        functools.partial(middle_kernel, len(mine)),
        in_specs=[pl.BlockSpec(memory_space=pltpu.SMEM)] * 2 + [anywhere] * (len(arguments) - 7) + [vmem] * 5,
        out_specs=[vmem] * len(shapes),
        out_shape=shapes,
        scratch_shapes=[
            pltpu.VMEM((n, model), bf16), pltpu.VMEM((n, model), bf16),
            pltpu.VMEM((2 * size, n), bf16), pltpu.VMEM((2 * size, model), bf16),
            pltpu.VMEM((hidden, model), bf16), pltpu.VMEM((model, hidden), bf16),
            pltpu.VMEM((extra, model), bf16), pltpu.VMEM((extra, model), bf16),
            pltpu.SemaphoreType.DMA((2 * len(mine) + 9,)),
        ],
        compiler_params=pltpu.CompilerParams(vmem_limit_bytes=VMEM_LIMIT),
        cost_estimate=pl.CostEstimate(
            flops=2 * n * model * (6 * size + 12 * hidden),
            bytes_accessed=n * model * 14 + 8 * packed * model * 2,
            transcendentals=4 * n * hidden,
        ),
        name="middle_layer",
    )(*arguments)


def first_norm_kernel(halves, core_ref, own_ref, got_ref, up_ref, got_up_ref, middle_ref, gain_ref, sum_ref, bias_ref, *refs):
    biases = refs[: -4]
    grad_ref, low_ref, small_ref, acc = refs[-4:]
    step = pl.program_id(0)
    model = own_ref.shape[1]

    @pl.when(step == 0)
    def _():
        acc[...] = jnp.zeros_like(acc)

    source = jnp.where(core_ref[1] == 1, own_ref[...].astype(f32), got_ref[...].astype(f32))
    upstream = up_ref[...] + got_up_ref[...].astype(f32)
    centre = source - jnp.mean(source, axis=1, keepdims=True)
    inverse = lax.rsqrt(jnp.mean(centre * centre, axis=1, keepdims=True) + epsilon)
    unit = centre * inverse
    scaled = upstream * gain_ref[...]
    change = scaled - jnp.mean(scaled, axis=1, keepdims=True)
    change = change - unit * jnp.mean(scaled * unit, axis=1, keepdims=True)
    grad = middle_ref[...] + inverse * change
    grad_ref[...] = grad
    low_ref[...] = grad.astype(bf16)
    acc[0:1, :] += jnp.sum(upstream * unit, axis=0, keepdims=True)
    acc[1:2, :] += jnp.sum(upstream, axis=0, keepdims=True)

    @pl.when(step == pl.num_programs(0) - 1)
    def _():
        small_ref[...] = jnp.zeros_like(small_ref)
        at = 0
        for ref, count in ((acc, 2), (sum_ref, 4)):
            for index in range(count):
                for lane in range(0, model, 128):
                    small_ref[at : at + 1, :] = ref[index : index + 1, lane : lane + 128]
                    at += 1
        width = sum(ref.shape[1] for ref in biases)
        for index in range(2):
            row = at + core_ref[0] * (width // 128)
            for ref in biases:
                for lane in range(0, ref.shape[1], 128):
                    small_ref[pl.ds(row, 1), :] = ref[index : index + 1, lane : lane + 128]
                    row = row + 1
            at += halves * width // 128
        for index in range(4):
            for lane in range(0, model, 128):
                small_ref[at : at + 1, :] = bias_ref[index : index + 1, lane : lane + 128]
                at += 1


def first_norm(halves, flags, own, got, up, got_up, middle, gain, sums, up_bias, biases):
    n, model = own.shape
    count = 4 if n % 32 == 0 and n >= 512 else 1
    rows = pl.BlockSpec((n // count, model), lambda i: (i, 0))
    size = (10 * model + 2 * halves * sum(v.shape[1] for v in biases)) // 128
    arguments = [flags, own, got, up, got_up, middle, gain, sums, up_bias, *biases]
    return pl.pallas_call(
        functools.partial(first_norm_kernel, halves),
        grid=(count,),
        in_specs=[pl.BlockSpec(memory_space=pltpu.SMEM)] + [rows] * 5 + [resident(v.shape) for v in arguments[6:]],
        out_specs=[rows, rows, pl.BlockSpec((size, 128), lambda i: (0, 0))],
        out_shape=[
            jax.ShapeDtypeStruct((n, model), f32), jax.ShapeDtypeStruct((n, model), bf16),
            jax.ShapeDtypeStruct((size, 128), f32),
        ],
        scratch_shapes=[pltpu.VMEM((2, model), f32)],
        compiler_params=pltpu.CompilerParams(vmem_limit_bytes=ATTEND_VMEM_LIMIT),
        cost_estimate=pl.CostEstimate(flops=20 * n * model, bytes_accessed=16 * n * model, transcendentals=0),
        name="first_norm",
    )(*arguments)


def finish_kernel(width, order_ref, first_ref, second_ref, qkv_ref, pos_ref):
    count = first_ref.shape[0] // (4 * width)

    def run(refs):
        for index in range(4):
            rows = []
            for ref in refs:
                for head in range(count):
                    start = (head * 4 + index) * width
                    rows.append(ref[start : start + width, :].astype(f32))
            value = jnp.concatenate(rows, axis=0).T
            if index < 3:
                qkv_ref[index] = value
            else:
                pos_ref[...] = value

    pl.when(order_ref[0] == 0)(lambda: run((first_ref, second_ref)))
    pl.when(order_ref[0] == 1)(lambda: run((second_ref, first_ref)))


def finish(order, first, second, flat, width):
    model = first.shape[1]
    return pl.pallas_call(
        functools.partial(finish_kernel, width),
        in_specs=[pl.BlockSpec(memory_space=pltpu.SMEM)] + [pl.BlockSpec(memory_space=pltpu.VMEM)] * 2,
        out_shape=[
            jax.ShapeDtypeStruct((3, model, flat), f32), jax.ShapeDtypeStruct((model, flat), f32),
        ],
        compiler_params=pltpu.CompilerParams(vmem_limit_bytes=VMEM_LIMIT),
        name="finish",
    )(order, first, second)


def unpack_kernel(order_ref, first_ref, second_ref, out_ref, down_ref, up_ref):
    model = up_ref.shape[0]
    quarter = out_ref.shape[0] // 2

    def run(refs):
        for index, ref in enumerate(refs):
            here = slice(index * model, (index + 1) * model)
            out_ref[index * quarter : (index + 1) * quarter, :] = ref[:quarter, :].astype(f32)
            down_ref[here, :] = ref[quarter : quarter + model, :].astype(f32)
            up_ref[:, here] = ref[quarter + model :, :].astype(f32)

    pl.when(order_ref[0] == 0)(lambda: run((first_ref, second_ref)))
    pl.when(order_ref[0] == 1)(lambda: run((second_ref, first_ref)))


def unpack(order, first, second, flat, hidden):
    model = first.shape[1]
    return pl.pallas_call(
        unpack_kernel,
        in_specs=[pl.BlockSpec(memory_space=pltpu.SMEM)] + [pl.BlockSpec(memory_space=pltpu.VMEM)] * 2,
        out_shape=[
            jax.ShapeDtypeStruct((flat, model), f32), jax.ShapeDtypeStruct((hidden, model), f32),
            jax.ShapeDtypeStruct((model, hidden), f32),
        ],
        compiler_params=pltpu.CompilerParams(vmem_limit_bytes=VMEM_LIMIT),
        name="unpack",
    )(order, first, second)


class Paired:
    def __init__(self, dp_count):
        self.dp_count = dp_count
        self.core = lax.rem(lax.axis_index("dp"), 2)
        self.side = lax.axis_index("tensor")
        self.home = self.core == self.side
        self.index = self.core

    def trade(self, value):
        pairs = []
        for place in range(2 * self.dp_count):
            group, core, side = place // 4, place // 2 % 2, place % 2
            if core != side:
                pairs.append((place, group * 4 + side * 2 + core))
        return lax.ppermute(value, ("dp", "tensor"), pairs)

    def cross(self, value, flip):
        return lax.ppermute(value, "dp", [(i, i ^ flip) for i in range(self.dp_count)])

    def partner(self, value):
        return self.cross(value, 1)

    def across(self, value):
        return lax.ppermute(value, "tensor", [(0, 1), (1, 0)])

    def own(self, mine, traded):
        return jnp.where(self.home, mine, traded)

    def shift(self, blocks):
        return jnp.reshape(self.core * (blocks // 2), (1,)).astype(jnp.int32)

    def shared(self, value):
        return [value, self.partner(value)]

    def last_weights(self, out, down, up, bias):
        quarter, model = out.shape[0] // 2, out.shape[1]
        pack = jnp.concatenate([
            lax.dynamic_slice_in_dim(out, self.core * quarter, quarter, 0),
            lax.dynamic_slice_in_dim(down, self.core * model, model, 0),
            lax.dynamic_slice_in_dim(up, self.core * model, model, 1),
            lax.optimization_barrier(terms_of(lax.dynamic_slice_in_dim(bias, self.core * model, model, 0), 16)),
        ])
        return (out, down, up), pack, bias

    def last_first(self, pack):
        return self.across(pack)

    def last_second(self, first):
        return first, self.partner(first)

    def to_rows(self, attended):
        return attended, self.partner(attended)

    def to_heads(self, mine, other):
        return [mine, self.partner(other)]

    def summed(self, value, flips):
        for flip in flips:
            value = value + self.cross(value, flip)
        return value

    def flips(self):
        flips, flip = [], 2
        while flip < self.dp_count:
            flips.append(flip)
            flip *= 2
        return flips

    def groups(self):
        order = [0]
        for flip in self.flips()[::-1]:
            order = order + [place + flip for place in order]
        return [[place + core for place in order] for core in range(2)]

    def swap(self, value):
        return lax.all_to_all(value, "dp", 0, 0, axis_index_groups=self.groups(), tiled=True)


    def early_start(self, keep, send):
        gone = self.across(add(keep[1], self.partner(send[1])))
        return keep[0], self.partner(send[0]), gone

    def late_start(self, grads):
        keep, got = grads[0], self.partner(grads)[1]
        return jnp.where(self.home, keep, got), jnp.where(self.home, got, keep)

    def spread(self, value):
        count = self.dp_count // 2
        return self.swap(value).reshape(count, value.shape[0] // count, -1)

    def collect(self, value):
        copies = jnp.broadcast_to(value[None], (self.dp_count // 2, *value.shape))
        return self.swap(copies.reshape(-1, value.shape[1]))

    def joined(self, value, flips):
        for flip in flips:
            first = lax.rem(lax.axis_index("dp") // flip, 2) == 0
            other = self.cross(value, flip)
            value = jnp.concatenate([jnp.where(first, value, other), jnp.where(first, other, value)])
        return value


def total_of(terms):
    return jnp.sum(terms.astype(f32), axis=0).astype(bf16)


def add(a, b):
    return (a.astype(f32) + b.astype(f32)).astype(bf16)


def terms_of(vector, rows):
    terms, rest = [], vector
    for _ in range(3):
        terms.append(lax.reduce_precision(rest, 8, 7))
        rest = rest - terms[-1]
    terms += [jnp.zeros_like(vector)] * (rows - 3)
    return jnp.stack(terms).astype(bf16)


class Plain:
    def __init__(self):
        self.index = lax.axis_index("tensor")
        self.core = self.side = jnp.zeros((), jnp.int32)
        self.home = self.core == 0

    def trade(self, value):
        return value

    def own(self, mine, traded):
        return mine

    def shift(self, blocks):
        return jnp.zeros((1,), jnp.int32)

    def gather(self, value, axis=0):
        return lax.all_gather(value, "tensor", axis=axis, tiled=True)

    def shared(self, value):
        return [self.gather(value)]

    def last_weights(self, out, down, up, bias):
        out, down, up, bias = self.gather(out), self.gather(down), self.gather(up, 1), self.gather(bias)
        model = out.shape[1]
        half, wide = out.shape[0] // 2, down.shape[0] // 2
        packs = [
            jnp.concatenate([
                out[half + number * (half // 2) :][: half // 2],
                down[wide + number * model :][:model],
                up[:, wide + number * model :][:, :model],
                terms_of(bias[wide + number * model :][:model], 16),
            ])
            for number in range(2)
        ]
        return (out[:half], down[:wide], up[:, :wide]), packs, bias[:wide]

    def last_first(self, packs):
        return packs

    def last_second(self, first):
        return first

    def to_rows(self, attended):
        rows = lax.all_to_all(attended[0], "tensor", 1, 0, tiled=True)
        rows = rows.reshape(2, rows.shape[0] // 2, rows.shape[1])
        return rows, rows

    def to_heads(self, mine, other):
        return [lax.all_to_all(jnp.concatenate([mine, other]), "tensor", 0, 1, tiled=True)]

    def scatter(self, mine):
        return lax.psum_scatter(mine, "tensor", scatter_dimension=0, tiled=True)

    def total(self, value):
        return lax.psum(value, ("dp", "tensor"))

    def early_start(self, keep, send):
        quarters = [keep[0], send[0], keep[1], send[1]]
        model = keep[0].shape[1]
        quarter = keep[0].shape[0] - 2 * model
        pieces_of = (
            (jnp.concatenate([v[:quarter] for v in quarters]), 0),
            (jnp.concatenate([v[quarter : quarter + model] for v in quarters]), 0),
            (jnp.concatenate([v[quarter + model :] for v in quarters], axis=1), 1),
        )
        return [
            lax.psum_scatter(v.astype(f32), "tensor", scatter_dimension=d, tiled=True)
            for v, d in pieces_of
        ]


def norm_rows(values, norm_gain, norm_bias):
    centre = values - jnp.mean(values, axis=-1, keepdims=True)
    inverse = lax.rsqrt(jnp.mean(centre * centre, axis=-1, keepdims=True) + epsilon)
    normal = centre * inverse
    return normal * norm_gain + norm_bias


def local(
    inputs, lengths, norm1_gain, norm1_bias, query_key_value_weight, content_bias, position_bias,
    pos_weight, output_weight, out_bias, norm2_gain, norm2_bias, up_projection_weight, up_bias,
    down_projection_weight, down_bias, cotangent,
):
    tensor_count = lax.axis_size("tensor")
    dp_count = lax.axis_size("dp")
    heads, width = content_bias.shape
    paired = tensor_count == 2 and dp_count >= 2 and dp_count & (dp_count - 1) == 0 and heads % 2 == 0
    moves = Paired(dp_count) if paired else Plain()
    _, shard_rows, model = inputs.shape
    seq = shard_rows * tensor_count
    flat = heads * width
    hidden = up_bias.shape[0]
    shift = moves.shift(seq // ROWS)
    core, side = (jnp.reshape(v, (1,)).astype(jnp.int32) for v in (moves.core, moves.side))
    shift = jnp.concatenate([shift, core])
    home = jnp.reshape(moves.home, (1,)).astype(jnp.int32)

    together = lax.optimization_barrier

    row = lax.axis_index("tensor") * shard_rows + jnp.arange(shard_rows, dtype=jnp.int32)
    valid = (row < lengths[0])[:, None]

    got_source = moves.trade(inputs[0])
    vectors = jnp.concatenate([content_bias.reshape(-1), position_bias.reshape(-1)])
    terms = terms_of(vectors, 16).reshape(-1, flat)
    pieces_of = [query_key_value_weight.reshape(3 * model, flat), pos_weight, terms]
    got_pack = moves.trade(jnp.concatenate(pieces_of))
    own_last, last_pack, own_bias = moves.last_weights(
        output_weight, down_projection_weight, up_projection_weight, up_bias
    )
    own_cot = jnp.where(valid, cotangent[0], jnp.zeros_like(cotangent[0]))
    got_cot = moves.trade(own_cot)
    sine, cosine, table_t, table = waves(seq, model)
    got_pack, sine, cosine, table_t, table = together((got_pack, sine, cosine, table_t, table))

    source = moves.own(inputs[0], got_source).astype(f32)
    normed1 = norm_rows(source, norm1_gain, norm1_bias)
    rows1 = moves.shared(normed1.astype(bf16))
    q, kv, pos_rows, biases, qkv = project(
        home, rows1, query_key_value_weight, pos_weight, vectors.reshape(2, flat), got_pack
    )
    if paired:
        last_pack, pos_rows = together((last_pack, pos_rows))
    first_last = moves.last_first(last_pack)
    calls = min(FORWARD_CALLS, heads)
    each = heads // calls
    kept, mine, theirs = [], [], []
    for call in range(calls):
        low, *keep = attend_forward(
            width, call * each, each, shift, q, kv, biases, pos_rows, sine, cosine, table
        )
        kept.append(keep)
        low, other = moves.to_rows(low)
        mine.append(low)
        theirs.append(other)
        if call == 0 and paired:
            first_last, mine[0] = together((first_last, mine[0]))
    first_last, second_last = moves.last_second(first_last)

    y, middle_grad, att_mine, att_other, *packs, row_sums, up_bias_grad = middle_layer(
        core, side, (inputs[0], got_source), (own_cot, got_cot), mine, theirs, own_last, first_last, second_last,
        own_bias[None], [v[None] for v in (out_bias, norm2_gain, norm2_bias, down_bias)],
    )
    att_grads = moves.to_heads(att_mine, att_other)
    early = moves.early_start(packs[:2], packs[2:])

    calls = min(BACKWARD_CALLS, heads)
    step = heads // calls
    before, bias_grads = [], []
    for call in range(calls):
        first = call * step
        held = first // each
        low_out, inverse_sum, weights = kept[held]
        grads, weight_grads, bias_grad = attend_backward(
            width, first, step, held * each, call, before, shift, weights, att_grads, low_out, inverse_sum, q, kv,
            biases, pos_rows, sine, cosine, table_t, rows1,
        )
        bias_grads.append(bias_grad)
        if paired and call == 0:
            early = add(add(early[0], early[1]), early[2])
            early, weight_grads = together((early, weight_grads))
            early = moves.spread(early)
        before = [grads, weight_grads]

    def upstream(part):
        return jnp.einsum("nks,nkr->sr", grads[part], qkv, preferred_element_type=f32)

    got_y = moves.trade(y)
    if paired:
        early, weight_grads, got_y, grads = together((early, weight_grads, got_y, grads))
        kept_late, gone_late = moves.late_start(weight_grads.reshape(2, -1, model))
        gone_late, early, grads, *bias_grads = together((gone_late, early, grads, *bias_grads))
        got_late = moves.across(gone_late)
        early = total_of(early)
        got_up = moves.partner(upstream(1).astype(bf16))
        up = upstream(0)
        flips = moves.flips()
        early = moves.joined(early, flips[:1:-1])
        early, got_late, up = together((early, got_late, up))
        early = moves.joined(early, flips[1:2])
        late = moves.spread(add(kept_late, got_late))
    else:
        up = lax.psum_scatter(upstream(0), "tensor", scatter_dimension=0, tiled=True)
        got_up = jnp.zeros(up.shape, bf16)
        room = jnp.zeros((2, flat * tensor_count), f32)
        bias_grads = jnp.concatenate(bias_grads, axis=1)
        bias_grads = [lax.dynamic_update_slice_in_dim(room, bias_grads, moves.index * flat, 1)]
    input_grad, input_low, small = first_norm(
        2 if paired else 1, jnp.concatenate([core, home]).astype(jnp.int32), inputs[0], got_source, up, got_up,
        middle_grad, norm1_gain[None], row_sums, up_bias_grad, bias_grads,
    )
    if paired:
        flips = moves.flips()
        late, small, input_low, got_y = together((late, small, input_low, got_y))
        late = total_of(late)
        small = moves.summed(small, [1])
        small = moves.summed(small + moves.across(small), flips[:1])
        early, small = together((early, small))
        early = moves.joined(early, flips[:1])
        small = moves.summed(small, flips[1:])
        small, input_low = together((small, input_low))
        got_grad = moves.trade(input_low)
    else:
        small = moves.total(small)
    small = small.reshape(-1)
    if paired:
        input_grad = moves.own(input_grad, got_grad.astype(f32))
    output = moves.own(y, got_y)
    output = jnp.where(valid, output, jnp.zeros_like(output))

    vectors, at = [], 0
    for _ in range(6):
        vectors.append(small[at : at + model])
        at += model
    for count in (flat, flat, hidden):
        here = small[at : at + count * tensor_count]
        vectors.append(lax.dynamic_slice_in_dim(here, lax.axis_index("tensor") * count, count, 0))
        at += count * tensor_count

    if paired:
        late = moves.collect(late)
        out_grad, down_grad, up_grad = unpack(core, early, moves.partner(early), flat, hidden)
        late, out_grad, down_grad, up_grad, input_grad, output, *vectors = together(
            (late, out_grad, down_grad, up_grad, input_grad, output, *vectors)
        )
        qkv_grad, pos_grad = finish(core, late, moves.partner(late), flat, width)
    else:
        out_grad, down_grad, up_grad = (lax.psum(v.astype(bf16), "dp").astype(f32) for v in early)
        late = lax.psum(weight_grads[:calls], "dp").astype(f32).reshape(-1, 4, width, model)[:heads]
        qkv_grad = late[:, :3].transpose(1, 3, 0, 2).reshape(3, model, flat)
        pos_grad = late[:, 3].transpose(2, 0, 1).reshape(model, flat)

    return (
        output[None],
        input_grad[None],
        vectors[0],
        vectors[1],
        qkv_grad,
        vectors[6].reshape(heads, width),
        vectors[7].reshape(heads, width),
        pos_grad,
        out_grad,
        vectors[2],
        vectors[3],
        vectors[4],
        up_grad,
        vectors[8],
        down_grad,
        vectors[5],
    )


def solution(mesh):
    rows = P("dp", "tensor", None)
    return jax.shard_map(
        local,
        mesh=mesh,
        in_specs=(
            rows, P("dp"), P(), P(), P(None, None, "tensor"), P("tensor", None),
            P("tensor", None), P(None, "tensor"), P("tensor", None), P(), P(), P(),
            P(None, "tensor"), P("tensor"), P("tensor", None), P(), rows,
        ),
        out_specs=(
            rows, rows, P(), P(), P(None, None, "tensor"), P("tensor", None),
            P("tensor", None), P(None, "tensor"), P("tensor", None), P(), P(), P(),
            P(None, "tensor"), P("tensor"), P("tensor", None), P(),
        ),
        check_vma=False,
    )
```
